32 devices in a mesh: seq: 8 (over z, y), head: 4 (over x, core).
Axes of the slice: x: 2, y: 2, z: 4, core: 2. Of those that a mesh axis runs over, the one named last changes fastest.
Arguments:
- mixer_input: bfloat16 [16384, 5120], P('seq', 'head'), may hold values from -6 to 6
- write_map: bfloat16 [16384, 128], P('seq', 'head'), may hold values from -0.5 to 0.5
- read_map: bfloat16 [16384, 128], P('seq', 'head'), may hold values from -6 to 6
- step_size: float32 [80, 16384], P('head', 'seq'), may hold values from 0 to 0.5
- log_decay: float32 [80, 16384], P('head', 'seq'), may hold values from -3 to 0
- skip_gain: float32 [80], P('head'), may hold values from 0.5 to 1.5
- level_table: float32 [7, 8], replicated, may hold values from 0.5 to 2
- level_index: int32 [7, 16384], P(None, 'seq'), may hold values from 0 to 7
Outputs:
- mixer_output: bfloat16 [16384, 5120], P('seq', 'head')
The draws below stay inside these ranges and needn't reach their ends.
All inputs are finite; a program needn't handle non-finite values.
Results may differ from the reference program's by a relative error of at most 0.0043.
Values may be sent and summed in bfloat16 or wider, within the bound.
No kernel may reach another device: no remote copies, remote signals or barrier semaphores. Data moves between devices by JAX's collectives and lax.ppermute only.
A program may use at most 256 MiB of HBM per device.

```python
import math
import jax
import jax.numpy as jnp
from jax import lax

HEAD_TOTAL = 80
HEAD_DIM = 64
STATE = 128
BLOCK = 256
LEVEL_CHOICES = 8
SEQUENCE_TOKENS = 16384
LEVELS = 7


def decay_rates(key):
    base_key = jax.random.fold_in(key, 7)
    ranking = jax.random.permutation(jax.random.fold_in(base_key, 1), HEAD_TOTAL)
    fast_count = max(1, HEAD_TOTAL // 8)
    lasting_count = HEAD_TOTAL // 2
    middle_count = (HEAD_TOTAL - lasting_count - fast_count) // 2
    fast_rate = 1.0 / jax.random.uniform(jax.random.fold_in(base_key, 2), (HEAD_TOTAL,), minval=30.0, maxval=50.0)
    slow_rate = jax.random.uniform(jax.random.fold_in(base_key, 3), (HEAD_TOTAL,), minval=0.1, maxval=0.6) / SEQUENCE_TOKENS
    medium_rate = jax.random.uniform(jax.random.fold_in(base_key, 4), (HEAD_TOTAL,), minval=0.64, maxval=1.0) / BLOCK
    gentle_rate = jax.random.uniform(jax.random.fold_in(base_key, 5), (HEAD_TOTAL,), minval=0.16, maxval=0.19) / BLOCK
    return jnp.where(ranking < fast_count, fast_rate, jnp.where(ranking < fast_count + middle_count, medium_rate, jnp.where(ranking < HEAD_TOTAL - lasting_count, gentle_rate, slow_rate)))


def rough_factor(key, salt):
    return jnp.exp(jax.random.uniform(jax.random.fold_in(key, salt), (HEAD_TOTAL, SEQUENCE_TOKENS), minval=-0.7, maxval=0.7))


def draw_log_decay(key, part):
    forget_rate = decay_rates(key)
    block_total = SEQUENCE_TOKENS // BLOCK
    block_multiplier = jnp.exp(jax.random.uniform(jax.random.fold_in(key, 21), (HEAD_TOTAL, block_total), minval=-0.7, maxval=0.7))
    block_multiplier = jnp.repeat(block_multiplier, BLOCK, axis=1)
    token_multiplier = rough_factor(key, 22)
    spike_positions = jax.random.randint(jax.random.fold_in(key, 23), (2,), 0, SEQUENCE_TOKENS)
    spike_lengths = jnp.log(jax.random.uniform(jax.random.fold_in(key, 24), (2, HEAD_TOTAL), minval=0.5, maxval=0.8))
    struck_flags = jnp.arange(SEQUENCE_TOKENS)[None, :] == spike_positions[:, None]
    spike_events = jnp.sum(jnp.where(struck_flags[:, None, :], spike_lengths[:, :, None], 0.0), axis=0)
    return (-forget_rate[:, None] * block_multiplier * token_multiplier + spike_events).astype(jnp.float32)


def draw_step_size(key, part):
    forget_rate = decay_rates(key)
    memory = jnp.minimum(1.0 / forget_rate, SEQUENCE_TOKENS * 1.0)
    return (rough_factor(key, 31) / jnp.sqrt(memory)[:, None]).astype(jnp.float32)


def set_ends(values, stream_key, low, top_value):
    longest = values.shape.index(max(values.shape))
    spots = []
    for shift in (0, 1):
        where = [jax.random.randint(jax.random.fold_in(stream_key, axis), (), 0, length) for axis, length in enumerate(values.shape)]
        where[longest] = (where[longest] + shift) % values.shape[longest]
        spots.append(tuple(where))
    return values.at[spots[0]].set(low).at[spots[1]].set(top_value)


def levels(rng, dims, pieces, smallest, largest):
    loudness = 1.0
    for dim, shards_of in pieces:
        heights = jax.random.uniform(jax.random.fold_in(jax.random.fold_in(rng, 6), dim), (shards_of,), jnp.float32, smallest / len(pieces), largest / len(pieces))
        loudness = loudness * jnp.repeat(jnp.exp(heights), dims[dim] // shards_of).reshape((-1,) + (1,) * (len(dims) - 1 - dim))
    return loudness


def normal_values(own_key, dims, spread, limit, cuts=(), kind=jnp.bfloat16):
    entries = spread * jax.random.normal(own_key, dims, jnp.float32)
    if cuts:
        entries = entries * levels(own_key, dims, cuts, -0.22, 0.18)
    return jnp.clip(entries, -limit, limit).astype(kind)


def setup_inputs(seed: int = 0) -> dict:
    seeds = jax.random.split(jax.random.key(seed), 9)
    return {
        "mixer_input": normal_values(seeds[0], (SEQUENCE_TOKENS, HEAD_TOTAL * HEAD_DIM), 1.0, 6.0, ((0, 8), (1, 4))),
        "write_map": normal_values(seeds[1], (SEQUENCE_TOKENS, STATE), STATE ** -0.5, 0.5, ((0, 8), (1, 4))),
        "read_map": normal_values(seeds[2], (SEQUENCE_TOKENS, STATE), 1.0, 6.0, ((0, 8), (1, 4))),
        "step_size": draw_step_size(jax.random.fold_in(seeds[8], 71), 0),
        "log_decay": draw_log_decay(jax.random.fold_in(seeds[8], 71), 0),
        "skip_gain": jnp.clip(0.5 + 1.0 * jax.random.uniform(seeds[5], (HEAD_TOTAL,), jnp.float32) ** levels(seeds[5], (HEAD_TOTAL,), ((0, 4),), -0.2, 0.2), 0.5, 1.5),
        "level_table": jnp.clip(jnp.exp(jax.random.uniform(seeds[6], (LEVELS, LEVEL_CHOICES), jnp.float32, math.log(0.5), math.log(2.0))), 0.5, 2.0),
        "level_index": set_ends(jax.random.randint(seeds[7], (LEVELS, SEQUENCE_TOKENS), 0, LEVEL_CHOICES), jax.random.fold_in(seeds[7], 1), 0, LEVEL_CHOICES - 1).astype(jnp.int32),
    }


def tree_merge(lower_state, lower_total, upper_state, upper_total):
    merged = jnp.exp(upper_total)[..., None, None] * lower_state + upper_state
    return merged, lower_total + upper_total


def reference(mixer_input, write_map, read_map, step_size, log_decay, skip_gain, level_table, level_index):
    block_count = SEQUENCE_TOKENS // BLOCK
    tree_depth = LEVELS - 1
    level_weight = jnp.take_along_axis(level_table, level_index, axis=1)
    write_rows = write_map.astype(jnp.float32).reshape(block_count, BLOCK, STATE)
    read_rows = read_map.astype(jnp.float32).reshape(block_count, BLOCK, STATE)
    scores = jnp.einsum("btn,bsn->bts", read_rows, write_rows)
    queries = (level_weight[1:].T.reshape(block_count, BLOCK, tree_depth, 1) * read_rows[:, :, None, :]).reshape(block_count, BLOCK, tree_depth * STATE)
    causal = jnp.tril(jnp.ones((BLOCK, BLOCK), dtype=bool))
    positions = jnp.arange(block_count, dtype=jnp.int32)
    first_weight = level_weight[0].reshape(block_count, BLOCK, 1)

    def head_out(packed):
        head_input, head_step, head_decay, head_skip = packed
        decay_sum = jnp.cumsum(head_decay.reshape(block_count, BLOCK), axis=1)
        block_decay = decay_sum[:, -1]
        input_f32 = head_input.astype(jnp.float32).reshape(block_count, BLOCK, HEAD_DIM)
        step_block = head_step.reshape(block_count, BLOCK)
        inputs = (input_f32 * step_block[:, :, None]).astype(jnp.bfloat16)
        gap = jnp.where(causal[None], decay_sum[:, :, None] - decay_sum[:, None, :], -jnp.inf)
        mixing = (scores * jnp.exp(gap)).astype(jnp.bfloat16)
        intra_part = jnp.einsum("bts,bsp->btp", mixing.astype(jnp.float32), inputs.astype(jnp.float32))
        end_inputs = (input_f32 * (step_block * jnp.exp(block_decay[:, None] - decay_sum))[:, :, None]).astype(jnp.bfloat16)
        level_state = jnp.einsum("bsn,bsp->bnp", write_rows, end_inputs.astype(jnp.float32))
        level_total = block_decay
        running = jnp.zeros((block_count,), jnp.float32)
        states = []
        for bit_pos in range(tree_depth):
            shifted = positions >> bit_pos
            bit_flag = (shifted & 1).astype(jnp.float32)
            bucket_at = jnp.maximum(shifted - 1, 0)
            states.append((bit_flag * jnp.exp(running))[:, None, None] * level_state[bucket_at])
            running = running + bit_flag * level_total[bucket_at]
            if bit_pos + 1 < tree_depth:
                paired_state = level_state.reshape(-1, 2, STATE, HEAD_DIM)
                paired_total = level_total.reshape(-1, 2)
                level_state, level_total = tree_merge(paired_state[:, 0], paired_total[:, 0], paired_state[:, 1], paired_total[:, 1])
        stacked = jnp.stack(states, axis=1).reshape(block_count, tree_depth * STATE, HEAD_DIM)
        inter_part = jnp.einsum("btk,bkp->btp", queries, stacked, precision=lax.Precision.HIGHEST)
        result = first_weight * intra_part + jnp.exp(decay_sum)[:, :, None] * inter_part + head_skip * input_f32
        return result.astype(jnp.bfloat16).reshape(SEQUENCE_TOKENS, HEAD_DIM)

    head_inputs = mixer_input.reshape(SEQUENCE_TOKENS, HEAD_TOTAL, HEAD_DIM).transpose(1, 0, 2)
    outputs = lax.map(head_out, (head_inputs, step_size, log_decay, skip_gain))
    return outputs.transpose(1, 0, 2).reshape(SEQUENCE_TOKENS, HEAD_TOTAL * HEAD_DIM)
```

```python
import functools

import jax
import jax.numpy as jnp
from jax import lax
from jax.experimental import pallas as pl
from jax.experimental.pallas import tpu as pltpu
from jax.sharding import PartitionSpec as P

BLOCK = 256
HALF = BLOCK // 2
LANES = 128
LOG2E = 1.4426950408889634
F32 = jnp.float32
BF16 = jnp.bfloat16
NT = (((1,), (1,)), ((), ()))
NN = (((1,), (0,)), ((), ()))
TN = (((0,), (0,)), ((), ()))


def dot(a, b, dims=NN):
    return lax.dot_general(a, b, dims, preferred_element_type=F32)


def three(a):
    high = a.astype(BF16)
    rest = a - high.astype(F32)
    middle = rest.astype(BF16)
    return high, middle, (rest - middle.astype(F32)).astype(BF16)


def exact_left(mask, a):
    high, middle, low = three(a)
    return (dot(mask, low, NT) + dot(mask, middle, NT)) + dot(mask, high, NT)


def exact_right(a, mask):
    high, middle, low = three(a)
    return (dot(low, mask, NT) + dot(middle, mask, NT)) + dot(high, mask, NT)


def spread(padded, heads, width, per_head):
    row = lax.broadcasted_iota(jnp.int32, (2 * padded, width), 0)
    lane = lax.broadcasted_iota(jnp.int32, (2 * padded, width), 1)
    row = jnp.where(row >= padded, row - padded, row)
    own = (row * per_head <= lane) & (lane < (row + 1) * per_head) & (row < heads)
    return own.astype(F32).astype(BF16)


def pair_up(value, padded):
    lane = lax.broadcasted_iota(jnp.int32, value.shape, 1)
    high = value.astype(BF16).astype(F32)
    return jnp.where(lane < padded, high, value - high).astype(BF16)


def prep_kernel(
    heads, padded, width, log_decay, step_size, level_index, level_table,
    cum_t, cum_h, f_step, f_end, f_off, f_cum, f_run, f_total, weight_t, weight_h, rows,
    decay_two, step_two, sums,
):
    tokens = log_decay.shape[1]
    blocks = tokens // BLOCK
    per_head = width // heads
    decay_two[...] = jnp.zeros_like(decay_two)
    step_two[...] = jnp.zeros_like(step_two)
    for base in (0, padded):
        decay_two[base : base + heads, :] = log_decay[...]
        step_two[base : base + heads, :] = step_size[...]
    t_at = lax.broadcasted_iota(jnp.int32, (BLOCK, BLOCK), 0)
    s_at = lax.broadcasted_iota(jnp.int32, (BLOCK, BLOCK), 1)
    lower = (t_at >= s_at).astype(F32).astype(BF16)
    same = (t_at == s_at).astype(F32).astype(BF16)
    weight = jnp.zeros(level_index.shape, F32)
    index = level_index[...]
    for entry in range(level_table.shape[1]):
        weight = weight + jnp.where(index == entry, level_table[:, entry : entry + 1], 0.0)
    weight_h[...] = weight
    for c in range(blocks):
        at = slice(c * BLOCK, (c + 1) * BLOCK)
        sums[at, :] = exact_left(lower, decay_two[:, at])
        cum_h[:, at] = exact_right(decay_two[0:padded, at], lower) * LOG2E
        weight_t[at, :] = exact_left(same, weight_h[:, at])
    before = [jnp.zeros((1, 2 * padded), F32)]
    ends = []
    for c in range(blocks):
        ends.append(sums[(c + 1) * BLOCK - 1 : (c + 1) * BLOCK, :])
        before.append(before[-1] + ends[-1])
    total = before[-1]
    after = [jnp.zeros((1, 2 * padded), F32)]
    for c in reversed(range(blocks)):
        after.append(after[-1] + ends[c])
    after = after[::-1]
    for c in range(blocks):
        at = slice(c * BLOCK, (c + 1) * BLOCK)
        cum = sums[at, :]
        step = exact_left(same, step_two[:, at])
        cum_t[at, :] = cum * LOG2E
        f_step[at, :] = pair_up(step, padded)
        to_end = jnp.exp(ends[c] - cum)
        f_end[at, :] = pair_up(step * to_end, padded)
        f_total[at, :] = pair_up(step * jnp.exp((ends[c] - cum) + after[c + 1]), padded)
        f_cum[at, :] = pair_up(jnp.exp(cum), padded)
        f_run[at, :] = pair_up(jnp.exp(cum + before[c]), padded)
        middle = sums[c * BLOCK + HALF - 1 : c * BLOCK + HALF, :]
        first = cum[:HALF]
        f_off[c * BLOCK : c * BLOCK + HALF, :] = pair_up(
            step[:HALF] * jnp.exp(middle - first), padded
        )
        f_off[c * BLOCK + HALF : (c + 1) * BLOCK, :] = pair_up(jnp.exp(cum[HALF:] - middle), padded)
    where = lax.broadcasted_iota(jnp.int32, (rows.shape[0], 2 * padded), 0)
    table = jnp.zeros((rows.shape[0], 2 * padded), F32)
    for c in range(blocks):
        table = jnp.where(where == c, ends[c], table)
    table = jnp.where(where == blocks, total, table)
    rows[...] = dot(pair_up(jnp.exp(table), padded), spread(padded, heads, width, per_head))


def state_kernel(heads, padded, tile, mixer, factor, write_t, rows, mine, mine_exp, payload):
    width = mixer.shape[1]
    state = write_t.shape[0]
    blocks = pl.num_programs(0)
    c = pl.program_id(0)
    wide = spread(padded, heads, width, width // heads)

    @pl.when(c == 0)
    def _():
        mine[...] = jnp.zeros_like(mine)

    for left in range(0, width, tile):
        at = slice(left, left + tile)
        scaled = (mixer[:, at].astype(F32) * dot(factor[...], wide[:, at])).astype(BF16)
        mine[:, at] += dot(write_t[...], scaled)

    @pl.when(c == blocks - 1)
    def _():
        row_count = payload.shape[0] - state
        total = rows[blocks_row(rows) : blocks_row(rows) + 1, :]
        payload[0:state, :] = mine[...].astype(BF16)
        payload[state:, :] = exp_rows(total, row_count)
        mine_exp[...] = jnp.broadcast_to(total, mine_exp.shape)


def blocks_row(rows):
    return rows.shape[0] - 8


def exp_rows(total, count):
    where = lax.broadcasted_iota(jnp.int32, (count, total.shape[1]), 0)
    high = total.astype(BF16).astype(F32)
    return jnp.where(where == 0, high, jnp.where(where == 1, total - high, 0.0)).astype(BF16)


def merge_kernel(flags, bit, received, mine, mine_exp, merged, merged_exp, payload):
    state = mine.shape[0]
    extra = received[state:, :].astype(F32)
    other_exp = extra[0:1] + extra[1:2]
    own_exp = mine_exp[0:1, :]
    upper = (jnp.zeros((1, mine.shape[1]), jnp.int32) + flags[bit]) > 0
    own_scale = jnp.where(upper, 1.0, other_exp)
    other_scale = jnp.where(upper, own_exp, 1.0)
    new = own_scale * mine[...] + other_scale * received[0:state, :].astype(F32)
    merged[...] = new
    total = own_exp * other_exp
    merged_exp[...] = jnp.broadcast_to(total, merged_exp.shape)
    payload[0:state, :] = new.astype(BF16)
    payload[state:, :] = exp_rows(total, payload.shape[0] - state)


def local_kernel(
    heads, padded, tile, bits, first, mixer, write_t, read_t, cum_t, cum_h, f_step, f_end, f_off,
    f_cum, weight_t, weight_h, rows, skip, slots_in, base, slots, scores, inter, fresh,
):
    width = mixer.shape[1]
    per_head = width // heads
    g = pl.program_id(0)
    c = first + g
    wide = spread(padded, heads, width, per_head)

    @pl.when(g == 0)
    def _():
        slots[...] = slots_in[...]

    for bit in range(bits):

        @pl.when((c >> bit) & 1 == 1)
        def _(bit=bit):
            query = (read_t[...].astype(F32) * weight_h[bit + 1 : bit + 2, :]).astype(BF16)
            part = dot(query, slots[bit].astype(BF16), TN)
            if bit == 0:
                inter[...] = part
            else:

                @pl.when(c & ((1 << bit) - 1) == 0)
                def _():
                    inter[...] = part

                @pl.when(c & ((1 << bit) - 1) != 0)
                def _():
                    inter[...] += part

    @pl.when(c == 0)
    def _():
        inter[...] = jnp.zeros_like(inter)

    t_at = lax.broadcasted_iota(jnp.int32, (BLOCK, BLOCK), 0)
    s_at = lax.broadcasted_iota(jnp.int32, (BLOCK, BLOCK), 1)
    weighted = dot(read_t[...], write_t[...], TN) * weight_t[:, 0:1]
    scores[...] = jnp.where(t_at >= s_at, weighted, 0.0)
    off_scores = scores[HALF:, :HALF].astype(BF16)
    lane = lax.broadcasted_iota(jnp.int32, (HALF, LANES), 1)
    heads_here = LANES // per_head
    for left in range(0, width, tile):
        at = slice(left, left + tile)
        mixer_f = mixer[:, at].astype(F32)
        inputs = (mixer_f * dot(f_step[...], wide[:, at])).astype(BF16)
        off = dot(f_off[...], wide[:, at])
        off_inputs = (mixer_f[:HALF] * off[:HALF]).astype(BF16)
        off_part = dot(off_scores, off_inputs) * off[HALF:]
        rest = inter[:, at] * dot(f_cum[...], wide[:, at]) + skip[:, at] * mixer_f
        end_inputs = (mixer_f * dot(f_end[...], wide[:, at])).astype(BF16)
        fresh[:, at] = dot(write_t[...], end_inputs)
        for inner in range(0, tile, LANES):
            lanes = slice(inner, inner + LANES)
            out = slice(left + inner, left + inner + LANES)
            head = (left + inner) // per_head
            for half in range(2):
                rows_at = slice(half * HALF, (half + 1) * HALF)
                here = inputs[rows_at, lanes].astype(F32)
                left_side = []
                right_side = []
                for k in range(heads_here):
                    gap = cum_t[rows_at, head + k : head + k + 1] - cum_h[head + k : head + k + 1, rows_at]
                    mixing = scores[rows_at, rows_at] * jnp.exp2(jnp.minimum(gap, 0.0))
                    left_side.append(mixing.astype(BF16))
                    own = (lane >= k * per_head) & (lane < (k + 1) * per_head)
                    right_side.append(jnp.where(own, here, 0.0).astype(BF16))
                part = dot(jnp.concatenate(left_side, 1), jnp.concatenate(right_side, 0))
                part = part + rest[rows_at, lanes]
                if half == 1:
                    part = part + off_part[:, lanes]
                base[rows_at, out] = part

    shrink = rows[pl.ds(c, 1), :]
    for bit in range(bits):
        below = (1 << bit) - 1

        @pl.when(((c >> bit) & 1 == 1) & (c & below == below))
        def _(bit=bit):
            fresh[...] += shrink * slots[bit]

        @pl.when(((c >> bit) & 1 == 1) & (c & below != below))
        def _(bit=bit):
            slots[bit] = shrink * slots[bit]

        @pl.when(((c >> bit) & 1 == 0) & (c & below == below))
        def _(bit=bit):
            slots[bit] = fresh[...]


def final_kernel(padded, heads, tile, local_bits, bits, flags, base, read_t, weight_h, factor, *rest):
    received = rest[:bits]
    out, buckets = rest[bits], rest[bits + 1]
    width = base.shape[1]
    state = read_t.shape[0]
    wide = spread(padded, heads, width, width // heads)

    @pl.when(pl.program_id(0) == 0)
    def _():
        running = jnp.ones((1, width), F32)
        for bit in range(bits):
            upper = (jnp.zeros((1, width), jnp.int32) + flags[bit]) > 0
            extra = received[bit][state:, :].astype(F32)
            scale = jnp.where(upper, running, 0.0)
            buckets[bit * state : (bit + 1) * state, :] = (
                received[bit][0:state, :].astype(F32) * scale
            ).astype(BF16)
            running = jnp.where(upper, running * (extra[0:1] + extra[1:2]), running)

    read_f = read_t[...].astype(F32)
    queries = jnp.concatenate(
        [
            (read_f * weight_h[local_bits + 1 + bit : local_bits + 2 + bit, :]).astype(BF16)
            for bit in range(bits)
        ],
        0,
    )
    for left in range(0, width, tile):
        at = slice(left, left + tile)
        part = dot(queries, buckets[:, at], TN)
        out[:, at] = (base[:, at] + part * dot(factor[...], wide[:, at])).astype(BF16)


def gather_columns(mine, axis):
    pieces = mine
    size = lax.axis_size(axis)
    stride = size // 2
    while stride:
        other = lax.ppermute(pieces, axis, [(i, i ^ stride) for i in range(size)])
        pieces = jnp.concatenate([pieces, other], 0)
        stride //= 2
    return pieces


def cost(flops, bytes_accessed):
    return pl.CostEstimate(flops=flops, bytes_accessed=bytes_accessed, transcendentals=0)


def on_device(
    mixer_input, write_map, read_map, step_size, log_decay, skip_gain, level_table, level_index
):
    tokens, width = mixer_input.shape
    heads = log_decay.shape[0]
    per_head = width // heads
    blocks = tokens // BLOCK
    local_bits = blocks.bit_length() - 1
    ranks = lax.axis_size("seq")
    device_bits = ranks.bit_length() - 1
    levels = level_table.shape[0]
    padded = -(-heads // 32) * 32
    tile = 256
    rank = lax.axis_index("seq")
    flags = (rank >> jnp.arange(device_bits, dtype=jnp.int32)) & 1

    write_t = gather_columns(write_map.T, "head")
    read_t = gather_columns(read_map.T, "head")
    state = write_t.shape[0]

    sds = jax.ShapeDtypeStruct
    narrow = sds((tokens, 2 * padded), BF16)
    row_count = -(-blocks // 8) * 8 + 8
    (
        cum_t, cum_h, f_step, f_end, f_off, f_cum, f_run, f_total, weight_t, weight_h, rows
    ) = pl.pallas_call(
        functools.partial(prep_kernel, heads, padded, width),
        out_shape=(
            sds((tokens, 2 * padded), F32), sds((padded, tokens), F32),
            narrow, narrow, narrow, narrow, narrow, narrow,
            sds((tokens, levels), F32), sds((levels, tokens), F32), sds((row_count, width), F32),
        ),
        scratch_shapes=[
            pltpu.VMEM((2 * padded, tokens), F32),
            pltpu.VMEM((2 * padded, tokens), F32),
            pltpu.VMEM((tokens, 2 * padded), F32),
        ],
        name="prep",
    )(log_decay, step_size, level_index, level_table)

    by_token = lambda columns: pl.BlockSpec((BLOCK, columns), lambda g: (g, 0))
    by_lane = lambda count: pl.BlockSpec((count, BLOCK), lambda g: (0, g))
    whole = lambda shape: pl.BlockSpec(shape, lambda g: (0,) * len(shape))
    payload_rows = state + 8
    mine, mine_exp, payload = pl.pallas_call(
        functools.partial(state_kernel, heads, padded, tile),
        grid=(blocks,),
        in_specs=[by_token(width), by_token(2 * padded), by_lane(state), whole((row_count, width))],
        out_specs=(whole((state, width)), whole((8, width)), whole((payload_rows, width))),
        out_shape=(
            sds((state, width), F32), sds((8, width), F32), sds((payload_rows, width), BF16)
        ),
        cost_estimate=cost(2 * tokens * width * state, tokens * width * 2),
        name="state",
    )(mixer_input, f_total, write_t, rows)

    skip_row = jnp.repeat(skip_gain, per_head)[None, :]

    def local(first, count, slots):
        shift = lambda columns: pl.BlockSpec((BLOCK, columns), lambda g: (g + first, 0))
        shift_lane = lambda n: pl.BlockSpec((n, BLOCK), lambda g: (0, g + first))
        return pl.pallas_call(
            functools.partial(local_kernel, heads, padded, tile, local_bits, first),
            grid=(count,),
            in_specs=[
                shift(width), shift_lane(state), shift_lane(state), shift(2 * padded),
                shift_lane(padded), shift(2 * padded), shift(2 * padded), shift(2 * padded),
                shift(2 * padded), shift(levels), shift_lane(levels), whole((row_count, width)),
                whole((1, width)), whole((local_bits, state, width)),
            ],
            out_specs=(by_token(width), whole((local_bits, state, width))),
            out_shape=(
                sds((count * BLOCK, width), F32), sds((local_bits, state, width), F32)
            ),
            scratch_shapes=[
                pltpu.VMEM((BLOCK, BLOCK), F32),
                pltpu.VMEM((BLOCK, width), F32),
                pltpu.VMEM((state, width), F32),
            ],
            cost_estimate=cost(count * BLOCK * width * 2 * 3000, count * BLOCK * width * 8),
            name="local",
        )(
            mixer_input, write_t, read_t, cum_t, cum_h, f_step, f_end, f_off, f_cum, weight_t,
            weight_h, rows, skip_row, slots,
        )

    slots = jnp.zeros((local_bits, state, width), F32)
    base, slots = local(0, blocks, slots)

    received = []
    for bit in range(device_bits):
        other = lax.ppermute(payload, "seq", [(i, i ^ 1 << bit) for i in range(ranks)])
        received.append(other)
        if bit + 1 < device_bits:
            mine, mine_exp, payload = pl.pallas_call(
                lambda f, *refs, bit=bit: merge_kernel(f, bit, *refs),
                in_specs=[pl.BlockSpec(memory_space=pltpu.SMEM)]
                + [pl.BlockSpec(memory_space=pltpu.VMEM)] * 3,
                out_shape=(
                    sds((state, width), F32), sds((8, width), F32), sds((payload_rows, width), BF16)
                ),
                cost_estimate=cost(4 * state * width, state * width * 12),
                name="merge",
            )(flags, other, mine, mine_exp)

    return pl.pallas_call(
        functools.partial(final_kernel, padded, heads, tile, local_bits, device_bits),
        grid=(blocks,),
        in_specs=[
            pl.BlockSpec(memory_space=pltpu.SMEM), by_token(width), by_lane(state),
            by_lane(levels), by_token(2 * padded),
        ]
        + [whole((payload_rows, width))] * device_bits,
        out_specs=by_token(width),
        out_shape=sds((tokens, width), BF16),
        scratch_shapes=[pltpu.VMEM((device_bits * state, width), BF16)],
        cost_estimate=cost(2 * tokens * width * state * device_bits, tokens * width * 6),
        name="final",
    )(flags, base, read_t, weight_h, f_run, *received)


def solution(mesh):
    placed = (
        P("seq", "head"),
        P("seq", "head"),
        P("seq", "head"),
        P("head", "seq"),
        P("head", "seq"),
        P("head"),
        P(),
        P(None, "seq"),
    )
    return jax.shard_map(
        on_device, mesh=mesh, in_specs=placed, out_specs=P("seq", "head"), check_vma=False
    )
```

```python
import functools

import jax
import jax.numpy as jnp
from jax import lax
from jax.experimental import pallas as pl
from jax.experimental.pallas import tpu as pltpu
from jax.sharding import PartitionSpec as P

BLOCK = 256
HALF = BLOCK // 2
LANES = 128
LOG2E = 1.4426950408889634
F32 = jnp.float32
BF16 = jnp.bfloat16
NT = (((1,), (1,)), ((), ()))
NN = (((1,), (0,)), ((), ()))
TN = (((0,), (0,)), ((), ()))
VMEM_SPEC = pl.BlockSpec(memory_space=pltpu.VMEM)
SMEM_SPEC = pl.BlockSpec(memory_space=pltpu.SMEM)
ANY_SPEC = pl.BlockSpec(memory_space=pl.ANY)


def dot(a, b, dims=NN):
    return lax.dot_general(a, b, dims, preferred_element_type=F32)


def three(a):
    high = a.astype(BF16)
    rest = a - high.astype(F32)
    middle = rest.astype(BF16)
    return high, middle, (rest - middle.astype(F32)).astype(BF16)


def two(a):
    high = a.astype(BF16).astype(F32)
    return high, a - high


def iota(shape, dim):
    return lax.broadcasted_iota(jnp.int32, shape, dim)


def as_bf16(mask):
    return mask.astype(F32).astype(BF16)


def spread(first_row, padded, heads, width):
    per_head = width // heads
    row = iota((4 * padded, width), 0) - first_row
    lane = iota((4 * padded, width), 1)
    inside = (row >= 0) & (row < 2 * padded)
    row = jnp.where(row >= padded, row - padded, row)
    own = (row * per_head <= lane) & (lane < (row + 1) * per_head) & (row < heads)
    return as_bf16(own & inside)


class Rows:
    def __init__(self, blocks):
        halves = 2 * blocks
        self.after, self.run = 0, halves
        self.middle, self.upper, self.decay = 2 * halves, 2 * halves + blocks, 2 * halves + 2 * blocks
        self.total = 2 * halves + 3 * blocks
        self.count = -(-(self.total + 1) // 16) * 16

    def ranges(self, tokens):
        halves = tokens // HALF
        low, high = [], []
        for a in range(halves):
            low.append((a + 1) * HALF), high.append(tokens)
        for a in range(halves):
            low.append(0), high.append(a * HALF)
        for c in range(halves // 2):
            low.append(c * BLOCK), high.append(c * BLOCK + HALF)
        for c in range(halves // 2):
            low.append(c * BLOCK + HALF), high.append((c + 1) * BLOCK)
        for c in range(halves // 2):
            low.append(c * BLOCK), high.append((c + 1) * BLOCK)
        low.append(0), high.append(tokens)
        pad = self.count - len(low)
        return jnp.array([low + [0] * pad, high + [0] * pad], jnp.int32).T


def prep_kernel(
    heads, padded, log_decay, step_size, level_index, level_table, ranges,
    factors, columns, cum_h, weight_h, rows, decay, steps, packed,
):
    tokens = log_decay.shape[1]
    width = rows.shape[1]
    blocks = tokens // BLOCK
    decay[...] = jnp.zeros_like(decay)
    steps[...] = jnp.zeros_like(steps)
    decay[0:heads, :] = log_decay[...]
    steps[0:heads, :] = step_size[...]
    lower = as_bf16(iota((BLOCK, BLOCK), 0) >= iota((BLOCK, BLOCK), 1))
    levels = level_index.shape[0]
    weight = jnp.zeros(level_index.shape, F32)
    index = level_index[...]
    for entry in range(level_table.shape[1]):
        weight = weight + jnp.where(index == entry, level_table[:, entry : entry + 1], 0.0)
    weight_h[...] = weight
    packed[...] = jnp.zeros_like(packed)
    for c in range(blocks):
        at = slice(c * BLOCK, (c + 1) * BLOCK)
        high, middle, low = three(decay[:, at])
        cum = (dot(low, lower, NT) + dot(middle, lower, NT)) + dot(high, lower, NT)
        step = steps[:, at]
        mid = cum[:, HALF - 1 : HALF]
        end = cum[:, BLOCK - 1 : BLOCK]
        first = iota((padded, BLOCK), 1) < HALF
        column = two(step * jnp.exp(jnp.where(first, mid, end) - cum))
        row = two(jnp.exp(cum - jnp.where(first, 0.0, mid)))
        four = jnp.concatenate([column[0], column[1], row[0], row[1]], 0)
        factors[at, :] = four.T.astype(BF16)
        scaled = cum * LOG2E
        cum_h[:, at] = scaled - jnp.log2(step)
        packed[0:padded, :] = scaled
        packed[padded : padded + levels, :] = weight_h[:, at]
        columns[at, :] = packed[...].T
    token = iota((rows.shape[0], tokens), 1)
    chosen = as_bf16((token >= ranges[:, 0:1]) & (token < ranges[:, 1:2]))
    high, middle, low = three(decay[...])
    sums = (dot(chosen, low, NT) + dot(chosen, middle, NT)) + dot(chosen, high, NT)
    high, low = two(jnp.exp(sums))
    per_head = width // heads
    head = iota((padded, width), 0) * per_head
    lane = iota((padded, width), 1)
    own = as_bf16((head <= lane) & (lane < head + per_head))
    rows[...] = dot(high.astype(BF16), own) + dot(low.astype(BF16), own)


def scale_kernel(heads, padded, layout, mixer, factors, rows, scaled, to_total):
    tokens, width = mixer.shape
    wide = spread(0, padded, heads, width)

    def step(a, carry):
        at = pl.ds(pl.multiple_of(a * HALF, HALF), HALF)
        row = rows[pl.ds(layout.after + a, 1), :]
        value = mixer[at, :].astype(F32) * dot(factors[at, :], wide)
        scaled[at, :] = value.astype(BF16)
        to_total[at, :] = (value * row).astype(BF16)
        return carry

    lax.fori_loop(0, tokens // HALF, step, 0)


def exp_rows(total, count):
    where = iota((count, total.shape[1]), 0)
    high = total.astype(BF16).astype(F32)
    return jnp.where(where == 0, high, jnp.where(where == 1, total - high, 0.0)).astype(BF16)


def state_kernel(layout, to_total, write_t, rows, mine, mine_exp, payload):
    state = write_t.shape[0]
    new = dot(write_t[...], to_total[...])
    mine[...] = new
    payload[0:state, :] = new.astype(BF16)
    total = rows[layout.total : layout.total + 1, :]
    payload[state:, :] = exp_rows(total, payload.shape[0] - state)
    mine_exp[...] = jnp.broadcast_to(total, mine_exp.shape)


def merge_kernel(bit, flags, received, mine, mine_exp, after, merged, merged_exp, payload):
    state = mine.shape[0]
    extra = received[state:, :].astype(F32)
    other_exp = extra[0:1] + extra[1:2]
    own_exp = mine_exp[0:1, :]
    upper = (jnp.zeros((1, mine.shape[1]), jnp.int32) + flags[bit]) > 0
    own_scale = jnp.where(upper, 1.0, other_exp)
    other_scale = jnp.where(upper, own_exp, 1.0)
    new = own_scale * mine[...] + other_scale * received[0:state, :].astype(F32)
    merged[...] = new
    total = own_exp * other_exp
    merged_exp[...] = jnp.broadcast_to(total, merged_exp.shape)
    payload[0:state, :] = new.astype(BF16)
    payload[state:, :] = exp_rows(total, payload.shape[0] - state)


def local_kernel(
    heads, padded, bits, first, count, layout, tile,
    mixer, scaled, write_t, read_t, factors, columns, cum_h, weight_h, rows, skip, slots_in, after,
    base, reach, slots, scores, inter, fresh,
):
    width = mixer.shape[1]
    per_head = width // heads
    heads_here = LANES // per_head
    wide = spread(2 * padded, padded, heads, width)
    if first == 0:
        slots[...] = jnp.zeros_like(slots)
    else:
        slots[...] = slots_in[...]

    def block(g, carry):
        c = first + g
        at = pl.ds(pl.multiple_of(c * BLOCK, BLOCK), BLOCK)
        out_at = pl.ds(pl.multiple_of(g * BLOCK, BLOCK), BLOCK)
        read = read_t[:, at]
        write = write_t[:, at]

        inter[...] = jnp.zeros_like(inter)
        for bit in range(bits):

            @pl.when((c >> bit) & 1 == 1)
            def _(bit=bit):
                query = (read.astype(F32) * weight_h[bit + 1 : bit + 2, at]).astype(BF16)
                inter[...] += dot(query, slots[bit].astype(BF16), TN)

        weighted = dot(read, write, TN) * columns[at, padded : padded + 1]
        causal = iota((HALF, HALF), 0) >= iota((HALF, HALF), 1)
        off_scores = weighted[HALF:, :HALF].astype(BF16)
        scores[0] = jnp.where(causal, weighted[:HALF, :HALF], 0.0)
        scores[1] = jnp.where(causal, weighted[HALF:, HALF:], 0.0)
        lane = iota((HALF, LANES), 1)
        own = [as_bf16((lane >= k * per_head) & (lane < (k + 1) * per_head)) for k in range(heads_here)]
        middle = rows[pl.ds(layout.middle + c, 1), :]
        for half in range(2):
            half_at = pl.ds(pl.multiple_of(c * BLOCK + half * HALF, HALF), HALF)
            put_at = pl.ds(pl.multiple_of(g * BLOCK + half * HALF, HALF), HALF)
            first_at = pl.ds(pl.multiple_of(c * BLOCK, HALF), HALF)
            row_at = slice(half * HALF, (half + 1) * HALF)
            run = rows[pl.ds(layout.run + 2 * c + half, 1), :]
            for left in range(0, width, tile):
                lanes = slice(left, left + tile)
                near = dot(factors[half_at, :], wide[:, lanes])
                reach[put_at, lanes] = near * run[:, lanes]
                if half == 0:
                    rest = near * inter[row_at, lanes]
                else:
                    off = dot(off_scores, scaled[first_at, lanes])
                    rest = near * (off + middle[:, lanes] * inter[row_at, lanes])
                for inner in range(left, left + tile, LANES):
                    here = slice(inner, inner + LANES)
                    head = inner // per_head
                    value = mixer[half_at, here]
                    left_side = []
                    for k in range(heads_here):
                        gap = columns[half_at, head + k : head + k + 1] - cum_h[head + k : head + k + 1, half_at]
                        mixing = scores[half] * jnp.exp2(jnp.minimum(gap, 0.0))
                        left_side.append(mixing.astype(BF16))
                    part = dot(
                        jnp.concatenate(left_side, 1),
                        jnp.concatenate([value * mask for mask in own], 0),
                    )
                    base[put_at, here] = (
                        part + rest[:, inner - left : inner - left + LANES]
                        + skip[:, here] * value.astype(F32)
                    )

        upper = rows[pl.ds(layout.upper + c, 1), :]
        start = pl.multiple_of(c * BLOCK, HALF)
        fresh[...] = upper * dot(
            write_t[:, pl.ds(start, HALF)], scaled[pl.ds(start, HALF), :]
        ) + dot(write_t[:, pl.ds(start + HALF, HALF)], scaled[pl.ds(start + HALF, HALF), :])
        shrink = rows[pl.ds(layout.decay + c, 1), :]
        for bit in range(bits):
            below = (1 << bit) - 1

            @pl.when(((c >> bit) & 1 == 1) & (c & below == below))
            def _(bit=bit):
                fresh[...] += shrink * slots[bit]

            @pl.when(((c >> bit) & 1 == 1) & (c & below != below))
            def _(bit=bit):
                slots[bit] = shrink * slots[bit]

            @pl.when(((c >> bit) & 1 == 0) & (c & below == below))
            def _(bit=bit):
                slots[bit] = fresh[...]

        return carry

    lax.fori_loop(0, count, block, 0)


def final_kernel(starts, local_bits, bits, flags, read_t, weight_h, *rest):
    pieces = len(starts) - 1
    received, rest = rest[:bits], rest[bits:]
    bases, reaches, rest = rest[:pieces], rest[pieces : 2 * pieces], rest[2 * pieces :]
    out, buckets, ready, sems = rest
    width = out.shape[1]
    state = read_t.shape[0]
    running = jnp.ones((1, width), F32)
    for bit in range(bits):
        upper = (jnp.zeros((1, width), jnp.int32) + flags[bit]) > 0
        extra = received[bit][state:, :].astype(F32)
        scale = jnp.where(upper, running, 0.0)
        buckets[bit * state : (bit + 1) * state, :] = (
            received[bit][0:state, :].astype(F32) * scale
        ).astype(BF16)
        running = jnp.where(upper, running * (extra[0:1] + extra[1:2]), running)

    def copy(c, at):
        return pltpu.make_async_copy(ready.at[c], out.at[pl.ds(at, BLOCK), :], sems.at[c])

    for piece in range(pieces):

        def block(g, carry, piece=piece):
            c = starts[piece] + g
            at = pl.multiple_of(c * BLOCK, BLOCK)
            from_at = pl.ds(pl.multiple_of(g * BLOCK, BLOCK), BLOCK)
            read_f = read_t[:, pl.ds(at, BLOCK)].astype(F32)
            queries = jnp.concatenate(
                [
                    (read_f * weight_h[local_bits + 1 + bit : local_bits + 2 + bit, pl.ds(at, BLOCK)]).astype(BF16)
                    for bit in range(bits)
                ],
                0,
            )
            part = dot(queries, buckets[...], TN)
            ready[c] = (bases[piece][from_at, :] + part * reaches[piece][from_at, :]).astype(BF16)
            copy(c, at).start()
            return carry

        lax.fori_loop(0, starts[piece + 1] - starts[piece], block, 0)
    for c in range(starts[-1]):
        copy(c, c * BLOCK).wait()


def gather_columns(mine, axis):
    pieces = mine
    size = lax.axis_size(axis)
    stride = size // 2
    while stride:
        other = lax.ppermute(pieces, axis, [(i, i ^ stride) for i in range(size)])
        pieces = jnp.concatenate([pieces, other], 0)
        stride //= 2
    return pieces


def cost(flops, bytes_accessed):
    return pl.CostEstimate(flops=flops, bytes_accessed=bytes_accessed, transcendentals=0)


def grant(mebibytes):
    return pltpu.CompilerParams(vmem_limit_bytes=mebibytes << 20)


def on_device(
    mixer_input, write_map, read_map, step_size, log_decay, skip_gain, level_table, level_index
):
    tokens, width = mixer_input.shape
    heads = log_decay.shape[0]
    per_head = width // heads
    blocks = tokens // BLOCK
    local_bits = blocks.bit_length() - 1
    ranks = lax.axis_size("seq")
    device_bits = ranks.bit_length() - 1
    levels = level_table.shape[0]
    padded = LANES // 4
    tile = 256
    layout = Rows(blocks)
    rank = lax.axis_index("seq")
    flags = (rank >> jnp.arange(device_bits, dtype=jnp.int32)) & 1
    sds = jax.ShapeDtypeStruct

    write_t = gather_columns(write_map.T, "head")
    read_t = gather_columns(read_map.T, "head")
    state = write_t.shape[0]

    factors, columns, cum_h, weight_h, rows = pl.pallas_call(
        functools.partial(prep_kernel, heads, padded),
        in_specs=[VMEM_SPEC] * 5,
        out_specs=(VMEM_SPEC,) * 5,
        out_shape=(
            sds((tokens, LANES), BF16), sds((tokens, LANES), F32), sds((padded, tokens), F32),
            sds((levels, tokens), F32), sds((layout.count, width), F32),
        ),
        scratch_shapes=[
            pltpu.VMEM((padded, tokens), F32),
            pltpu.VMEM((padded, tokens), F32),
            pltpu.VMEM((LANES, BLOCK), F32),
        ],
        compiler_params=grant(12),
        cost_estimate=cost(2_000_000_000, 4_000_000),
        name="prep",
    )(log_decay, step_size, level_index, level_table, layout.ranges(tokens))

    scaled, to_total = pl.pallas_call(
        functools.partial(scale_kernel, heads, padded, layout),
        in_specs=[VMEM_SPEC] * 3,
        out_specs=(VMEM_SPEC,) * 2,
        out_shape=(sds((tokens, width), BF16),) * 2,
        compiler_params=grant(8),
        cost_estimate=cost(3_000_000_000, tokens * width * 6),
        name="scale",
    )(mixer_input, factors, rows)

    payload_rows = state + 8
    carried = (sds((state, width), F32), sds((8, width), F32), sds((payload_rows, width), BF16))
    mine, mine_exp, payload = pl.pallas_call(
        functools.partial(state_kernel, layout),
        in_specs=[VMEM_SPEC] * 3,
        out_specs=(VMEM_SPEC,) * 3,
        out_shape=carried,
        compiler_params=grant(8),
        cost_estimate=cost(2 * tokens * width * state, tokens * width * 2),
        name="state",
    )(to_total, write_t, rows)

    skip_row = jnp.repeat(skip_gain, per_head)[None, :]

    def local(first, count, slots, after):
        return pl.pallas_call(
            functools.partial(
                local_kernel, heads, padded, local_bits, first, count, layout, tile
            ),
            in_specs=[VMEM_SPEC] * 10 + [VMEM_SPEC, ANY_SPEC],
            out_specs=(VMEM_SPEC,) * 3,
            out_shape=(
                sds((count * BLOCK, width), F32), sds((count * BLOCK, width), F32),
                sds((local_bits, state, width), F32),
            ),
            scratch_shapes=[
                pltpu.VMEM((2, HALF, HALF), F32),
                pltpu.VMEM((BLOCK, width), F32),
                pltpu.VMEM((state, width), F32),
            ],
            compiler_params=grant(12),
            cost_estimate=cost(count * BLOCK * width * 2 * 2000, count * BLOCK * width * 8),
            name="local",
        )(
            mixer_input, scaled, write_t, read_t, factors, columns, cum_h, weight_h, rows, skip_row,
            slots, after,
        )

    shares = [1] * (device_bits - 2) + [1, 2] if device_bits > 1 else [1]
    starts = [0]
    for k, share in enumerate(shares):
        starts.append(starts[-1] + blocks * share // sum(shares))
    starts[-1] = blocks

    slots = jnp.zeros((8, LANES), F32)
    bases, reaches, received = [], [], []
    after = rows
    for bit in range(device_bits):
        other = lax.ppermute(payload, "seq", [(i, i ^ 1 << bit) for i in range(ranks)])
        if bit < len(starts) - 1 and starts[bit + 1] > starts[bit]:
            base, reach, slots = local(starts[bit], starts[bit + 1] - starts[bit], slots, after)
            bases.append(base)
            reaches.append(reach)
        received.append(other)
        if bit + 1 < device_bits:
            mine, mine_exp, payload = pl.pallas_call(
                functools.partial(merge_kernel, bit),
                in_specs=[SMEM_SPEC] + [VMEM_SPEC] * 3 + [ANY_SPEC],
                out_specs=(VMEM_SPEC,) * 3,
                out_shape=carried,
                compiler_params=grant(8),
                cost_estimate=cost(4 * state * width, state * width * 12),
                name="merge",
            )(flags, other, mine, mine_exp, slots)
            after = mine_exp

    return pl.pallas_call(
        functools.partial(final_kernel, starts, local_bits, device_bits),
        in_specs=[SMEM_SPEC] + [VMEM_SPEC] * (2 + device_bits + 2 * len(bases)),
        out_specs=ANY_SPEC,
        out_shape=sds((tokens, width), BF16),
        scratch_shapes=[
            pltpu.VMEM((device_bits * state, width), BF16),
            pltpu.VMEM((blocks, BLOCK, width), BF16),
            pltpu.SemaphoreType.DMA((blocks,)),
        ],
        compiler_params=grant(12),
        cost_estimate=cost(2 * tokens * width * state * device_bits, tokens * width * 6),
        name="final",
    )(flags, read_t, weight_h, *received, *bases, *reaches)


def solution(mesh):
    placed = (
        P("seq", "head"),
        P("seq", "head"),
        P("seq", "head"),
        P("head", "seq"),
        P("head", "seq"),
        P("head"),
        P(),
        P(None, "seq"),
    )
    return jax.shard_map(
        on_device, mesh=mesh, in_specs=placed, out_specs=P("seq", "head"), check_vma=False
    )
```

```python
import functools

import jax
import jax.numpy as jnp
from jax import lax
from jax.experimental import pallas as pl
from jax.experimental.pallas import tpu as pltpu
from jax.sharding import PartitionSpec as P

BLOCK = 256
HALF = BLOCK // 2
LANES = 128
LOG2E = 1.4426950408889634
F32 = jnp.float32
BF16 = jnp.bfloat16
NT = (((1,), (1,)), ((), ()))
NN = (((1,), (0,)), ((), ()))
TN = (((0,), (0,)), ((), ()))
VMEM_SPEC = pl.BlockSpec(memory_space=pltpu.VMEM)
SMEM_SPEC = pl.BlockSpec(memory_space=pltpu.SMEM)
ANY_SPEC = pl.BlockSpec(memory_space=pl.ANY)
HBM_SPEC = pl.BlockSpec(memory_space=pltpu.HBM)


def dot(a, b, dims=NN):
    return lax.dot_general(a, b, dims, preferred_element_type=F32)


def three(a):
    high = a.astype(BF16)
    rest = a - high.astype(F32)
    middle = rest.astype(BF16)
    return high, middle, (rest - middle.astype(F32)).astype(BF16)


def two(a):
    high = a.astype(BF16).astype(F32)
    return high, a - high


def iota(shape, dim):
    return lax.broadcasted_iota(jnp.int32, shape, dim)


def as_bf16(mask):
    return mask.astype(F32).astype(BF16)


def spread(first_row, padded, heads, width):
    per_head = width // heads
    row = iota((4 * padded, width), 0) - first_row
    lane = iota((4 * padded, width), 1)
    inside = (row >= 0) & (row < 2 * padded)
    row = jnp.where(row >= padded, row - padded, row)
    own = (row * per_head <= lane) & (lane < (row + 1) * per_head) & (row < heads)
    return as_bf16(own & inside)


class Rows:
    def __init__(self, blocks):
        halves = 2 * blocks
        self.after, self.run = 0, halves
        self.middle, self.upper, self.decay = 2 * halves, 2 * halves + blocks, 2 * halves + 2 * blocks
        self.total = 2 * halves + 3 * blocks
        self.skip = self.total + 8 - self.total % 8
        self.count = -(-(self.skip + 8) // 16) * 16

    def ranges(self, tokens):
        halves = tokens // HALF
        blocks = halves // 2
        k = iota((self.count, 1), 0)
        low = (k + 1) * HALF
        high = jnp.full_like(k, tokens)
        low = jnp.where(k >= self.run, 0, low)
        high = jnp.where(k >= self.run, (k - self.run) * HALF, high)
        for first, start, size in (
            (self.middle, 0, HALF), (self.upper, HALF, HALF), (self.decay, 0, BLOCK)
        ):
            here = (k - first) * BLOCK + start
            low = jnp.where(k >= first, here, low)
            high = jnp.where(k >= first, here + size, high)
        low = jnp.where(k >= self.total, 0, low)
        high = jnp.where(k == self.total, tokens, jnp.where(k > self.total, 0, high))
        return low, high


def prep_kernel(
    heads, padded, layout, log_decay_far, step_size_far, level_index_far, level_table_far, gain_far,
    factors, columns, cum_h, weight_h, rows,
    log_decay, step_size, level_index, level_table, gain, decay, steps, packed, sems,
):
    pairs = (
        (log_decay_far, log_decay), (step_size_far, step_size), (level_index_far, level_index),
        (level_table_far, level_table), (gain_far, gain),
    )
    copies = [pltpu.make_async_copy(far, near, sems.at[n]) for n, (far, near) in enumerate(pairs)]
    for copy in copies:
        copy.start()
    tokens = log_decay.shape[1]
    width = rows.shape[1]
    blocks = tokens // BLOCK
    decay[...] = jnp.zeros_like(decay)
    steps[...] = jnp.zeros_like(steps)
    for copy in copies:
        copy.wait()
    decay[0:heads, :] = log_decay[...]
    steps[0:heads, :] = step_size[...]
    lower = as_bf16(iota((BLOCK, BLOCK), 0) >= iota((BLOCK, BLOCK), 1))
    levels = level_index.shape[0]
    weight = jnp.zeros(level_index.shape, F32)
    index = level_index[...]
    for entry in range(level_table.shape[1]):
        weight = weight + jnp.where(index == entry, level_table[:, entry : entry + 1], 0.0)
    weight_h[...] = weight
    packed[...] = jnp.zeros_like(packed)
    for c in range(blocks):
        at = slice(c * BLOCK, (c + 1) * BLOCK)
        high, middle, low = three(decay[:, at])
        cum = (dot(low, lower, NT) + dot(middle, lower, NT)) + dot(high, lower, NT)
        step = steps[:, at]
        mid = cum[:, HALF - 1 : HALF]
        end = cum[:, BLOCK - 1 : BLOCK]
        first = iota((padded, BLOCK), 1) < HALF
        column = two(step * jnp.exp(jnp.where(first, mid, end) - cum))
        row = two(jnp.exp(cum - jnp.where(first, 0.0, mid)))
        four = jnp.concatenate([column[0], column[1], row[0], row[1]], 0)
        factors[at, :] = four.T.astype(BF16)
        scaled = cum * LOG2E
        cum_h[:, at] = scaled - jnp.log2(step)
        packed[0:padded, :] = scaled
        packed[padded : padded + levels, :] = weight_h[:, at]
        columns[at, :] = packed[...].T
    token = iota((rows.shape[0], tokens), 1)
    begin, finish = layout.ranges(tokens)
    chosen = as_bf16((token >= begin) & (token < finish))
    high, middle, low = three(decay[...])
    sums = (dot(chosen, low, NT) + dot(chosen, middle, NT)) + dot(chosen, high, NT)
    high, low = two(jnp.exp(sums))
    per_head = width // heads
    head = iota((padded, width), 0) * per_head
    lane = iota((padded, width), 1)
    own = as_bf16((head <= lane) & (lane < head + per_head))
    rows[...] = dot(high.astype(BF16), own) + dot(low.astype(BF16), own)
    gains = jnp.broadcast_to(gain[...], (8, heads))
    high, middle, low = three(gains)
    own = own[:heads]
    rows[layout.skip : layout.skip + 8, :] = (dot(low, own) + dot(middle, own)) + dot(high, own)


def scale_kernel(heads, padded, layout, mixer, factors, rows, scaled, to_total):
    tokens, width = mixer.shape
    wide = spread(0, padded, heads, width)

    def step(a, carry):
        at = pl.ds(pl.multiple_of(a * HALF, HALF), HALF)
        row = rows[pl.ds(layout.after + a, 1), :]
        value = mixer[at, :].astype(F32) * dot(factors[at, :], wide)
        scaled[at, :] = value.astype(BF16)
        to_total[at, :] = (value * row).astype(BF16)
        return carry

    lax.fori_loop(0, tokens // HALF, step, 0)


def exp_rows(total, count):
    where = iota((count, total.shape[1]), 0)
    high = total.astype(BF16).astype(F32)
    return jnp.where(where == 0, high, jnp.where(where == 1, total - high, 0.0)).astype(BF16)


def state_kernel(layout, to_total, write_t, rows, mine, mine_exp, payload):
    state = write_t.shape[0]
    new = dot(write_t[...], to_total[...])
    mine[...] = new
    payload[0:state, :] = new.astype(BF16)
    total = rows[layout.total : layout.total + 1, :]
    payload[state:, :] = exp_rows(total, payload.shape[0] - state)
    mine_exp[...] = jnp.broadcast_to(total, mine_exp.shape)


def upper_half(bit, width):
    rank = lax.axis_index("seq")
    return ((jnp.zeros((1, width), jnp.int32) + rank) >> bit) & 1 > 0


def merge_kernel(bit, received, mine, mine_exp, after, payload, *more):
    state, width = mine.shape
    extra = received[state:, :].astype(F32)
    other_exp = extra[0:1] + extra[1:2]
    own_exp = mine_exp[0:1, :]
    upper = upper_half(bit, width)
    own_scale = jnp.where(upper, 1.0, other_exp)
    other_scale = jnp.where(upper, own_exp, 1.0)
    new = own_scale * mine[...] + other_scale * received[0:state, :].astype(F32)
    payload[0:state, :] = new.astype(BF16)
    total = own_exp * other_exp
    payload[state:, :] = exp_rows(total, payload.shape[0] - state)
    if more:
        merged, merged_exp = more
        merged[...] = new
        merged_exp[...] = jnp.broadcast_to(total, merged_exp.shape)


def join_kernel(first, second, joined):
    joined[: first.shape[0], :] = first[...]
    joined[first.shape[0] :, :] = second[...]


def local_kernel(
    heads, padded, bits, first, count, layout, tile,
    mixer, scaled, write_t, read_t, factors, columns, cum_h, weight_h, rows, slots_in, after,
    base, reach, slots, scores, inter, fresh,
):
    width = mixer.shape[1]
    per_head = width // heads
    heads_here = LANES // per_head
    skip = rows[layout.skip : layout.skip + 1, :]
    wide = spread(2 * padded, padded, heads, width)
    if first == 0:
        slots[...] = jnp.zeros_like(slots)
    else:
        slots[...] = slots_in[...]

    def block(g, carry):
        c = first + g
        at = pl.ds(pl.multiple_of(c * BLOCK, BLOCK), BLOCK)
        out_at = pl.ds(pl.multiple_of(g * BLOCK, BLOCK), BLOCK)
        read = read_t[:, at]
        write = write_t[:, at]

        inter[...] = jnp.zeros_like(inter)
        for bit in range(bits):

            @pl.when((c >> bit) & 1 == 1)
            def _(bit=bit):
                query = (read.astype(F32) * weight_h[bit + 1 : bit + 2, at]).astype(BF16)
                inter[...] += dot(query, slots[bit].astype(BF16), TN)

        weighted = dot(read, write, TN) * columns[at, padded : padded + 1]
        causal = iota((HALF, HALF), 0) >= iota((HALF, HALF), 1)
        off_scores = weighted[HALF:, :HALF].astype(BF16)
        scores[0] = jnp.where(causal, weighted[:HALF, :HALF], 0.0)
        scores[1] = jnp.where(causal, weighted[HALF:, HALF:], 0.0)
        lane = iota((HALF, LANES), 1)
        own = [as_bf16((lane >= k * per_head) & (lane < (k + 1) * per_head)) for k in range(heads_here)]
        middle = rows[pl.ds(layout.middle + c, 1), :]
        for half in range(2):
            half_at = pl.ds(pl.multiple_of(c * BLOCK + half * HALF, HALF), HALF)
            put_at = pl.ds(pl.multiple_of(g * BLOCK + half * HALF, HALF), HALF)
            first_at = pl.ds(pl.multiple_of(c * BLOCK, HALF), HALF)
            row_at = slice(half * HALF, (half + 1) * HALF)
            run = rows[pl.ds(layout.run + 2 * c + half, 1), :]
            for left in range(0, width, tile):
                lanes = slice(left, left + tile)
                near = dot(factors[half_at, :], wide[:, lanes])
                reach[put_at, lanes] = near * run[:, lanes]
                if half == 0:
                    rest = near * inter[row_at, lanes]
                else:
                    off = dot(off_scores, scaled[first_at, lanes])
                    rest = near * (off + middle[:, lanes] * inter[row_at, lanes])
                for inner in range(left, left + tile, LANES):
                    here = slice(inner, inner + LANES)
                    head = inner // per_head
                    value = mixer[half_at, here]
                    left_side = []
                    for k in range(heads_here):
                        gap = columns[half_at, head + k : head + k + 1] - cum_h[head + k : head + k + 1, half_at]
                        mixing = scores[half] * jnp.exp2(jnp.minimum(gap, 0.0))
                        left_side.append(mixing.astype(BF16))
                    part = dot(
                        jnp.concatenate(left_side, 1),
                        jnp.concatenate([value * mask for mask in own], 0),
                    )
                    base[put_at, here] = (
                        part + rest[:, inner - left : inner - left + LANES]
                        + skip[:, here] * value.astype(F32)
                    )

        upper = rows[pl.ds(layout.upper + c, 1), :]
        start = pl.multiple_of(c * BLOCK, HALF)
        fresh[...] = upper * dot(
            write_t[:, pl.ds(start, HALF)], scaled[pl.ds(start, HALF), :]
        ) + dot(write_t[:, pl.ds(start + HALF, HALF)], scaled[pl.ds(start + HALF, HALF), :])
        shrink = rows[pl.ds(layout.decay + c, 1), :]
        for bit in range(bits):
            below = (1 << bit) - 1

            @pl.when(((c >> bit) & 1 == 1) & (c & below == below))
            def _(bit=bit):
                fresh[...] += shrink * slots[bit]

            @pl.when(((c >> bit) & 1 == 1) & (c & below != below))
            def _(bit=bit):
                slots[bit] = shrink * slots[bit]

            @pl.when(((c >> bit) & 1 == 0) & (c & below == below))
            def _(bit=bit):
                slots[bit] = fresh[...]

        return carry

    lax.fori_loop(0, count, block, 0)


def bucket_rows(received, bits, state, width, wanted):
    running = jnp.ones((1, width), F32)
    out = []
    for bit in range(bits):
        upper = upper_half(bit, width)
        if bit in wanted:
            scale = jnp.where(upper, running, 0.0)
            out.append((received[bit][0:state, :].astype(F32) * scale).astype(BF16))
        if bit + 1 < bits:
            extra = received[bit][state:, :].astype(F32)
            running = jnp.where(upper, running * (extra[0:1] + extra[1:2]), running)
    return jnp.concatenate(out, 0) if len(out) > 1 else out[0]


def read_levels(read_t, weight_h, at, levels):
    read_f = read_t[:, at].astype(F32)
    queries = [(read_f * weight_h[level : level + 1, at]).astype(BF16) for level in levels]
    return jnp.concatenate(queries, 0) if len(queries) > 1 else queries[0]


def middle_kernel(starts, local_bits, bits, read_t, weight_h, *rest):
    pieces = len(starts) - 1
    received, rest = rest[:bits], rest[bits:]
    bases, reaches, rest = rest[:pieces], rest[pieces : 2 * pieces], rest[2 * pieces :]
    outs, buckets = rest[:pieces], rest[pieces]
    buckets[...] = bucket_rows(received, bits, read_t.shape[0], buckets.shape[1], range(bits))
    for piece in range(pieces):

        def block(g, carry, piece=piece):
            at = pl.ds(pl.multiple_of((starts[piece] + g) * BLOCK, BLOCK), BLOCK)
            here = pl.ds(pl.multiple_of(g * BLOCK, BLOCK), BLOCK)
            levels = [local_bits + 1 + bit for bit in range(bits)]
            part = dot(read_levels(read_t, weight_h, at, levels), buckets[...], TN)
            outs[piece][here, :] = bases[piece][here, :] + part * reaches[piece][here, :]
            return carry

        lax.fori_loop(0, starts[piece + 1] - starts[piece], block, 0)


def final_kernel(starts, local_bits, bits, read_t, weight_h, *rest):
    pieces = len(starts) - 1
    received, rest = rest[:bits], rest[bits:]
    bases, reaches, rest = rest[:pieces], rest[pieces : 2 * pieces], rest[2 * pieces :]
    out, buckets, ready, sems = rest
    buckets[...] = bucket_rows(received, bits, read_t.shape[0], out.shape[1], [bits - 1])

    def copy(c, at):
        return pltpu.make_async_copy(ready.at[c], out.at[pl.ds(at, BLOCK), :], sems.at[c])

    for piece in range(pieces):

        def block(g, carry, piece=piece):
            c = starts[piece] + g
            at = pl.multiple_of(c * BLOCK, BLOCK)
            here = pl.ds(pl.multiple_of(g * BLOCK, BLOCK), BLOCK)
            query = read_levels(read_t, weight_h, pl.ds(at, BLOCK), [local_bits + bits])
            part = dot(query, buckets[...], TN)
            ready[c] = (bases[piece][here, :] + part * reaches[piece][here, :]).astype(BF16)
            copy(c, at).start()
            return carry

        lax.fori_loop(0, starts[piece + 1] - starts[piece], block, 0)
    for c in range(starts[-1]):
        copy(c, c * BLOCK).wait()


def gather_columns(mine, axis, other):
    pieces, _ = lax.optimization_barrier((mine, other)) if other is not None else (mine, None)
    size = lax.axis_size(axis)
    stride = size // 2
    first = None
    while stride:
        other = lax.ppermute(pieces, axis, [(i, i ^ stride) for i in range(size)])
        first = other if first is None else first
        pieces = pl.pallas_call(
            join_kernel,
            in_specs=[VMEM_SPEC] * 2,
            out_specs=VMEM_SPEC,
            out_shape=jax.ShapeDtypeStruct((2 * pieces.shape[0], pieces.shape[1]), BF16),
            compiler_params=grant(2),
            cost_estimate=cost(0, 4 * pieces.size),
            name="join",
        )(pieces, other)
        stride //= 2
    return pieces, first


def cost(flops, bytes_accessed):
    return pl.CostEstimate(flops=flops, bytes_accessed=bytes_accessed, transcendentals=0)


def grant(mebibytes):
    return pltpu.CompilerParams(vmem_limit_bytes=mebibytes << 20)


def on_device(
    mixer_input, write_map, read_map, step_size, log_decay, skip_gain, level_table, level_index
):
    tokens, width = mixer_input.shape
    heads = log_decay.shape[0]
    per_head = width // heads
    blocks = tokens // BLOCK
    local_bits = blocks.bit_length() - 1
    ranks = lax.axis_size("seq")
    device_bits = ranks.bit_length() - 1
    levels = level_table.shape[0]
    padded = LANES // 4
    tile = 256
    layout = Rows(blocks)
    sds = jax.ShapeDtypeStruct

    write_t, arrived = gather_columns(write_map.T, "head", None)
    read_t, _ = gather_columns(read_map.T, "head", arrived)
    state = write_t.shape[0]

    factors, columns, cum_h, weight_h, rows = pl.pallas_call(
        functools.partial(prep_kernel, heads, padded, layout),
        in_specs=[HBM_SPEC] * 5,
        out_specs=(VMEM_SPEC,) * 5,
        out_shape=(
            sds((tokens, LANES), BF16), sds((tokens, LANES), F32), sds((padded, tokens), F32),
            sds((levels, tokens), F32), sds((layout.count, width), F32),
        ),
        scratch_shapes=[
            pltpu.VMEM((heads, tokens), F32),
            pltpu.VMEM((heads, tokens), F32),
            pltpu.VMEM(level_index.shape, jnp.int32),
            pltpu.VMEM(level_table.shape, F32),
            pltpu.VMEM((1, heads), F32),
            pltpu.VMEM((padded, tokens), F32),
            pltpu.VMEM((padded, tokens), F32),
            pltpu.VMEM((LANES, BLOCK), F32),
            pltpu.SemaphoreType.DMA((5,)),
        ],
        compiler_params=grant(6),
        cost_estimate=cost(2_000_000_000, 4_000_000),
        name="prep",
    )(log_decay, step_size, level_index, level_table, skip_gain[None, :])

    scaled, to_total = pl.pallas_call(
        functools.partial(scale_kernel, heads, padded, layout),
        in_specs=[VMEM_SPEC] * 3,
        out_specs=(VMEM_SPEC,) * 2,
        out_shape=(sds((tokens, width), BF16),) * 2,
        compiler_params=grant(4),
        cost_estimate=cost(3_000_000_000, tokens * width * 6),
        name="scale",
    )(mixer_input, factors, rows)

    payload_rows = state + 8
    carried = (sds((state, width), F32), sds((8, width), F32), sds((payload_rows, width), BF16))
    mine, mine_exp, payload = pl.pallas_call(
        functools.partial(state_kernel, layout),
        in_specs=[VMEM_SPEC] * 3,
        out_specs=(VMEM_SPEC,) * 3,
        out_shape=carried,
        compiler_params=grant(4),
        cost_estimate=cost(2 * tokens * width * state, tokens * width * 2),
        name="state",
    )(to_total, write_t, rows)

    def local(first, count, slots, after):
        return pl.pallas_call(
            functools.partial(
                local_kernel, heads, padded, local_bits, first, count, layout, tile
            ),
            in_specs=[VMEM_SPEC] * 10 + [ANY_SPEC],
            out_specs=(VMEM_SPEC,) * 3,
            out_shape=(
                sds((count * BLOCK, width), F32), sds((count * BLOCK, width), F32),
                sds((local_bits, state, width), F32),
            ),
            scratch_shapes=[
                pltpu.VMEM((2, HALF, HALF), F32),
                pltpu.VMEM((BLOCK, width), F32),
                pltpu.VMEM((state, width), F32),
            ],
            compiler_params=grant(8),
            cost_estimate=cost(count * BLOCK * width * 2 * 2000, count * BLOCK * width * 8),
            name="local",
        )(
            mixer_input, scaled, write_t, read_t, factors, columns, cum_h, weight_h, rows,
            slots, after,
        )

    shares = [1] * (device_bits - 2) + [1, 2] if device_bits > 1 else [1]
    starts = [0]
    for k, share in enumerate(shares):
        starts.append(starts[-1] + blocks * share // sum(shares))
    starts[-1] = blocks

    slots = jnp.zeros((8, LANES), F32)
    bases, reaches, received = [], [], []
    after = rows
    for bit in range(device_bits):
        other = lax.ppermute(payload, "seq", [(i, i ^ 1 << bit) for i in range(ranks)])
        if bit < len(starts) - 1 and starts[bit + 1] > starts[bit]:
            base, reach, slots = local(starts[bit], starts[bit + 1] - starts[bit], slots, after)
            bases.append(base)
            reaches.append(reach)
        received.append(other)
        if bit + 1 < device_bits:
            last = bit + 2 == device_bits
            shapes = (carried[2],) if last else (carried[2],) + carried[:2]
            payload, *more = pl.pallas_call(
                functools.partial(merge_kernel, bit),
                in_specs=[VMEM_SPEC] * 3 + [ANY_SPEC],
                out_specs=(VMEM_SPEC,) * len(shapes),
                out_shape=shapes,
                compiler_params=grant(4),
                cost_estimate=cost(4 * state * width, state * width * 12),
                name="merge",
            )(other, mine, mine_exp, slots)
            if more:
                mine, mine_exp = more
            after = payload

    if device_bits > 1:
        count = len(bases)
        bases = pl.pallas_call(
            functools.partial(middle_kernel, starts, local_bits, device_bits - 1),
            in_specs=[VMEM_SPEC] * (2 + device_bits - 1 + 2 * count),
            out_specs=(VMEM_SPEC,) * count,
            out_shape=tuple(sds(base.shape, F32) for base in bases),
            input_output_aliases={2 + device_bits - 1 + k: k for k in range(count)},
            scratch_shapes=[pltpu.VMEM(((device_bits - 1) * state, width), BF16)],
            compiler_params=grant(4),
            cost_estimate=cost(2 * tokens * width * state * 2, tokens * width * 6),
            name="middle",
        )(read_t, weight_h, *received[:-1], *bases, *reaches)

    return pl.pallas_call(
        functools.partial(final_kernel, starts, local_bits, device_bits),
        in_specs=[VMEM_SPEC] * (2 + device_bits + 2 * len(bases)),
        out_specs=ANY_SPEC,
        out_shape=sds((tokens, width), BF16),
        scratch_shapes=[
            pltpu.VMEM((state, width), BF16),
            pltpu.VMEM((blocks, BLOCK, width), BF16),
            pltpu.SemaphoreType.DMA((blocks,)),
        ],
        compiler_params=grant(8),
        cost_estimate=cost(2 * tokens * width * state * device_bits, tokens * width * 6),
        name="final",
    )(read_t, weight_h, *received, *bases, *reaches)


def solution(mesh):
    placed = (
        P("seq", "head"),
        P("seq", "head"),
        P("seq", "head"),
        P("head", "seq"),
        P("head", "seq"),
        P("head"),
        P(),
        P(None, "seq"),
    )
    return jax.shard_map(
        on_device, mesh=mesh, in_specs=placed, out_specs=P("seq", "head"), check_vma=False
    )
```

```python
import functools

import jax
import jax.numpy as jnp
from jax import lax
from jax.experimental import pallas as pl
from jax.experimental.pallas import tpu as pltpu
from jax.sharding import PartitionSpec as P


BLOCK = 256
HALF = BLOCK // 2
LANES = 128
LOG2E = 1.4426950408889634
F32 = jnp.float32
BF16 = jnp.bfloat16
NT = (((1,), (1,)), ((), ()))
NN = (((1,), (0,)), ((), ()))
TN = (((0,), (0,)), ((), ()))
VMEM_SPEC = pl.BlockSpec(memory_space=pltpu.VMEM)
SMEM_SPEC = pl.BlockSpec(memory_space=pltpu.SMEM)
ANY_SPEC = pl.BlockSpec(memory_space=pl.ANY)
HBM_SPEC = pl.BlockSpec(memory_space=pltpu.HBM)


def dot(a, b, dims=NN):
    return lax.dot_general(a, b, dims, preferred_element_type=F32)


def three(a):
    high = a.astype(BF16)
    rest = a - high.astype(F32)
    middle = rest.astype(BF16)
    return high, middle, (rest - middle.astype(F32)).astype(BF16)


def two(a):
    high = a.astype(BF16).astype(F32)
    return high, a - high


def iota(shape, dim):
    return lax.broadcasted_iota(jnp.int32, shape, dim)


def as_bf16(mask):
    return mask.astype(F32).astype(BF16)


def spread(first_row, padded, heads, width):
    per_head = width // heads
    row = iota((4 * padded, width), 0) - first_row
    lane = iota((4 * padded, width), 1)
    inside = (row >= 0) & (row < 2 * padded)
    row = jnp.where(row >= padded, row - padded, row)
    own = (row * per_head <= lane) & (lane < (row + 1) * per_head) & (row < heads)
    return as_bf16(own & inside)


class Rows:
    def __init__(self, blocks):
        halves = 2 * blocks
        self.after, self.run = 0, halves
        self.middle, self.upper, self.decay = 2 * halves, 2 * halves + blocks, 2 * halves + 2 * blocks
        self.total = 2 * halves + 3 * blocks
        self.skip = self.total + 8 - self.total % 8
        self.count = -(-(self.skip + 8) // 16) * 16

    def ranges(self, tokens):
        halves = tokens // HALF
        blocks = halves // 2
        k = iota((self.count, 1), 0)
        low = (k + 1) * HALF
        high = jnp.full_like(k, tokens)
        low = jnp.where(k >= self.run, 0, low)
        high = jnp.where(k >= self.run, (k - self.run) * HALF, high)
        for first, start, size in (
            (self.middle, 0, HALF), (self.upper, HALF, HALF), (self.decay, 0, BLOCK)
        ):
            here = (k - first) * BLOCK + start
            low = jnp.where(k >= first, here, low)
            high = jnp.where(k >= first, here + size, high)
        low = jnp.where(k >= self.total, 0, low)
        high = jnp.where(k == self.total, tokens, jnp.where(k > self.total, 0, high))
        return low, high


def prep_kernel(
    heads, padded, layout, log_decay_far, step_size_far, level_index_far, level_table_far, gain_far,
    factors, columns, cum_h, weight_h, rows,
    log_decay, step_size, level_index, level_table, gain, decay, steps, packed, sems,
):
    pairs = (
        (log_decay_far, log_decay), (step_size_far, step_size), (level_index_far, level_index),
        (level_table_far, level_table), (gain_far, gain),
    )
    copies = [pltpu.make_async_copy(far, near, sems.at[n]) for n, (far, near) in enumerate(pairs)]
    for copy in copies:
        copy.start()
    tokens = log_decay.shape[1]
    width = rows.shape[1]
    blocks = tokens // BLOCK
    decay[...] = jnp.zeros_like(decay)
    steps[...] = jnp.zeros_like(steps)
    for copy in copies:
        copy.wait()
    decay[0:heads, :] = log_decay[...]
    steps[0:heads, :] = step_size[...]
    lower = as_bf16(iota((BLOCK, BLOCK), 0) >= iota((BLOCK, BLOCK), 1))
    levels = level_index.shape[0]
    weight = jnp.zeros(level_index.shape, F32)
    index = level_index[...]
    for entry in range(level_table.shape[1]):
        weight = weight + jnp.where(index == entry, level_table[:, entry : entry + 1], 0.0)
    weight_h[...] = weight
    packed[...] = jnp.zeros_like(packed)
    for c in range(blocks):
        at = slice(c * BLOCK, (c + 1) * BLOCK)
        high, middle, low = three(decay[:, at])
        cum = (dot(low, lower, NT) + dot(middle, lower, NT)) + dot(high, lower, NT)
        step = steps[:, at]
        mid = cum[:, HALF - 1 : HALF]
        end = cum[:, BLOCK - 1 : BLOCK]
        first = iota((padded, BLOCK), 1) < HALF
        column = two(step * jnp.exp(jnp.where(first, mid, end) - cum))
        row = two(jnp.exp(cum - jnp.where(first, 0.0, mid)))
        four = jnp.concatenate([column[0], column[1], row[0], row[1]], 0)
        factors[at, :] = four.T.astype(BF16)
        scaled = cum * LOG2E
        cum_h[:, at] = scaled - jnp.log2(step)
        packed[0:padded, :] = scaled
        packed[padded : padded + levels, :] = weight_h[:, at]
        columns[at, :] = packed[...].T
    token = iota((rows.shape[0], tokens), 1)
    begin, finish = layout.ranges(tokens)
    chosen = as_bf16((token >= begin) & (token < finish))
    high, middle, low = three(decay[...])
    sums = (dot(chosen, low, NT) + dot(chosen, middle, NT)) + dot(chosen, high, NT)
    high, low = two(jnp.exp(sums))
    per_head = width // heads
    head = iota((padded, width), 0) * per_head
    lane = iota((padded, width), 1)
    own = as_bf16((head <= lane) & (lane < head + per_head))
    rows[...] = dot(high.astype(BF16), own) + dot(low.astype(BF16), own)
    gains = jnp.broadcast_to(gain[...], (8, heads))
    high, middle, low = three(gains)
    own = own[:heads]
    rows[layout.skip : layout.skip + 8, :] = (dot(low, own) + dot(middle, own)) + dot(high, own)


def scale_kernel(heads, padded, layout, mixer, factors, rows, scaled, to_total):
    tokens, width = mixer.shape
    wide = spread(0, padded, heads, width)

    def step(a, carry):
        at = pl.ds(pl.multiple_of(a * HALF, HALF), HALF)
        row = rows[pl.ds(layout.after + a, 1), :]
        value = mixer[at, :].astype(F32) * dot(factors[at, :], wide)
        scaled[at, :] = value.astype(BF16)
        to_total[at, :] = (value * row).astype(BF16)
        return carry

    lax.fori_loop(0, tokens // HALF, step, 0)


def exp_rows(total, count):
    where = iota((count, total.shape[1]), 0)
    high = total.astype(BF16).astype(F32)
    return jnp.where(where == 0, high, jnp.where(where == 1, total - high, 0.0)).astype(BF16)


def own_columns(width):
    rank = lax.axis_index("seq")
    mine = (rank & 1) * (width // 2)
    other = width // 2 - mine
    aligned = lambda at: pl.ds(pl.multiple_of(at, LANES), width // 2)
    return aligned(mine), aligned(other)


def state_kernel(layout, to_total, write_t, rows, first, second, mine, mine_exp, whole):
    state = write_t.shape[0]
    own, other = own_columns(whole.shape[1])
    whole[...] = dot(write_t[...], to_total[...])
    for payload, at in ((first, other), (second, own)):
        payload[0:state, :] = whole[:, at].astype(BF16)
        total = rows[layout.total : layout.total + 1, at]
        payload[state:, :] = exp_rows(total, payload.shape[0] - state)
    mine[...] = whole[:, own]
    mine_exp[...] = jnp.broadcast_to(rows[layout.total : layout.total + 1, own], mine_exp.shape)


def upper_half(bit, width):
    rank = lax.axis_index("seq")
    return ((jnp.zeros((1, width), jnp.int32) + rank) >> bit) & 1 > 0


def merge_kernel(bit, received, mine, mine_exp, after, payload, *more):
    state, width = mine.shape
    extra = received[state:, :].astype(F32)
    other_exp = extra[0:1] + extra[1:2]
    own_exp = mine_exp[0:1, :]
    upper = upper_half(bit, width)
    own_scale = jnp.where(upper, 1.0, other_exp)
    other_scale = jnp.where(upper, own_exp, 1.0)
    new = own_scale * mine[...] + other_scale * received[0:state, :].astype(F32)
    payload[0:state, :] = new.astype(BF16)
    total = own_exp * other_exp
    payload[state:, :] = exp_rows(total, payload.shape[0] - state)
    if more:
        merged, merged_exp = more
        merged[...] = new
        merged_exp[...] = jnp.broadcast_to(total, merged_exp.shape)


def join_kernel(first, second, *rest):
    joined = rest[-1]
    joined[: first.shape[0], :] = first[...]
    joined[first.shape[0] :, :] = second[...]


def local_kernel(
    heads, padded, bits, first, count, layout, tile,
    mixer, scaled, write_t, read_t, factors, columns, cum_h, weight_h, rows, slots_in, after,
    base, reach, slots, scores, narrow, off_scores, queries,
):
    width = mixer.shape[1]
    state = write_t.shape[0]
    per_head = width // heads
    heads_here = LANES // per_head
    wide = spread(2 * padded, padded, heads, width)
    causal = iota((HALF, HALF), 0) >= iota((HALF, HALF), 1)
    lane = iota((HALF, LANES), 1)
    own = [as_bf16((lane >= k * per_head) & (lane < (k + 1) * per_head)) for k in range(heads_here)]
    live = [bit for bit in range(bits) if (first >> bit) & 1]
    for bit in live:
        slots[bit] = slots_in[bit]
        narrow[bit * state : (bit + 1) * state, :] = slots_in[bit].astype(BF16)

    def head_part(c):
        at = slice(c * BLOCK, (c + 1) * BLOCK)
        live = [bit for bit in range(bits) if (c >> bit) & 1]
        if live:
            queries[0 : len(live) * state, :] = read_levels(read_t, weight_h, at, [bit + 1 for bit in live])
        weighted = dot(read_t[:, at], write_t[:, at], TN) * columns[at, padded : padded + 1]
        off_scores[...] = weighted[HALF:, :HALF].astype(BF16)
        scores[0] = jnp.where(causal, weighted[:HALF, :HALF], 0.0)
        scores[1] = jnp.where(causal, weighted[HALF:, HALF:], 0.0)

    def half_part(c, half):
        live = [bit for bit in range(bits) if (c >> bit) & 1]
        low = c * BLOCK + half * HALF
        half_at = slice(low, low + HALF)
        put_at = slice(low - first * BLOCK, low - first * BLOCK + HALF)
        for left in range(0, width, tile):
            lanes = slice(left, left + tile)
            near = dot(factors[half_at, :], wide[:, lanes])
            reach[put_at, lanes] = near * rows[layout.run + 2 * c + half : layout.run + 2 * c + half + 1, lanes]
            rest = None
            if half == 1:
                rest = dot(off_scores[...], scaled[c * BLOCK : c * BLOCK + HALF, lanes])
            if live:
                stored = [narrow[bit * state : (bit + 1) * state, lanes] for bit in live]
                stored = jnp.concatenate(stored, 0) if len(stored) > 1 else stored[0]
                level = dot(
                    queries[0 : len(live) * state, half * HALF : (half + 1) * HALF], stored, TN
                )
                middle = rows[layout.middle + c : layout.middle + c + 1, lanes]
                rest = level if rest is None else rest + middle * level
            skipped = rows[layout.skip : layout.skip + 1, lanes] * mixer[half_at, lanes].astype(F32)
            rest = skipped if rest is None else skipped + near * rest
            for inner in range(0, tile, LANES):
                here = slice(left + inner, left + inner + LANES)
                head = (left + inner) // per_head
                value = mixer[half_at, here]
                left_side = []
                for k in range(heads_here):
                    gap = columns[half_at, head + k : head + k + 1] - cum_h[head + k : head + k + 1, half_at]
                    mixing = scores[half] * jnp.exp2(jnp.minimum(gap, 0.0))
                    left_side.append(mixing.astype(BF16))
                part = dot(
                    jnp.concatenate(left_side, 1),
                    jnp.concatenate([value * mask for mask in own], 0),
                )
                base[put_at, here] = part + rest[:, inner : inner + LANES]

    def update_part(c):
        live = [bit for bit in range(bits) if (c >> bit) & 1]
        ones = 0
        while ones < bits and (c >> ones) & 1:
            ones += 1
        low = c * BLOCK
        if ones == bits:
            return
        for left in range(0, width, tile):
            lanes = slice(left, left + tile)
            shrink = rows[layout.decay + c : layout.decay + c + 1, lanes]
            upper = rows[layout.upper + c : layout.upper + c + 1, lanes]
            fresh = upper * dot(
                write_t[:, low : low + HALF], scaled[low : low + HALF, lanes]
            ) + dot(write_t[:, low + HALF : low + BLOCK], scaled[low + HALF : low + BLOCK, lanes])
            for bit in range(ones):
                fresh = fresh + shrink * slots[bit, :, lanes]
            slots[ones, :, lanes] = fresh
            narrow[ones * state : (ones + 1) * state, lanes] = fresh.astype(BF16)
            for bit in live:
                if bit > ones:
                    kept = shrink * slots[bit, :, lanes]
                    slots[bit, :, lanes] = kept
                    narrow[bit * state : (bit + 1) * state, lanes] = kept.astype(BF16)

    when_here = pl.when(lax.axis_index("seq") >= 0)
    for c in range(first, first + count):
        when_here(functools.partial(head_part, c))
        when_here(functools.partial(half_part, c, 0))
        when_here(functools.partial(half_part, c, 1))
        when_here(functools.partial(update_part, c))


def bucket_rows(received, bits, state, width, wanted):
    running = jnp.ones((1, width), F32)
    out = []
    for bit in range(bits):
        upper = upper_half(bit, width)
        if bit in wanted:
            scale = jnp.where(upper, running, 0.0)
            out.append((received[bit][0:state, :].astype(F32) * scale).astype(BF16))
        if bit + 1 < bits:
            extra = received[bit][state:, :].astype(F32)
            running = jnp.where(upper, running * (extra[0:1] + extra[1:2]), running)
    return jnp.concatenate(out, 0) if len(out) > 1 else out[0]


def read_levels(read_t, weight_h, at, levels):
    read_f = read_t[:, at].astype(F32)
    queries = [(read_f * weight_h[level : level + 1, at]).astype(BF16) for level in levels]
    return jnp.concatenate(queries, 0) if len(queries) > 1 else queries[0]


def middle_kernel(starts, local_bits, bits, read_t, weight_h, *rest):
    pieces = len(starts) - 1
    received, rest = (rest[:bits], rest[bits : 2 * bits]), rest[2 * bits :]
    bases, reaches, rest = rest[:pieces], rest[pieces : 2 * pieces], rest[2 * pieces :]
    outs, buckets = rest[:pieces], rest[pieces]
    width = buckets.shape[1]
    for parts, at in zip(received, own_columns(width)):
        buckets[:, at] = bucket_rows(parts, bits, read_t.shape[0], width // 2, range(bits))
    for piece in range(pieces):

        def block(g, carry, piece=piece):
            at = pl.ds(pl.multiple_of((starts[piece] + g) * BLOCK, BLOCK), BLOCK)
            here = pl.ds(pl.multiple_of(g * BLOCK, BLOCK), BLOCK)
            levels = [local_bits + 1 + bit for bit in range(bits)]
            part = dot(read_levels(read_t, weight_h, at, levels), buckets[...], TN)
            outs[piece][here, :] = bases[piece][here, :] + part * reaches[piece][here, :]
            return carry

        lax.fori_loop(0, starts[piece + 1] - starts[piece], block, 0)


def final_kernel(starts, local_bits, bits, side, read_t, weight_h, *rest):
    pieces = len(starts) - 1
    received, rest = rest[:bits], rest[bits:]
    bases, reaches, rest = rest[:pieces], rest[pieces : 2 * pieces], rest[2 * pieces :]
    out, buckets, ready, sems = rest[-4:]
    columns = own_columns(out.shape[1])[side]
    buckets[...] = bucket_rows(received, bits, read_t.shape[0], buckets.shape[1], [bits - 1])

    def copy(c, at):
        return pltpu.make_async_copy(ready.at[c], out.at[pl.ds(at, BLOCK), columns], sems.at[c])

    for piece in range(pieces):

        def block(g, carry, piece=piece):
            c = starts[piece] + g
            at = pl.multiple_of(c * BLOCK, BLOCK)
            here = pl.ds(pl.multiple_of(g * BLOCK, BLOCK), BLOCK)
            query = read_levels(read_t, weight_h, pl.ds(at, BLOCK), [local_bits + bits])
            part = dot(query, buckets[...], TN)
            ready[c] = (bases[piece][here, columns] + part * reaches[piece][here, columns]).astype(BF16)
            copy(c, at).start()
            return carry

        lax.fori_loop(0, starts[piece + 1] - starts[piece], block, 0)
    for c in range(starts[-1]):
        copy(c, c * BLOCK).wait()


def gather_columns(mine, axis, after):
    pieces = mine
    size = lax.axis_size(axis)
    stride = size // 2
    while stride:
        other = lax.ppermute(pieces, axis, [(i, i ^ stride) for i in range(size)])
        pieces = pl.pallas_call(
            join_kernel,
            in_specs=[VMEM_SPEC] * 2 + [ANY_SPEC],
            out_specs=VMEM_SPEC,
            out_shape=jax.ShapeDtypeStruct((2 * pieces.shape[0], pieces.shape[1]), BF16),
            compiler_params=grant(2),
            cost_estimate=cost(0, 4 * pieces.size),
            name="join",
        )(pieces, other, after)
        stride //= 2
    return pieces


def cost(flops, bytes_accessed):
    return pl.CostEstimate(flops=flops, bytes_accessed=bytes_accessed, transcendentals=0)


def grant(mebibytes):
    return pltpu.CompilerParams(vmem_limit_bytes=mebibytes << 20)


def on_device(
    mixer_input, write_map, read_map, step_size, log_decay, skip_gain, level_table, level_index
):
    tokens, width = mixer_input.shape
    heads = log_decay.shape[0]
    blocks = tokens // BLOCK
    local_bits = blocks.bit_length() - 1
    ranks = lax.axis_size("seq")
    device_bits = ranks.bit_length() - 1
    levels = level_table.shape[0]
    padded = LANES // 4
    tile = 256
    layout = Rows(blocks)
    sds = jax.ShapeDtypeStruct

    factors, columns, cum_h, weight_h, rows = pl.pallas_call(
        functools.partial(prep_kernel, heads, padded, layout),
        in_specs=[HBM_SPEC] * 5,
        out_specs=(VMEM_SPEC,) * 5,
        out_shape=(
            sds((tokens, LANES), BF16), sds((tokens, LANES), F32), sds((padded, tokens), F32),
            sds((levels, tokens), F32), sds((layout.count, width), F32),
        ),
        scratch_shapes=[
            pltpu.VMEM((heads, tokens), F32),
            pltpu.VMEM((heads, tokens), F32),
            pltpu.VMEM(level_index.shape, jnp.int32),
            pltpu.VMEM(level_table.shape, F32),
            pltpu.VMEM((1, heads), F32),
            pltpu.VMEM((padded, tokens), F32),
            pltpu.VMEM((padded, tokens), F32),
            pltpu.VMEM((LANES, BLOCK), F32),
            pltpu.SemaphoreType.DMA((5,)),
        ],
        compiler_params=grant(6),
        cost_estimate=cost(2_000_000_000, 4_000_000),
        name="prep",
    )(
        *(
            pltpu.with_memory_space_constraint(value, pltpu.HBM)
            for value in (log_decay, step_size, level_index, level_table, skip_gain[None, :])
        )
    )

    write_t = gather_columns(write_map.T, "head", rows)
    read_t = gather_columns(read_map.T, "head", rows)
    state = write_t.shape[0]

    scaled, to_total = pl.pallas_call(
        functools.partial(scale_kernel, heads, padded, layout),
        in_specs=[VMEM_SPEC] * 3,
        out_specs=(VMEM_SPEC,) * 2,
        out_shape=(sds((tokens, width), BF16),) * 2,
        compiler_params=grant(4),
        cost_estimate=cost(3_000_000_000, tokens * width * 6),
        name="scale",
    )(mixer_input, factors, rows)

    half = width // 2
    carried = (sds((state + 8, half), BF16), sds((state, half), F32), sds((8, half), F32))
    first_out, second_out, mine, mine_exp = pl.pallas_call(
        functools.partial(state_kernel, layout),
        in_specs=[VMEM_SPEC] * 3,
        out_specs=(VMEM_SPEC,) * 4,
        out_shape=carried[:1] + carried,
        scratch_shapes=[pltpu.VMEM((state, width), F32)],
        compiler_params=grant(4),
        cost_estimate=cost(2 * tokens * width * state, tokens * width * 2),
        name="state",
    )(to_total, write_t, rows)

    def local(first, count, slots, after):
        return pl.pallas_call(
            functools.partial(
                local_kernel, heads, padded, local_bits, first, count, layout, tile
            ),
            in_specs=[VMEM_SPEC] * 10 + [ANY_SPEC],
            out_specs=(VMEM_SPEC,) * 3,
            out_shape=(
                sds((count * BLOCK, width), F32), sds((count * BLOCK, width), F32),
                sds((local_bits, state, width), F32),
            ),
            scratch_shapes=[
                pltpu.VMEM((2, HALF, HALF), F32),
                pltpu.VMEM((local_bits * state, width), BF16),
                pltpu.VMEM((HALF, HALF), BF16),
                pltpu.VMEM((local_bits * state, BLOCK), BF16),
            ],
            compiler_params=grant(8),
            cost_estimate=cost(count * BLOCK * width * 2 * 2000, count * BLOCK * width * 8),
            name="local",
        )(
            mixer_input, scaled, write_t, read_t, factors, columns, cum_h, weight_h, rows,
            slots, after,
        )

    def swap(value, bit):
        return lax.ppermute(value, "seq", [(i, i ^ 1 << bit) for i in range(ranks)])

    shares = [3] * (device_bits - 1) + [2]
    starts = [0]
    for share in shares:
        starts.append(starts[-1] + max(1, blocks * share // sum(shares)))
    starts = [min(start, blocks) for start in starts[:-1]] + [blocks]

    slots = jnp.zeros((local_bits, 8, LANES), F32)
    bases, reaches = [], []
    own_parts = [swap(first_out, 0)]
    other_parts = [swap(second_out, 0)]
    after = rows
    payload = None
    for bit in range(device_bits):
        if starts[bit + 1] > starts[bit]:
            base, reach, slots = local(starts[bit], starts[bit + 1] - starts[bit], slots, after)
            bases.append(base)
            reaches.append(reach)
        if bit + 1 < device_bits:
            last = bit + 2 == device_bits
            shapes = carried[:1] if last else carried
            payload, *more = pl.pallas_call(
                functools.partial(merge_kernel, bit),
                in_specs=[VMEM_SPEC] * 3 + [ANY_SPEC],
                out_specs=(VMEM_SPEC,) * len(shapes),
                out_shape=shapes,
                compiler_params=grant(4),
                cost_estimate=cost(2 * state * width, state * width * 6),
                name="merge",
            )(own_parts[bit], mine, mine_exp, slots)
            if more:
                mine, mine_exp = more
            after = payload
            own_parts.append(swap(payload, bit + 1))
            if bit > 0:
                other_parts.append(swap(own_parts[bit], 0))
    starts = sorted(set(starts))
    count = len(bases)

    if device_bits > 1:
        near_bits = device_bits - 1
        bases = pl.pallas_call(
            functools.partial(middle_kernel, starts, local_bits, near_bits),
            in_specs=[VMEM_SPEC] * (2 + 2 * near_bits + 2 * count),
            out_specs=(VMEM_SPEC,) * count,
            out_shape=tuple(sds(base.shape, F32) for base in bases),
            input_output_aliases={2 + 2 * near_bits + k: k for k in range(count)},
            scratch_shapes=[pltpu.VMEM((near_bits * state, width), BF16)],
            compiler_params=grant(4),
            cost_estimate=cost(2 * tokens * width * state * 2, tokens * width * 6),
            name="middle",
        )(read_t, weight_h, *own_parts[:-1], *other_parts, *bases, *reaches)
        other_parts.append(swap(own_parts[-1], 0))

    out = None
    for side, parts in enumerate((own_parts, other_parts)):
        operands = [read_t, weight_h, *parts, *bases, *reaches]
        specs = [VMEM_SPEC] * len(operands)
        aliases = {}
        if out is not None:
            aliases = {len(operands): 0}
            operands.append(out)
            specs.append(ANY_SPEC)
        out = pl.pallas_call(
            functools.partial(final_kernel, starts, local_bits, device_bits, side),
            in_specs=specs,
            out_specs=ANY_SPEC,
            out_shape=sds((tokens, width), BF16),
            input_output_aliases=aliases,
            scratch_shapes=[
                pltpu.VMEM((state, half), BF16),
                pltpu.VMEM((blocks, BLOCK, half), BF16),
                pltpu.SemaphoreType.DMA((blocks,)),
            ],
            compiler_params=grant(6),
            cost_estimate=cost(tokens * width * state, tokens * width * 3),
            name="final",
        )(*operands)
    return out


def solution(mesh):
    placed = (
        P("seq", "head"),
        P("seq", "head"),
        P("seq", "head"),
        P("head", "seq"),
        P("head", "seq"),
        P("head"),
        P(),
        P(None, "seq"),
    )

    return jax.shard_map(
        on_device, mesh=mesh, in_specs=placed, out_specs=P("seq", "head"), check_vma=False
    )
```

```python
import functools

import jax
import jax.numpy as jnp
from jax import lax
from jax.experimental import pallas as pl
from jax.experimental.pallas import tpu as pltpu
from jax.sharding import PartitionSpec as P


BLOCK = 256
HALF = BLOCK // 2
LANES = 128
LOG2E = 1.4426950408889634
F32 = jnp.float32
BF16 = jnp.bfloat16
NT = (((1,), (1,)), ((), ()))
NN = (((1,), (0,)), ((), ()))
TN = (((0,), (0,)), ((), ()))
VMEM_SPEC = pl.BlockSpec(memory_space=pltpu.VMEM)
SMEM_SPEC = pl.BlockSpec(memory_space=pltpu.SMEM)
ANY_SPEC = pl.BlockSpec(memory_space=pl.ANY)
HBM_SPEC = pl.BlockSpec(memory_space=pltpu.HBM)


def dot(a, b, dims=NN):
    return lax.dot_general(a, b, dims, preferred_element_type=F32)


def three(a):
    high = a.astype(BF16)
    rest = a - high.astype(F32)
    middle = rest.astype(BF16)
    return high, middle, (rest - middle.astype(F32)).astype(BF16)


def two(a):
    high = a.astype(BF16).astype(F32)
    return high, a - high


def iota(shape, dim):
    return lax.broadcasted_iota(jnp.int32, shape, dim)


def as_bf16(mask):
    return mask.astype(F32).astype(BF16)


def spread(first_row, padded, heads, width):
    per_head = width // heads
    row = iota((4 * padded, width), 0) - first_row
    lane = iota((4 * padded, width), 1)
    inside = (row >= 0) & (row < 2 * padded)
    row = jnp.where(row >= padded, row - padded, row)
    own = (row * per_head <= lane) & (lane < (row + 1) * per_head) & (row < heads)
    return as_bf16(own & inside)


class Rows:
    def __init__(self, blocks):
        halves = 2 * blocks
        self.after, self.run = 0, halves
        self.middle, self.upper, self.decay = 2 * halves, 2 * halves + blocks, 2 * halves + 2 * blocks
        self.total = 2 * halves + 3 * blocks
        self.skip = self.total + 8 - self.total % 8
        self.count = -(-(self.skip + 8) // 16) * 16

    def ranges(self, tokens):
        halves = tokens // HALF
        blocks = halves // 2
        k = iota((self.count, 1), 0)
        low = (k + 1) * HALF
        high = jnp.full_like(k, tokens)
        low = jnp.where(k >= self.run, 0, low)
        high = jnp.where(k >= self.run, (k - self.run) * HALF, high)
        for first, start, size in (
            (self.middle, 0, HALF), (self.upper, HALF, HALF), (self.decay, 0, BLOCK)
        ):
            here = (k - first) * BLOCK + start
            low = jnp.where(k >= first, here, low)
            high = jnp.where(k >= first, here + size, high)
        low = jnp.where(k >= self.total, 0, low)
        high = jnp.where(k == self.total, tokens, jnp.where(k > self.total, 0, high))
        return low, high


def prep_kernel(
    heads, padded, layout, log_decay_far, step_size_far, level_index_far, level_table_far, gain_far,
    factors, columns, cum_h, weight_h, rows,
    log_decay, step_size, level_index, level_table, gain, decay, steps, packed, sems,
):
    pairs = (
        (log_decay_far, log_decay), (step_size_far, step_size), (level_index_far, level_index),
        (level_table_far, level_table), (gain_far, gain),
    )
    copies = [pltpu.make_async_copy(far, near, sems.at[n]) for n, (far, near) in enumerate(pairs)]
    for copy in copies:
        copy.start()
    tokens = log_decay.shape[1]
    width = rows.shape[1]
    blocks = tokens // BLOCK
    decay[...] = jnp.zeros_like(decay)
    steps[...] = jnp.zeros_like(steps)
    for copy in copies:
        copy.wait()
    decay[0:heads, :] = log_decay[...]
    steps[0:heads, :] = step_size[...]
    lower = as_bf16(iota((BLOCK, BLOCK), 0) >= iota((BLOCK, BLOCK), 1))
    levels = level_index.shape[0]
    weight = jnp.zeros(level_index.shape, F32)
    index = level_index[...]
    for entry in range(level_table.shape[1]):
        weight = weight + jnp.where(index == entry, level_table[:, entry : entry + 1], 0.0)
    weight_h[...] = weight
    packed[...] = jnp.zeros_like(packed)
    for c in range(blocks):
        at = slice(c * BLOCK, (c + 1) * BLOCK)
        high, middle, low = three(decay[:, at])
        cum = (dot(low, lower, NT) + dot(middle, lower, NT)) + dot(high, lower, NT)
        step = steps[:, at]
        mid = cum[:, HALF - 1 : HALF]
        end = cum[:, BLOCK - 1 : BLOCK]
        first = iota((padded, BLOCK), 1) < HALF
        column = two(step * jnp.exp(jnp.where(first, mid, end) - cum))
        row = two(jnp.exp(cum - jnp.where(first, 0.0, mid)))
        four = jnp.concatenate([column[0], column[1], row[0], row[1]], 0)
        factors[at, :] = four.T.astype(BF16)
        scaled = cum * LOG2E
        cum_h[:, at] = scaled - jnp.log2(step)
        packed[0:padded, :] = scaled
        packed[padded : padded + levels, :] = weight_h[:, at]
        columns[at, :] = packed[...].T
    token = iota((rows.shape[0], tokens), 1)
    begin, finish = layout.ranges(tokens)
    chosen = as_bf16((token >= begin) & (token < finish))
    high, middle, low = three(decay[...])
    sums = (dot(chosen, low, NT) + dot(chosen, middle, NT)) + dot(chosen, high, NT)
    high, low = two(jnp.exp(sums))
    per_head = width // heads
    head = iota((padded, width), 0) * per_head
    lane = iota((padded, width), 1)
    own = as_bf16((head <= lane) & (lane < head + per_head))
    rows[...] = dot(high.astype(BF16), own) + dot(low.astype(BF16), own)
    gains = jnp.broadcast_to(gain[...], (8, heads))
    high, middle, low = three(gains)
    own = own[:heads]
    rows[layout.skip : layout.skip + 8, :] = (dot(low, own) + dot(middle, own)) + dot(high, own)


def scale_kernel(heads, padded, layout, mixer, factors, rows, scaled, to_total):
    tokens, width = mixer.shape
    wide = spread(0, padded, heads, width)

    def step(a, carry):
        at = pl.ds(pl.multiple_of(a * HALF, HALF), HALF)
        row = rows[pl.ds(layout.after + a, 1), :]
        value = mixer[at, :].astype(F32) * dot(factors[at, :], wide)
        scaled[at, :] = value.astype(BF16)
        to_total[at, :] = (value * row).astype(BF16)
        return carry

    lax.fori_loop(0, tokens // HALF, step, 0, unroll=4)


def exp_rows(total, count):
    where = iota((count, total.shape[1]), 0)
    high = total.astype(BF16).astype(F32)
    return jnp.where(where == 0, high, jnp.where(where == 1, total - high, 0.0)).astype(BF16)


def own_columns(width):
    rank = lax.axis_index("seq")
    mine = (rank & 1) * (width // 2)
    other = width // 2 - mine
    aligned = lambda at: pl.ds(pl.multiple_of(at, LANES), width // 2)
    return aligned(mine), aligned(other)


def state_kernel(layout, to_total, write_t, rows, first, second, mine, mine_exp, whole):
    state = write_t.shape[0]
    own, other = own_columns(whole.shape[1])
    whole[...] = dot(write_t[...], to_total[...])
    for payload, at in ((first, other), (second, own)):
        payload[0:state, :] = whole[:, at].astype(BF16)
        total = rows[layout.total : layout.total + 1, at]
        payload[state:, :] = exp_rows(total, payload.shape[0] - state)
    mine[...] = whole[:, own]
    mine_exp[...] = jnp.broadcast_to(rows[layout.total : layout.total + 1, own], mine_exp.shape)


def upper_half(bit, width):
    rank = lax.axis_index("seq")
    return ((jnp.zeros((1, width), jnp.int32) + rank) >> bit) & 1 > 0


def merge_kernel(bit, received, mine, mine_exp, after, payload, *more):
    state, width = mine.shape
    extra = received[state:, :].astype(F32)
    other_exp = extra[0:1] + extra[1:2]
    own_exp = mine_exp[0:1, :]
    upper = upper_half(bit, width)
    own_scale = jnp.where(upper, 1.0, other_exp)
    other_scale = jnp.where(upper, own_exp, 1.0)
    new = own_scale * mine[...] + other_scale * received[0:state, :].astype(F32)
    payload[0:state, :] = new.astype(BF16)
    total = own_exp * other_exp
    payload[state:, :] = exp_rows(total, payload.shape[0] - state)
    if more:
        merged, merged_exp = more
        merged[...] = new
        merged_exp[...] = jnp.broadcast_to(total, merged_exp.shape)


def join_kernel(first, second, *rest):
    joined = rest[-1]
    joined[: first.shape[0], :] = first[...]
    joined[first.shape[0] :, :] = second[...]


def local_kernel(
    heads, padded, bits, first, count, layout, tile,
    mixer, scaled, write_t, read_t, factors, columns, cum_h, weight_h, rows, slots_in, after,
    base, reach, slots, scores, narrow, off_scores, queries,
):
    width = mixer.shape[1]
    state = write_t.shape[0]
    per_head = width // heads
    heads_here = LANES // per_head
    wide = spread(2 * padded, padded, heads, width)
    causal = iota((HALF, HALF), 0) >= iota((HALF, HALF), 1)
    lane = iota((HALF, LANES), 1)
    own = [as_bf16((lane >= k * per_head) & (lane < (k + 1) * per_head)) for k in range(heads_here)]
    live = [bit for bit in range(bits) if (first >> bit) & 1]
    for bit in live:
        slots[bit] = slots_in[bit]
        narrow[bit * state : (bit + 1) * state, :] = slots_in[bit].astype(BF16)

    def head_part(c):
        at = slice(c * BLOCK, (c + 1) * BLOCK)
        live = [bit for bit in range(bits) if (c >> bit) & 1]
        if live:
            queries[0 : len(live) * state, :] = read_levels(read_t, weight_h, at, [bit + 1 for bit in live])
        weighted = dot(read_t[:, at], write_t[:, at], TN) * columns[at, padded : padded + 1]
        off_scores[...] = weighted[HALF:, :HALF].astype(BF16)
        scores[0] = jnp.where(causal, weighted[:HALF, :HALF], 0.0)
        scores[1] = jnp.where(causal, weighted[HALF:, HALF:], 0.0)

    def half_part(c, half):
        live = [bit for bit in range(bits) if (c >> bit) & 1]
        low = c * BLOCK + half * HALF
        half_at = slice(low, low + HALF)
        put_at = slice(low - first * BLOCK, low - first * BLOCK + HALF)
        for left in range(0, width, tile):
            lanes = slice(left, left + tile)
            near = dot(factors[half_at, :], wide[:, lanes])
            reach[put_at, lanes] = near * rows[layout.run + 2 * c + half : layout.run + 2 * c + half + 1, lanes]
            rest = None
            if half == 1:
                rest = dot(off_scores[...], scaled[c * BLOCK : c * BLOCK + HALF, lanes])
            if live:
                stored = [narrow[bit * state : (bit + 1) * state, lanes] for bit in live]
                stored = jnp.concatenate(stored, 0) if len(stored) > 1 else stored[0]
                level = dot(
                    queries[0 : len(live) * state, half * HALF : (half + 1) * HALF], stored, TN
                )
                middle = rows[layout.middle + c : layout.middle + c + 1, lanes]
                rest = level if rest is None else rest + middle * level
            skipped = rows[layout.skip : layout.skip + 1, lanes] * mixer[half_at, lanes].astype(F32)
            rest = skipped if rest is None else skipped + near * rest
            for inner in range(0, tile, LANES):
                here = slice(left + inner, left + inner + LANES)
                head = (left + inner) // per_head
                value = mixer[half_at, here]
                left_side = []
                for k in range(heads_here):
                    gap = columns[half_at, head + k : head + k + 1] - cum_h[head + k : head + k + 1, half_at]
                    mixing = scores[half] * jnp.exp2(jnp.minimum(gap, 0.0))
                    left_side.append(mixing.astype(BF16))
                part = dot(
                    jnp.concatenate(left_side, 1),
                    jnp.concatenate([value * mask for mask in own], 0),
                )
                base[put_at, here] = part + rest[:, inner : inner + LANES]

    def update_part(c):
        live = [bit for bit in range(bits) if (c >> bit) & 1]
        ones = 0
        while ones < bits and (c >> ones) & 1:
            ones += 1
        low = c * BLOCK
        if ones == bits:
            return
        for left in range(0, width, tile):
            lanes = slice(left, left + tile)
            shrink = rows[layout.decay + c : layout.decay + c + 1, lanes]
            upper = rows[layout.upper + c : layout.upper + c + 1, lanes]
            fresh = upper * dot(
                write_t[:, low : low + HALF], scaled[low : low + HALF, lanes]
            ) + dot(write_t[:, low + HALF : low + BLOCK], scaled[low + HALF : low + BLOCK, lanes])
            for bit in range(ones):
                fresh = fresh + shrink * slots[bit, :, lanes]
            slots[ones, :, lanes] = fresh
            narrow[ones * state : (ones + 1) * state, lanes] = fresh.astype(BF16)
            for bit in live:
                if bit > ones:
                    kept = shrink * slots[bit, :, lanes]
                    slots[bit, :, lanes] = kept
                    narrow[bit * state : (bit + 1) * state, lanes] = kept.astype(BF16)

    def first_region(c):
        head_part(c)
        half_part(c, 0)

    def second_region(c):
        half_part(c, 1)
        update_part(c)

    when_here = pl.when(lax.axis_index("seq") >= 0)
    for c in range(first, first + count):
        when_here(functools.partial(first_region, c))
        when_here(functools.partial(second_region, c))


def bucket_rows(received, bits, state, width):
    running = jnp.ones((1, width), F32)
    out = []
    for bit in range(bits):
        upper = upper_half(bit, width)
        scale = jnp.where(upper, running, 0.0)
        out.append((received[bit][0:state, :].astype(F32) * scale).astype(BF16))
        if bit + 1 < bits:
            extra = received[bit][state:, :].astype(F32)
            running = jnp.where(upper, running * (extra[0:1] + extra[1:2]), running)
    return jnp.concatenate(out, 0)


def read_levels(read_t, weight_h, at, levels):
    read_f = read_t[:, at].astype(F32)
    queries = [(read_f * weight_h[level : level + 1, at]).astype(BF16) for level in levels]
    return jnp.concatenate(queries, 0) if len(queries) > 1 else queries[0]


def final_kernel(starts, local_bits, bits, side, read_t, weight_h, *rest):
    pieces = len(starts) - 1
    received, rest = rest[:bits], rest[bits:]
    bases, reaches, rest = rest[:pieces], rest[pieces : 2 * pieces], rest[2 * pieces :]
    out, buckets, ready, sems = rest[-4:]
    columns = own_columns(out.shape[1])[side]
    buckets[...] = bucket_rows(received, bits, read_t.shape[0], buckets.shape[1])

    levels = [local_bits + 1 + bit for bit in range(bits)]

    def copy(c, at):
        return pltpu.make_async_copy(ready.at[c], out.at[pl.ds(at, BLOCK), columns], sems.at[c])

    for piece in range(pieces):

        def block(g, carry, piece=piece):
            c = starts[piece] + g
            at = pl.multiple_of(c * BLOCK, BLOCK)
            here = pl.ds(pl.multiple_of(g * BLOCK, BLOCK), BLOCK)
            query = read_levels(read_t, weight_h, pl.ds(at, BLOCK), levels)
            part = dot(query, buckets[...], TN)
            ready[c] = (bases[piece][here, columns] + part * reaches[piece][here, columns]).astype(BF16)
            copy(c, at).start()
            return carry

        lax.fori_loop(0, starts[piece + 1] - starts[piece], block, 0, unroll=True)
    for c in range(starts[-1]):
        copy(c, c * BLOCK).wait()


def gather_columns(mine, axis, after):
    pieces = mine
    size = lax.axis_size(axis)
    stride = size // 2
    while stride:
        other = lax.ppermute(pieces, axis, [(i, i ^ stride) for i in range(size)])
        pieces = pl.pallas_call(
            join_kernel,
            in_specs=[VMEM_SPEC] * 2 + [ANY_SPEC],
            out_specs=VMEM_SPEC,
            out_shape=jax.ShapeDtypeStruct((2 * pieces.shape[0], pieces.shape[1]), BF16),
            compiler_params=grant(2),
            cost_estimate=cost(0, 4 * pieces.size),
            name="join",
        )(pieces, other, after)
        stride //= 2
    return pieces


def cost(flops, bytes_accessed):
    return pl.CostEstimate(flops=flops, bytes_accessed=bytes_accessed, transcendentals=0)


def grant(mebibytes):
    return pltpu.CompilerParams(vmem_limit_bytes=mebibytes << 20)


def on_device(
    mixer_input, write_map, read_map, step_size, log_decay, skip_gain, level_table, level_index
):
    tokens, width = mixer_input.shape
    heads = log_decay.shape[0]
    blocks = tokens // BLOCK
    local_bits = blocks.bit_length() - 1
    ranks = lax.axis_size("seq")
    device_bits = ranks.bit_length() - 1
    levels = level_table.shape[0]
    padded = LANES // 4
    tile = 256
    layout = Rows(blocks)
    sds = jax.ShapeDtypeStruct

    factors, columns, cum_h, weight_h, rows = pl.pallas_call(
        functools.partial(prep_kernel, heads, padded, layout),
        in_specs=[HBM_SPEC] * 5,
        out_specs=(VMEM_SPEC,) * 5,
        out_shape=(
            sds((tokens, LANES), BF16), sds((tokens, LANES), F32), sds((padded, tokens), F32),
            sds((levels, tokens), F32), sds((layout.count, width), F32),
        ),
        scratch_shapes=[
            pltpu.VMEM((heads, tokens), F32),
            pltpu.VMEM((heads, tokens), F32),
            pltpu.VMEM(level_index.shape, jnp.int32),
            pltpu.VMEM(level_table.shape, F32),
            pltpu.VMEM((1, heads), F32),
            pltpu.VMEM((padded, tokens), F32),
            pltpu.VMEM((padded, tokens), F32),
            pltpu.VMEM((LANES, BLOCK), F32),
            pltpu.SemaphoreType.DMA((5,)),
        ],
        compiler_params=grant(6),
        cost_estimate=cost(2_000_000_000, 4_000_000),
        name="prep",
    )(
        *(
            pltpu.with_memory_space_constraint(value, pltpu.HBM)
            for value in (log_decay, step_size, level_index, level_table, skip_gain[None, :])
        )
    )

    write_t = gather_columns(write_map.T, "head", rows)
    read_t = gather_columns(read_map.T, "head", rows)
    state = write_t.shape[0]

    scaled, to_total = pl.pallas_call(
        functools.partial(scale_kernel, heads, padded, layout),
        in_specs=[VMEM_SPEC] * 3,
        out_specs=(VMEM_SPEC,) * 2,
        out_shape=(sds((tokens, width), BF16),) * 2,
        compiler_params=grant(4),
        cost_estimate=cost(3_000_000_000, tokens * width * 6),
        name="scale",
    )(mixer_input, factors, rows)

    half = width // 2
    carried = (sds((state + 8, half), BF16), sds((state, half), F32), sds((8, half), F32))
    first_out, second_out, mine, mine_exp = pl.pallas_call(
        functools.partial(state_kernel, layout),
        in_specs=[VMEM_SPEC] * 3,
        out_specs=(VMEM_SPEC,) * 4,
        out_shape=carried[:1] + carried,
        scratch_shapes=[pltpu.VMEM((state, width), F32)],
        compiler_params=grant(4),
        cost_estimate=cost(2 * tokens * width * state, tokens * width * 2),
        name="state",
    )(to_total, write_t, rows)

    def local(first, count, slots, after):
        return pl.pallas_call(
            functools.partial(
                local_kernel, heads, padded, local_bits, first, count, layout, tile
            ),
            in_specs=[VMEM_SPEC] * 10 + [ANY_SPEC],
            out_specs=(VMEM_SPEC,) * 3,
            out_shape=(
                sds((count * BLOCK, width), F32), sds((count * BLOCK, width), F32),
                sds((local_bits, state, width), F32),
            ),
            scratch_shapes=[
                pltpu.VMEM((2, HALF, HALF), F32),
                pltpu.VMEM((local_bits * state, width), BF16),
                pltpu.VMEM((HALF, HALF), BF16),
                pltpu.VMEM((local_bits * state, BLOCK), BF16),
            ],
            compiler_params=grant(8),
            cost_estimate=cost(count * BLOCK * width * 2 * 2000, count * BLOCK * width * 8),
            name="local",
        )(
            mixer_input, scaled, write_t, read_t, factors, columns, cum_h, weight_h, rows,
            slots, after,
        )

    def swap(value, bit):
        return lax.ppermute(value, "seq", [(i, i ^ 1 << bit) for i in range(ranks)])

    shares = [3] * (device_bits - 1) + [2]
    starts = [0]
    for share in shares:
        starts.append(starts[-1] + max(1, blocks * share // sum(shares)))
    starts = [min(start, blocks) for start in starts[:-1]] + [blocks]

    slots = jnp.zeros((local_bits, 8, LANES), F32)
    bases, reaches = [], []
    own_parts = [swap(first_out, 0)]
    other_parts = [swap(second_out, 0)]
    after = rows
    payload = None
    for bit in range(device_bits):
        if starts[bit + 1] > starts[bit]:
            base, reach, slots = local(starts[bit], starts[bit + 1] - starts[bit], slots, after)
            bases.append(base)
            reaches.append(reach)
        if bit + 1 < device_bits:
            last = bit + 2 == device_bits
            shapes = carried[:1] if last else carried
            payload, *more = pl.pallas_call(
                functools.partial(merge_kernel, bit),
                in_specs=[VMEM_SPEC] * 3 + [ANY_SPEC],
                out_specs=(VMEM_SPEC,) * len(shapes),
                out_shape=shapes,
                compiler_params=grant(4),
                cost_estimate=cost(2 * state * width, state * width * 6),
                name="merge",
            )(own_parts[bit], mine, mine_exp, slots)
            if more:
                mine, mine_exp = more
            after = payload
            own_parts.append(swap(payload, bit + 1))
            if bit > 0:
                other_parts.append(swap(own_parts[bit], 0))
    starts = sorted(set(starts))

    if device_bits > 1:
        other_parts.append(swap(own_parts[-1], 0))

    out = None
    for side, parts in enumerate((own_parts, other_parts)):
        operands = [read_t, weight_h, *parts, *bases, *reaches]
        specs = [VMEM_SPEC] * len(operands)
        aliases = {}
        if out is not None:
            aliases = {len(operands): 0}
            operands.append(out)
            specs.append(ANY_SPEC)
        out = pl.pallas_call(
            functools.partial(final_kernel, starts, local_bits, device_bits, side),
            in_specs=specs,
            out_specs=ANY_SPEC,
            out_shape=sds((tokens, width), BF16),
            input_output_aliases=aliases,
            scratch_shapes=[
                pltpu.VMEM((device_bits * state, half), BF16),
                pltpu.VMEM((blocks, BLOCK, half), BF16),
                pltpu.SemaphoreType.DMA((blocks,)),
            ],
            compiler_params=grant(6),
            cost_estimate=cost(tokens * width * state, tokens * width * 3),
            name="final",
        )(*operands)
    return out


def solution(mesh):
    placed = (
        P("seq", "head"),
        P("seq", "head"),
        P("seq", "head"),
        P("head", "seq"),
        P("head", "seq"),
        P("head"),
        P(),
        P(None, "seq"),
    )

    return jax.shard_map(
        on_device, mesh=mesh, in_specs=placed, out_specs=P("seq", "head"), check_vma=False
    )
```

```python
import functools

import jax
import jax.numpy as jnp
from jax import lax
from jax.experimental import pallas as pl
from jax.experimental.pallas import tpu as pltpu
from jax.sharding import PartitionSpec as P


BLOCK = 256
HALF = BLOCK // 2
LANES = 128
LOG2E = 1.4426950408889634
F32 = jnp.float32
BF16 = jnp.bfloat16
NT = (((1,), (1,)), ((), ()))
NN = (((1,), (0,)), ((), ()))
TN = (((0,), (0,)), ((), ()))
VMEM_SPEC = pl.BlockSpec(memory_space=pltpu.VMEM)
SMEM_SPEC = pl.BlockSpec(memory_space=pltpu.SMEM)
ANY_SPEC = pl.BlockSpec(memory_space=pl.ANY)
HBM_SPEC = pl.BlockSpec(memory_space=pltpu.HBM)


def dot(a, b, dims=NN):
    return lax.dot_general(a, b, dims, preferred_element_type=F32)


def three(a):
    high = a.astype(BF16)
    rest = a - high.astype(F32)
    middle = rest.astype(BF16)
    return high, middle, (rest - middle.astype(F32)).astype(BF16)


def two(a):
    high = a.astype(BF16).astype(F32)
    return high, a - high


def iota(shape, dim):
    return lax.broadcasted_iota(jnp.int32, shape, dim)


def as_bf16(mask):
    return mask.astype(F32).astype(BF16)


def spread(first_row, padded, heads, width):
    per_head = width // heads
    row = iota((4 * padded, width), 0) - first_row
    lane = iota((4 * padded, width), 1)
    inside = (row >= 0) & (row < 2 * padded)
    row = jnp.where(row >= padded, row - padded, row)
    own = (row * per_head <= lane) & (lane < (row + 1) * per_head) & (row < heads)
    return as_bf16(own & inside)


class Rows:
    def __init__(self, blocks):
        halves = 2 * blocks
        self.after, self.run = 0, halves
        self.middle, self.upper, self.decay = 2 * halves, 2 * halves + blocks, 2 * halves + 2 * blocks
        self.total = 2 * halves + 3 * blocks
        self.skip = self.total + 8 - self.total % 8
        self.count = -(-(self.skip + 8) // 16) * 16

    def ranges(self, tokens):
        halves = tokens // HALF
        blocks = halves // 2
        k = iota((self.count, 1), 0)
        low = (k + 1) * HALF
        high = jnp.full_like(k, tokens)
        low = jnp.where(k >= self.run, 0, low)
        high = jnp.where(k >= self.run, (k - self.run) * HALF, high)
        for first, start, size in (
            (self.middle, 0, HALF), (self.upper, HALF, HALF), (self.decay, 0, BLOCK)
        ):
            here = (k - first) * BLOCK + start
            low = jnp.where(k >= first, here, low)
            high = jnp.where(k >= first, here + size, high)
        low = jnp.where(k >= self.total, 0, low)
        high = jnp.where(k == self.total, tokens, jnp.where(k > self.total, 0, high))
        return low, high


def prep_kernel(
    heads, padded, layout, log_decay_far, step_size_far, level_index_far, level_table_far, gain_far,
    factors, columns, cum_h, weight_h, rows,
    log_decay, step_size, level_index, level_table, gain, decay, steps, packed, sems,
):
    pairs = (
        (log_decay_far, log_decay), (step_size_far, step_size), (level_index_far, level_index),
        (level_table_far, level_table), (gain_far, gain),
    )
    copies = [pltpu.make_async_copy(far, near, sems.at[n]) for n, (far, near) in enumerate(pairs)]
    for copy in copies:
        copy.start()
    tokens = log_decay.shape[1]
    width = rows.shape[1]
    blocks = tokens // BLOCK
    decay[...] = jnp.zeros_like(decay)
    steps[...] = jnp.zeros_like(steps)
    for copy in copies:
        copy.wait()
    decay[0:heads, :] = log_decay[...]
    steps[0:heads, :] = step_size[...]
    lower = as_bf16(iota((BLOCK, BLOCK), 0) >= iota((BLOCK, BLOCK), 1))
    levels = level_index.shape[0]
    weight = jnp.zeros(level_index.shape, F32)
    index = level_index[...]
    for entry in range(level_table.shape[1]):
        weight = weight + jnp.where(index == entry, level_table[:, entry : entry + 1], 0.0)
    weight_h[...] = weight
    packed[...] = jnp.zeros_like(packed)
    for c in range(blocks):
        at = slice(c * BLOCK, (c + 1) * BLOCK)
        high, middle, low = three(decay[:, at])
        cum = (dot(low, lower, NT) + dot(middle, lower, NT)) + dot(high, lower, NT)
        step = steps[:, at]
        mid = cum[:, HALF - 1 : HALF]
        end = cum[:, BLOCK - 1 : BLOCK]
        first = iota((padded, BLOCK), 1) < HALF
        column = two(step * jnp.exp(jnp.where(first, mid, end) - cum))
        row = two(jnp.exp(cum - jnp.where(first, 0.0, mid)))
        four = jnp.concatenate([column[0], column[1], row[0], row[1]], 0)
        factors[at, :] = four.T.astype(BF16)
        scaled = cum * LOG2E
        cum_h[:, at] = scaled - jnp.log2(step)
        packed[0:padded, :] = scaled
        packed[padded : padded + levels, :] = weight_h[:, at]
        columns[at, :] = packed[...].T
    token = iota((rows.shape[0], tokens), 1)
    begin, finish = layout.ranges(tokens)
    chosen = as_bf16((token >= begin) & (token < finish))
    high, middle, low = three(decay[...])
    sums = (dot(chosen, low, NT) + dot(chosen, middle, NT)) + dot(chosen, high, NT)
    high, low = two(jnp.exp(sums))
    per_head = width // heads
    head = iota((padded, width), 0) * per_head
    lane = iota((padded, width), 1)
    own = as_bf16((head <= lane) & (lane < head + per_head))
    rows[...] = dot(high.astype(BF16), own) + dot(low.astype(BF16), own)
    gains = jnp.broadcast_to(gain[...], (8, heads))
    high, middle, low = three(gains)
    own = own[:heads]
    rows[layout.skip : layout.skip + 8, :] = (dot(low, own) + dot(middle, own)) + dot(high, own)


def scale_kernel(heads, padded, layout, mixer, factors, rows, scaled, to_total):
    tokens, width = mixer.shape
    wide = spread(0, padded, heads, width)

    def step(a, carry):
        at = pl.ds(pl.multiple_of(a * HALF, HALF), HALF)
        row = rows[pl.ds(layout.after + a, 1), :]
        value = mixer[at, :].astype(F32) * dot(factors[at, :], wide)
        scaled[at, :] = value.astype(BF16)
        to_total[at, :] = (value * row).astype(BF16)
        return carry

    lax.fori_loop(0, tokens // HALF, step, 0, unroll=4)


def exp_rows(total, count):
    where = iota((count, total.shape[1]), 0)
    high = total.astype(BF16).astype(F32)
    return jnp.where(where == 0, high, jnp.where(where == 1, total - high, 0.0)).astype(BF16)


def own_columns(width):
    rank = lax.axis_index("seq")
    mine = (rank & 1) * (width // 2)
    other = width // 2 - mine
    aligned = lambda at: pl.ds(pl.multiple_of(at, LANES), width // 2)
    return aligned(mine), aligned(other)


def state_kernel(layout, to_total, write_t, rows, first, second, mine, mine_exp, whole):
    state = write_t.shape[0]
    own, other = own_columns(whole.shape[1])
    whole[...] = dot(write_t[...], to_total[...])
    for payload, at in ((first, other), (second, own)):
        payload[0:state, :] = whole[:, at].astype(BF16)
        total = rows[layout.total : layout.total + 1, at]
        payload[state:, :] = exp_rows(total, payload.shape[0] - state)
    mine[...] = whole[:, own]
    mine_exp[...] = jnp.broadcast_to(rows[layout.total : layout.total + 1, own], mine_exp.shape)


def upper_half(bit, width):
    rank = lax.axis_index("seq")
    return ((jnp.zeros((1, width), jnp.int32) + rank) >> bit) & 1 > 0


def merge_kernel(bit, received, mine, mine_exp, after, payload, *more):
    state, width = mine.shape
    extra = received[state:, :].astype(F32)
    other_exp = extra[0:1] + extra[1:2]
    own_exp = mine_exp[0:1, :]
    upper = upper_half(bit, width)
    own_scale = jnp.where(upper, 1.0, other_exp)
    other_scale = jnp.where(upper, own_exp, 1.0)
    new = own_scale * mine[...] + other_scale * received[0:state, :].astype(F32)
    payload[0:state, :] = new.astype(BF16)
    total = own_exp * other_exp
    payload[state:, :] = exp_rows(total, payload.shape[0] - state)
    if more:
        merged, merged_exp = more
        merged[...] = new
        merged_exp[...] = jnp.broadcast_to(total, merged_exp.shape)


def join_kernel(first, second, *rest):
    joined = rest[-1]
    joined[: first.shape[0], :] = first[...]
    joined[first.shape[0] :, :] = second[...]


def local_kernel(
    heads, padded, bits, first, count, layout, tile,
    mixer, scaled, write_t, read_t, factors, columns, cum_h, weight_h, rows, slots_in, after,
    base, reach, slots, scores, narrow, off_scores, queries,
):
    width = mixer.shape[1]
    state = write_t.shape[0]
    per_head = width // heads
    heads_here = LANES // per_head
    wide = spread(2 * padded, padded, heads, width)
    causal = iota((HALF, HALF), 0) >= iota((HALF, HALF), 1)
    lane = iota((HALF, LANES), 1)
    own = [as_bf16((lane >= k * per_head) & (lane < (k + 1) * per_head)) for k in range(heads_here)]
    live = [bit for bit in range(bits) if (first >> bit) & 1]
    for bit in live:
        slots[bit] = slots_in[bit]
        narrow[bit * state : (bit + 1) * state, :] = slots_in[bit].astype(BF16)

    def head_part(c):
        at = slice(c * BLOCK, (c + 1) * BLOCK)
        live = [bit for bit in range(bits) if (c >> bit) & 1]
        if live:
            queries[0 : len(live) * state, :] = read_levels(read_t, weight_h, at, [bit + 1 for bit in live])
        weighted = dot(read_t[:, at], write_t[:, at], TN) * columns[at, padded : padded + 1]
        off_scores[...] = weighted[HALF:, :HALF].astype(BF16)
        scores[0] = jnp.where(causal, weighted[:HALF, :HALF], 0.0)
        scores[1] = jnp.where(causal, weighted[HALF:, HALF:], 0.0)

    def half_part(c, half):
        live = [bit for bit in range(bits) if (c >> bit) & 1]
        low = c * BLOCK + half * HALF
        half_at = slice(low, low + HALF)
        put_at = slice(low - first * BLOCK, low - first * BLOCK + HALF)
        for left in range(0, width, tile):
            lanes = slice(left, left + tile)
            near = dot(factors[half_at, :], wide[:, lanes])
            reach[put_at, lanes] = near * rows[layout.run + 2 * c + half : layout.run + 2 * c + half + 1, lanes]
            rest = None
            if half == 1:
                rest = dot(off_scores[...], scaled[c * BLOCK : c * BLOCK + HALF, lanes])
            if live:
                stored = [narrow[bit * state : (bit + 1) * state, lanes] for bit in live]
                stored = jnp.concatenate(stored, 0) if len(stored) > 1 else stored[0]
                level = dot(
                    queries[0 : len(live) * state, half * HALF : (half + 1) * HALF], stored, TN
                )
                middle = rows[layout.middle + c : layout.middle + c + 1, lanes]
                rest = level if rest is None else rest + middle * level
            skipped = rows[layout.skip : layout.skip + 1, lanes] * mixer[half_at, lanes].astype(F32)
            rest = skipped if rest is None else skipped + near * rest
            for inner in range(0, tile, LANES):
                here = slice(left + inner, left + inner + LANES)
                head = (left + inner) // per_head
                value = mixer[half_at, here]
                left_side = []
                for k in range(heads_here):
                    gap = columns[half_at, head + k : head + k + 1] - cum_h[head + k : head + k + 1, half_at]
                    mixing = scores[half] * jnp.exp2(jnp.minimum(gap, 0.0))
                    left_side.append(mixing.astype(BF16))
                part = dot(
                    jnp.concatenate(left_side, 1),
                    jnp.concatenate([value * mask for mask in own], 0),
                )
                base[put_at, here] = part + rest[:, inner : inner + LANES]

    def update_part(c):
        live = [bit for bit in range(bits) if (c >> bit) & 1]
        ones = 0
        while ones < bits and (c >> ones) & 1:
            ones += 1
        low = c * BLOCK
        if ones == bits:
            return
        for left in range(0, width, tile):
            lanes = slice(left, left + tile)
            shrink = rows[layout.decay + c : layout.decay + c + 1, lanes]
            upper = rows[layout.upper + c : layout.upper + c + 1, lanes]
            fresh = upper * dot(
                write_t[:, low : low + HALF], scaled[low : low + HALF, lanes]
            ) + dot(write_t[:, low + HALF : low + BLOCK], scaled[low + HALF : low + BLOCK, lanes])
            for bit in range(ones):
                fresh = fresh + shrink * slots[bit, :, lanes]
            slots[ones, :, lanes] = fresh
            narrow[ones * state : (ones + 1) * state, lanes] = fresh.astype(BF16)
            for bit in live:
                if bit > ones:
                    kept = shrink * slots[bit, :, lanes]
                    slots[bit, :, lanes] = kept
                    narrow[bit * state : (bit + 1) * state, lanes] = kept.astype(BF16)

    def first_region(c):
        head_part(c)
        half_part(c, 0)

    def second_region(c):
        half_part(c, 1)
        update_part(c)

    when_here = pl.when(lax.axis_index("seq") >= 0)
    for c in range(first, first + count):
        when_here(functools.partial(first_region, c))
        when_here(functools.partial(second_region, c))


def bucket_rows(received, bits, state, width, wanted):
    running = jnp.ones((1, width), F32)
    out = []
    for bit in range(bits):
        upper = upper_half(bit, width)
        if bit in wanted:
            scale = jnp.where(upper, running, 0.0)
            out.append((received[bit][0:state, :].astype(F32) * scale).astype(BF16))
        if bit + 1 < bits:
            extra = received[bit][state:, :].astype(F32)
            running = jnp.where(upper, running * (extra[0:1] + extra[1:2]), running)
    return jnp.concatenate(out, 0) if len(out) > 1 else out[0]


def read_levels(read_t, weight_h, at, levels):
    read_f = read_t[:, at].astype(F32)
    queries = [(read_f * weight_h[level : level + 1, at]).astype(BF16) for level in levels]
    return jnp.concatenate(queries, 0) if len(queries) > 1 else queries[0]


def near_kernel(starts, local_bits, bits, read_t, weight_h, *rest):
    pieces = len(starts) - 1
    received, rest = rest[:bits], rest[bits:]
    bases, reaches, rest = rest[:pieces], rest[pieces : 2 * pieces], rest[2 * pieces :]
    out, buckets = rest
    columns = own_columns(bases[0].shape[1])[1]
    buckets[...] = bucket_rows(received, bits, read_t.shape[0], buckets.shape[1], range(bits))
    levels = [local_bits + 1 + bit for bit in range(bits)]
    for piece in range(pieces):

        def block(g, carry, piece=piece):
            at = pl.ds(pl.multiple_of((starts[piece] + g) * BLOCK, BLOCK), BLOCK)
            here = pl.ds(pl.multiple_of(g * BLOCK, BLOCK), BLOCK)
            part = dot(read_levels(read_t, weight_h, at, levels), buckets[...], TN)
            out[at, :] = bases[piece][here, columns] + part * reaches[piece][here, columns]
            return carry

        lax.fori_loop(0, starts[piece + 1] - starts[piece], block, 0, unroll=True)


def final_kernel(starts, local_bits, bits, wanted, side, read_t, weight_h, *rest):
    pieces = len(starts) - 1
    received, rest = rest[:bits], rest[bits:]
    near = None
    if side:
        near, rest = rest[0], rest[1:]
        reaches = rest[:pieces]
    else:
        bases, reaches = rest[:pieces], rest[pieces : 2 * pieces]
    out, buckets, ready, sems = rest[-4:]
    columns = own_columns(out.shape[1])[side]
    buckets[...] = bucket_rows(received, bits, read_t.shape[0], buckets.shape[1], wanted)
    levels = [local_bits + 1 + bit for bit in wanted]

    def copy(c, at):
        return pltpu.make_async_copy(ready.at[c], out.at[pl.ds(at, BLOCK), columns], sems.at[c])

    for piece in range(pieces):

        def block(g, carry, piece=piece):
            c = starts[piece] + g
            at = pl.multiple_of(c * BLOCK, BLOCK)
            here = pl.ds(pl.multiple_of(g * BLOCK, BLOCK), BLOCK)
            query = read_levels(read_t, weight_h, pl.ds(at, BLOCK), levels)
            part = dot(query, buckets[...], TN)
            if side:
                base = near[pl.ds(at, BLOCK), :]
            else:
                base = bases[piece][here, columns]
            ready[c] = (base + part * reaches[piece][here, columns]).astype(BF16)
            copy(c, at).start()
            return carry

        lax.fori_loop(0, starts[piece + 1] - starts[piece], block, 0, unroll=True)
    for c in range(starts[-1]):
        copy(c, c * BLOCK).wait()


def gather_columns(mine, axis, after):
    pieces = mine
    size = lax.axis_size(axis)
    stride = size // 2
    while stride:
        other = lax.ppermute(pieces, axis, [(i, i ^ stride) for i in range(size)])
        pieces = pl.pallas_call(
            join_kernel,
            in_specs=[VMEM_SPEC] * 2 + [ANY_SPEC],
            out_specs=VMEM_SPEC,
            out_shape=jax.ShapeDtypeStruct((2 * pieces.shape[0], pieces.shape[1]), BF16),
            compiler_params=grant(2),
            cost_estimate=cost(0, 4 * pieces.size),
            name="join",
        )(pieces, other, after)
        stride //= 2
    return pieces


def cost(flops, bytes_accessed):
    return pl.CostEstimate(flops=flops, bytes_accessed=bytes_accessed, transcendentals=0)


def grant(mebibytes):
    return pltpu.CompilerParams(vmem_limit_bytes=mebibytes << 20)


def on_device(
    mixer_input, write_map, read_map, step_size, log_decay, skip_gain, level_table, level_index
):
    tokens, width = mixer_input.shape
    heads = log_decay.shape[0]
    blocks = tokens // BLOCK
    local_bits = blocks.bit_length() - 1
    ranks = lax.axis_size("seq")
    device_bits = ranks.bit_length() - 1
    levels = level_table.shape[0]
    padded = LANES // 4
    tile = 256
    layout = Rows(blocks)
    sds = jax.ShapeDtypeStruct

    factors, columns, cum_h, weight_h, rows = pl.pallas_call(
        functools.partial(prep_kernel, heads, padded, layout),
        in_specs=[HBM_SPEC] * 5,
        out_specs=(VMEM_SPEC,) * 5,
        out_shape=(
            sds((tokens, LANES), BF16), sds((tokens, LANES), F32), sds((padded, tokens), F32),
            sds((levels, tokens), F32), sds((layout.count, width), F32),
        ),
        scratch_shapes=[
            pltpu.VMEM((heads, tokens), F32),
            pltpu.VMEM((heads, tokens), F32),
            pltpu.VMEM(level_index.shape, jnp.int32),
            pltpu.VMEM(level_table.shape, F32),
            pltpu.VMEM((1, heads), F32),
            pltpu.VMEM((padded, tokens), F32),
            pltpu.VMEM((padded, tokens), F32),
            pltpu.VMEM((LANES, BLOCK), F32),
            pltpu.SemaphoreType.DMA((5,)),
        ],
        compiler_params=grant(6),
        cost_estimate=cost(2_000_000_000, 4_000_000),
        name="prep",
    )(
        *(
            pltpu.with_memory_space_constraint(value, pltpu.HBM)
            for value in (log_decay, step_size, level_index, level_table, skip_gain[None, :])
        )
    )

    write_t = gather_columns(write_map.T, "head", rows)
    read_t = gather_columns(read_map.T, "head", rows)
    state = write_t.shape[0]

    scaled, to_total = pl.pallas_call(
        functools.partial(scale_kernel, heads, padded, layout),
        in_specs=[VMEM_SPEC] * 3,
        out_specs=(VMEM_SPEC,) * 2,
        out_shape=(sds((tokens, width), BF16),) * 2,
        compiler_params=grant(4),
        cost_estimate=cost(3_000_000_000, tokens * width * 6),
        name="scale",
    )(mixer_input, factors, rows)

    half = width // 2
    carried = (sds((state + 8, half), BF16), sds((state, half), F32), sds((8, half), F32))
    first_out, second_out, mine, mine_exp = pl.pallas_call(
        functools.partial(state_kernel, layout),
        in_specs=[VMEM_SPEC] * 3,
        out_specs=(VMEM_SPEC,) * 4,
        out_shape=carried[:1] + carried,
        scratch_shapes=[pltpu.VMEM((state, width), F32)],
        compiler_params=grant(4),
        cost_estimate=cost(2 * tokens * width * state, tokens * width * 2),
        name="state",
    )(to_total, write_t, rows)

    def local(first, count, slots, after):
        return pl.pallas_call(
            functools.partial(
                local_kernel, heads, padded, local_bits, first, count, layout, tile
            ),
            in_specs=[VMEM_SPEC] * 10 + [ANY_SPEC],
            out_specs=(VMEM_SPEC,) * 3,
            out_shape=(
                sds((count * BLOCK, width), F32), sds((count * BLOCK, width), F32),
                sds((local_bits, state, width), F32),
            ),
            scratch_shapes=[
                pltpu.VMEM((2, HALF, HALF), F32),
                pltpu.VMEM((local_bits * state, width), BF16),
                pltpu.VMEM((HALF, HALF), BF16),
                pltpu.VMEM((local_bits * state, BLOCK), BF16),
            ],
            compiler_params=grant(8),
            cost_estimate=cost(count * BLOCK * width * 2 * 2000, count * BLOCK * width * 8),
            name="local",
        )(
            mixer_input, scaled, write_t, read_t, factors, columns, cum_h, weight_h, rows,
            slots, after,
        )

    def swap(value, bit):
        return lax.ppermute(value, "seq", [(i, i ^ 1 << bit) for i in range(ranks)])

    shares = ([3] + [2] * (device_bits - 2) + [3])[:device_bits]
    starts = [0]
    for share in shares:
        starts.append(starts[-1] + max(1, blocks * share // sum(shares)))
    starts = [min(start, blocks) for start in starts[:-1]] + [blocks]

    slots = jnp.zeros((local_bits, 8, LANES), F32)
    bases, reaches = [], []
    own_parts = [swap(first_out, 0)]
    other_parts = [swap(second_out, 0)]
    after = rows
    payload = None
    for bit in range(device_bits):
        if starts[bit + 1] > starts[bit]:
            base, reach, slots = local(starts[bit], starts[bit + 1] - starts[bit], slots, after)
            bases.append(base)
            reaches.append(reach)
        if bit + 1 < device_bits:
            last = bit + 2 == device_bits
            shapes = carried[:1] if last else carried
            payload, *more = pl.pallas_call(
                functools.partial(merge_kernel, bit),
                in_specs=[VMEM_SPEC] * 3 + [ANY_SPEC],
                out_specs=(VMEM_SPEC,) * len(shapes),
                out_shape=shapes,
                compiler_params=grant(4),
                cost_estimate=cost(2 * state * width, state * width * 6),
                name="merge",
            )(own_parts[bit], mine, mine_exp, slots)
            if more:
                mine, mine_exp = more
            after = payload
            own_parts.append(swap(payload, bit + 1))
            if bit > 0:
                other_parts.append(swap(own_parts[bit], 0))
    starts = sorted(set(starts))

    if device_bits > 1:
        other_parts.append(swap(own_parts[-1], 0))

    def finish(side, operands, wanted, out):
        specs = [VMEM_SPEC] * len(operands)
        aliases = {}
        if out is not None:
            aliases = {len(operands): 0}
            operands = operands + [out]
            specs.append(ANY_SPEC)
        return pl.pallas_call(
            functools.partial(final_kernel, starts, local_bits, device_bits, wanted, side),
            in_specs=specs,
            out_specs=ANY_SPEC,
            out_shape=sds((tokens, width), BF16),
            input_output_aliases=aliases,
            scratch_shapes=[
                pltpu.VMEM((len(wanted) * state, half), BF16),
                pltpu.VMEM((blocks, BLOCK, half), BF16),
                pltpu.SemaphoreType.DMA((blocks,)),
            ],
            compiler_params=grant(6),
            cost_estimate=cost(tokens * width * state, tokens * width * 3),
            name="final",
        )(*operands)

    out = finish(0, [read_t, weight_h, *own_parts, *bases, *reaches], list(range(device_bits)), None)
    near_bits = device_bits - 1
    near = pl.pallas_call(
        functools.partial(near_kernel, starts, local_bits, near_bits),
        in_specs=[VMEM_SPEC] * (2 + near_bits + 2 * len(bases)),
        out_specs=VMEM_SPEC,
        out_shape=sds((tokens, half), F32),
        scratch_shapes=[pltpu.VMEM((near_bits * state, half), BF16)],
        compiler_params=grant(4),
        cost_estimate=cost(tokens * width * state * 2, tokens * width * 3),
        name="near",
    )(read_t, weight_h, *other_parts[:-1], *bases, *reaches)
    return finish(1, [read_t, weight_h, *other_parts, near, *reaches], [device_bits - 1], out)


def solution(mesh):
    placed = (
        P("seq", "head"),
        P("seq", "head"),
        P("seq", "head"),
        P("head", "seq"),
        P("head", "seq"),
        P("head"),
        P(),
        P(None, "seq"),
    )

    return jax.shard_map(
        on_device, mesh=mesh, in_specs=placed, out_specs=P("seq", "head"), check_vma=False
    )
```

```python
import functools

import jax
import jax.numpy as jnp
from jax import lax
from jax.experimental import pallas as pl
from jax.experimental.pallas import tpu as pltpu
from jax.sharding import PartitionSpec as P


BLOCK = 256
HALF = BLOCK // 2
LANES = 128
LOG2E = 1.4426950408889634
F32 = jnp.float32
BF16 = jnp.bfloat16
NT = (((1,), (1,)), ((), ()))
NN = (((1,), (0,)), ((), ()))
TN = (((0,), (0,)), ((), ()))
VMEM_SPEC = pl.BlockSpec(memory_space=pltpu.VMEM)
SMEM_SPEC = pl.BlockSpec(memory_space=pltpu.SMEM)
ANY_SPEC = pl.BlockSpec(memory_space=pl.ANY)
HBM_SPEC = pl.BlockSpec(memory_space=pltpu.HBM)


def dot(a, b, dims=NN):
    return lax.dot_general(a, b, dims, preferred_element_type=F32)


def three(a):
    high = a.astype(BF16)
    rest = a - high.astype(F32)
    middle = rest.astype(BF16)
    return high, middle, (rest - middle.astype(F32)).astype(BF16)


def two(a):
    high = a.astype(BF16).astype(F32)
    return high, a - high


def iota(shape, dim):
    return lax.broadcasted_iota(jnp.int32, shape, dim)


def as_bf16(mask):
    return mask.astype(F32).astype(BF16)


def spread(first_row, padded, heads, width):
    per_head = width // heads
    row = iota((4 * padded, width), 0) - first_row
    lane = iota((4 * padded, width), 1)
    inside = (row >= 0) & (row < 2 * padded)
    row = jnp.where(row >= padded, row - padded, row)
    own = (row * per_head <= lane) & (lane < (row + 1) * per_head) & (row < heads)
    return as_bf16(own & inside)


class Rows:
    def __init__(self, blocks):
        halves = 2 * blocks
        self.after, self.run = 0, halves
        self.middle, self.upper, self.decay = 2 * halves, 2 * halves + blocks, 2 * halves + 2 * blocks
        self.total = 2 * halves + 3 * blocks
        self.skip = self.total + 8 - self.total % 8
        self.count = -(-(self.skip + 8) // 16) * 16

    def ranges(self, tokens):
        halves = tokens // HALF
        blocks = halves // 2
        k = iota((self.count, 1), 0)
        low = (k + 1) * HALF
        high = jnp.full_like(k, tokens)
        low = jnp.where(k >= self.run, 0, low)
        high = jnp.where(k >= self.run, (k - self.run) * HALF, high)
        for first, start, size in (
            (self.middle, 0, HALF), (self.upper, HALF, HALF), (self.decay, 0, BLOCK)
        ):
            here = (k - first) * BLOCK + start
            low = jnp.where(k >= first, here, low)
            high = jnp.where(k >= first, here + size, high)
        low = jnp.where(k >= self.total, 0, low)
        high = jnp.where(k == self.total, tokens, jnp.where(k > self.total, 0, high))
        return low, high


def prep_kernel(
    heads, padded, layout, log_decay_far, step_size_far, level_index_far, level_table_far, gain_far,
    factors, columns, cum_h, weight_h, rows,
    log_decay, step_size, level_index, level_table, gain, decay, steps, packed, sems,
):
    pairs = (
        (log_decay_far, log_decay), (step_size_far, step_size), (level_index_far, level_index),
        (level_table_far, level_table), (gain_far, gain),
    )
    copies = [pltpu.make_async_copy(far, near, sems.at[n]) for n, (far, near) in enumerate(pairs)]
    for copy in copies:
        copy.start()
    tokens = log_decay.shape[1]
    width = rows.shape[1]
    blocks = tokens // BLOCK
    decay[...] = jnp.zeros_like(decay)
    steps[...] = jnp.zeros_like(steps)
    for copy in copies:
        copy.wait()
    decay[0:heads, :] = log_decay[...]
    steps[0:heads, :] = step_size[...]
    lower = as_bf16(iota((BLOCK, BLOCK), 0) >= iota((BLOCK, BLOCK), 1))
    levels = level_index.shape[0]
    weight = jnp.zeros(level_index.shape, F32)
    index = level_index[...]
    for entry in range(level_table.shape[1]):
        weight = weight + jnp.where(index == entry, level_table[:, entry : entry + 1], 0.0)
    weight_h[...] = weight
    packed[...] = jnp.zeros_like(packed)
    for c in range(blocks):
        at = slice(c * BLOCK, (c + 1) * BLOCK)
        high, middle, low = three(decay[:, at])
        cum = (dot(low, lower, NT) + dot(middle, lower, NT)) + dot(high, lower, NT)
        step = steps[:, at]
        mid = cum[:, HALF - 1 : HALF]
        end = cum[:, BLOCK - 1 : BLOCK]
        first = iota((padded, BLOCK), 1) < HALF
        column = two(step * jnp.exp(jnp.where(first, mid, end) - cum))
        row = two(jnp.exp(cum - jnp.where(first, 0.0, mid)))
        four = jnp.concatenate([column[0], column[1], row[0], row[1]], 0)
        factors[at, :] = four.T.astype(BF16)
        scaled = cum * LOG2E
        cum_h[:, at] = scaled - jnp.log2(step)
        packed[0:padded, :] = scaled
        packed[padded : padded + levels, :] = weight_h[:, at]
        columns[at, :] = packed[...].T
    token = iota((rows.shape[0], tokens), 1)
    begin, finish = layout.ranges(tokens)
    chosen = as_bf16((token >= begin) & (token < finish))
    high, middle, low = three(decay[...])
    sums = (dot(chosen, low, NT) + dot(chosen, middle, NT)) + dot(chosen, high, NT)
    high, low = two(jnp.exp(sums))
    per_head = width // heads
    head = iota((padded, width), 0) * per_head
    lane = iota((padded, width), 1)
    own = as_bf16((head <= lane) & (lane < head + per_head))
    rows[...] = dot(high.astype(BF16), own) + dot(low.astype(BF16), own)
    gains = jnp.broadcast_to(gain[...], (8, heads))
    high, middle, low = three(gains)
    own = own[:heads]
    rows[layout.skip : layout.skip + 8, :] = (dot(low, own) + dot(middle, own)) + dot(high, own)


def scale_kernel(heads, padded, layout, mixer, factors, rows, scaled, to_total):
    tokens, width = mixer.shape
    wide = spread(0, padded, heads, width)

    def step(a, carry):
        at = pl.ds(pl.multiple_of(a * HALF, HALF), HALF)
        row = rows[pl.ds(layout.after + a, 1), :]
        value = mixer[at, :].astype(F32) * dot(factors[at, :], wide)
        scaled[at, :] = value.astype(BF16)
        to_total[at, :] = (value * row).astype(BF16)
        return carry

    lax.fori_loop(0, tokens // HALF, step, 0, unroll=4)


def exp_rows(total, count):
    where = iota((count, total.shape[1]), 0)
    high = total.astype(BF16).astype(F32)
    return jnp.where(where == 0, high, jnp.where(where == 1, total - high, 0.0)).astype(BF16)


def own_columns(width):
    rank = lax.axis_index("seq")
    mine = (rank & 1) * (width // 2)
    other = width // 2 - mine
    aligned = lambda at: pl.ds(pl.multiple_of(at, LANES), width // 2)
    return aligned(mine), aligned(other)


def state_kernel(layout, to_total, write_t, rows, first, second, mine, mine_exp, whole):
    state = write_t.shape[0]
    own, other = own_columns(whole.shape[1])
    whole[...] = dot(write_t[...], to_total[...])
    for payload, at in ((first, other), (second, own)):
        payload[0:state, :] = whole[:, at].astype(BF16)
        total = rows[layout.total : layout.total + 1, at]
        payload[state:, :] = exp_rows(total, payload.shape[0] - state)
    mine[...] = whole[:, own]
    mine_exp[...] = jnp.broadcast_to(rows[layout.total : layout.total + 1, own], mine_exp.shape)


def upper_half(bit, width):
    rank = lax.axis_index("seq")
    return ((jnp.zeros((1, width), jnp.int32) + rank) >> bit) & 1 > 0


def merge_kernel(bit, received, mine, mine_exp, after, payload, *more):
    state, width = mine.shape
    extra = received[state:, :].astype(F32)
    other_exp = extra[0:1] + extra[1:2]
    own_exp = mine_exp[0:1, :]
    upper = upper_half(bit, width)
    own_scale = jnp.where(upper, 1.0, other_exp)
    other_scale = jnp.where(upper, own_exp, 1.0)
    new = own_scale * mine[...] + other_scale * received[0:state, :].astype(F32)
    payload[0:state, :] = new.astype(BF16)
    total = own_exp * other_exp
    payload[state:, :] = exp_rows(total, payload.shape[0] - state)
    if more:
        merged, merged_exp = more
        merged[...] = new
        merged_exp[...] = jnp.broadcast_to(total, merged_exp.shape)


def join_kernel(first, second, *rest):
    joined = rest[-1]
    joined[: first.shape[0], :] = first[...]
    joined[first.shape[0] :, :] = second[...]


def local_kernel(
    heads, padded, bits, first, count, layout, tile,
    mixer, scaled, write_t, read_t, factors, columns, cum_h, weight_h, rows, slots_in, after,
    base, reach, slots, scores, narrow, off_scores, queries,
):
    width = mixer.shape[1]
    state = write_t.shape[0]
    per_head = width // heads
    heads_here = LANES // per_head
    wide = spread(2 * padded, padded, heads, width)
    causal = iota((HALF, HALF), 0) >= iota((HALF, HALF), 1)
    lane = iota((HALF, LANES), 1)
    own = [(lane >= k * per_head) & (lane < (k + 1) * per_head) for k in range(heads_here)]
    live = [bit for bit in range(bits) if (first >> bit) & 1]
    for bit in live:
        slots[bit] = slots_in[bit]
        narrow[bit * state : (bit + 1) * state, :] = slots_in[bit].astype(BF16)

    def head_part(c):
        at = slice(c * BLOCK, (c + 1) * BLOCK)
        live = [bit for bit in range(bits) if (c >> bit) & 1]
        if live:
            queries[0 : len(live) * state, :] = read_levels(read_t, weight_h, at, [bit + 1 for bit in live])
        weighted = dot(read_t[:, at], write_t[:, at], TN) * columns[at, padded : padded + 1]
        off_scores[...] = weighted[HALF:, :HALF].astype(BF16)
        scores[0] = jnp.where(causal, weighted[:HALF, :HALF], 0.0)
        scores[1] = jnp.where(causal, weighted[HALF:, HALF:], 0.0)

    def half_part(c, half):
        live = [bit for bit in range(bits) if (c >> bit) & 1]
        low = c * BLOCK + half * HALF
        half_at = slice(low, low + HALF)
        put_at = slice(low - first * BLOCK, low - first * BLOCK + HALF)
        for left in range(0, width, tile):
            lanes = slice(left, left + tile)
            near = dot(factors[half_at, :], wide[:, lanes])
            reach[put_at, lanes] = near * rows[layout.run + 2 * c + half : layout.run + 2 * c + half + 1, lanes]
            rest = None
            if half == 1:
                rest = dot(off_scores[...], scaled[c * BLOCK : c * BLOCK + HALF, lanes])
            if live:
                stored = [narrow[bit * state : (bit + 1) * state, lanes] for bit in live]
                stored = jnp.concatenate(stored, 0) if len(stored) > 1 else stored[0]
                level = dot(
                    queries[0 : len(live) * state, half * HALF : (half + 1) * HALF], stored, TN
                )
                middle = rows[layout.middle + c : layout.middle + c + 1, lanes]
                rest = level if rest is None else rest + middle * level
            skipped = rows[layout.skip : layout.skip + 1, lanes] * mixer[half_at, lanes].astype(F32)
            rest = skipped if rest is None else skipped + near * rest
            for inner in range(0, tile, LANES):
                here = slice(left + inner, left + inner + LANES)
                head = (left + inner) // per_head
                value = mixer[half_at, here]
                left_side = []
                for k in range(heads_here):
                    gap = columns[half_at, head + k : head + k + 1] - cum_h[head + k : head + k + 1, half_at]
                    mixing = scores[half] * jnp.exp2(jnp.minimum(gap, 0.0))
                    left_side.append(mixing.astype(BF16))
                part = dot(
                    jnp.concatenate(left_side, 1),
                    jnp.concatenate(
                        [jnp.where(mask, value.astype(F32), 0.0).astype(BF16) for mask in own], 0
                    ),
                )
                base[put_at, here] = part + rest[:, inner : inner + LANES]

    def update_part(c):
        live = [bit for bit in range(bits) if (c >> bit) & 1]
        ones = 0
        while ones < bits and (c >> ones) & 1:
            ones += 1
        low = c * BLOCK
        if ones == bits:
            return
        for left in range(0, width, tile):
            lanes = slice(left, left + tile)
            shrink = rows[layout.decay + c : layout.decay + c + 1, lanes]
            upper = rows[layout.upper + c : layout.upper + c + 1, lanes]
            fresh = upper * dot(
                write_t[:, low : low + HALF], scaled[low : low + HALF, lanes]
            ) + dot(write_t[:, low + HALF : low + BLOCK], scaled[low + HALF : low + BLOCK, lanes])
            for bit in range(ones):
                fresh = fresh + shrink * slots[bit, :, lanes]
            slots[ones, :, lanes] = fresh
            narrow[ones * state : (ones + 1) * state, lanes] = fresh.astype(BF16)
            for bit in live:
                if bit > ones:
                    kept = shrink * slots[bit, :, lanes]
                    slots[bit, :, lanes] = kept
                    narrow[bit * state : (bit + 1) * state, lanes] = kept.astype(BF16)

    def first_region(c):
        head_part(c)
        half_part(c, 0)

    def second_region(c):
        half_part(c, 1)
        update_part(c)

    when_here = pl.when(lax.axis_index("seq") >= 0)
    for c in range(first, first + count):
        when_here(functools.partial(first_region, c))
        when_here(functools.partial(second_region, c))


def bucket_rows(received, bits, state, width, wanted):
    running = jnp.ones((1, width), F32)
    out = []
    for bit in range(bits):
        upper = upper_half(bit, width)
        if bit in wanted:
            scale = jnp.where(upper, running, 0.0)
            out.append((received[bit][0:state, :].astype(F32) * scale).astype(BF16))
        if bit + 1 < bits:
            extra = received[bit][state:, :].astype(F32)
            running = jnp.where(upper, running * (extra[0:1] + extra[1:2]), running)
    return jnp.concatenate(out, 0) if len(out) > 1 else out[0]


def read_levels(read_t, weight_h, at, levels):
    read_f = read_t[:, at].astype(F32)
    queries = [(read_f * weight_h[level : level + 1, at]).astype(BF16) for level in levels]
    return jnp.concatenate(queries, 0) if len(queries) > 1 else queries[0]


def near_kernel(starts, local_bits, bits, read_t, weight_h, *rest):
    pieces = len(starts) - 1
    received, rest = rest[:bits], rest[bits:]
    bases, reaches, rest = rest[:pieces], rest[pieces : 2 * pieces], rest[2 * pieces :]
    out, buckets = rest
    columns = own_columns(bases[0].shape[1])[1]
    buckets[...] = bucket_rows(received, bits, read_t.shape[0], buckets.shape[1], range(bits))
    levels = [local_bits + 1 + bit for bit in range(bits)]
    for piece in range(pieces):

        def block(g, carry, piece=piece):
            at = pl.ds(pl.multiple_of((starts[piece] + g) * BLOCK, BLOCK), BLOCK)
            here = pl.ds(pl.multiple_of(g * BLOCK, BLOCK), BLOCK)
            part = dot(read_levels(read_t, weight_h, at, levels), buckets[...], TN)
            out[at, :] = bases[piece][here, columns] + part * reaches[piece][here, columns]
            return carry

        lax.fori_loop(0, starts[piece + 1] - starts[piece], block, 0, unroll=True)


def final_kernel(starts, local_bits, bits, wanted, side, read_t, weight_h, *rest):
    pieces = len(starts) - 1
    received, rest = rest[:bits], rest[bits:]
    near = None
    if side:
        near, rest = rest[0], rest[1:]
        reaches = rest[:pieces]
    else:
        bases, reaches = rest[:pieces], rest[pieces : 2 * pieces]
    out, buckets, ready, sems = rest[-4:]
    columns = own_columns(out.shape[1])[side]
    buckets[...] = bucket_rows(received, bits, read_t.shape[0], buckets.shape[1], wanted)
    levels = [local_bits + 1 + bit for bit in wanted]

    def copy(c, at):
        return pltpu.make_async_copy(ready.at[c], out.at[pl.ds(at, BLOCK), columns], sems.at[c])

    for piece in range(pieces):

        def block(g, carry, piece=piece):
            c = starts[piece] + g
            at = pl.multiple_of(c * BLOCK, BLOCK)
            here = pl.ds(pl.multiple_of(g * BLOCK, BLOCK), BLOCK)
            query = read_levels(read_t, weight_h, pl.ds(at, BLOCK), levels)
            part = dot(query, buckets[...], TN)
            if side:
                base = near[pl.ds(at, BLOCK), :]
            else:
                base = bases[piece][here, columns]
            ready[c] = (base + part * reaches[piece][here, columns]).astype(BF16)
            copy(c, at).start()
            return carry

        lax.fori_loop(0, starts[piece + 1] - starts[piece], block, 0, unroll=True)
    for c in range(starts[-1]):
        copy(c, c * BLOCK).wait()


def gather_columns(mine, axis, after):
    pieces = mine
    size = lax.axis_size(axis)
    stride = size // 2
    while stride:
        other = lax.ppermute(pieces, axis, [(i, i ^ stride) for i in range(size)])
        pieces = pl.pallas_call(
            join_kernel,
            in_specs=[VMEM_SPEC] * 2 + [ANY_SPEC],
            out_specs=VMEM_SPEC,
            out_shape=jax.ShapeDtypeStruct((2 * pieces.shape[0], pieces.shape[1]), BF16),
            compiler_params=grant(2),
            cost_estimate=cost(0, 4 * pieces.size),
            name="join",
        )(pieces, other, after)
        stride //= 2
    return pieces


def cost(flops, bytes_accessed):
    return pl.CostEstimate(flops=flops, bytes_accessed=bytes_accessed, transcendentals=0)


def grant(mebibytes):
    return pltpu.CompilerParams(vmem_limit_bytes=mebibytes << 20)


def on_device(
    mixer_input, write_map, read_map, step_size, log_decay, skip_gain, level_table, level_index
):
    tokens, width = mixer_input.shape
    heads = log_decay.shape[0]
    blocks = tokens // BLOCK
    local_bits = blocks.bit_length() - 1
    ranks = lax.axis_size("seq")
    device_bits = ranks.bit_length() - 1
    levels = level_table.shape[0]
    padded = LANES // 4
    tile = 256
    layout = Rows(blocks)
    sds = jax.ShapeDtypeStruct

    factors, columns, cum_h, weight_h, rows = pl.pallas_call(
        functools.partial(prep_kernel, heads, padded, layout),
        in_specs=[HBM_SPEC] * 5,
        out_specs=(VMEM_SPEC,) * 5,
        out_shape=(
            sds((tokens, LANES), BF16), sds((tokens, LANES), F32), sds((padded, tokens), F32),
            sds((levels, tokens), F32), sds((layout.count, width), F32),
        ),
        scratch_shapes=[
            pltpu.VMEM((heads, tokens), F32),
            pltpu.VMEM((heads, tokens), F32),
            pltpu.VMEM(level_index.shape, jnp.int32),
            pltpu.VMEM(level_table.shape, F32),
            pltpu.VMEM((1, heads), F32),
            pltpu.VMEM((padded, tokens), F32),
            pltpu.VMEM((padded, tokens), F32),
            pltpu.VMEM((LANES, BLOCK), F32),
            pltpu.SemaphoreType.DMA((5,)),
        ],
        compiler_params=grant(6),
        cost_estimate=cost(2_000_000_000, 4_000_000),
        name="prep",
    )(
        *(
            pltpu.with_memory_space_constraint(value, pltpu.HBM)
            for value in (log_decay, step_size, level_index, level_table, skip_gain[None, :])
        )
    )

    write_t = gather_columns(write_map.T, "head", rows)
    read_t = gather_columns(read_map.T, "head", rows)
    state = write_t.shape[0]

    scaled, to_total = pl.pallas_call(
        functools.partial(scale_kernel, heads, padded, layout),
        in_specs=[VMEM_SPEC] * 3,
        out_specs=(VMEM_SPEC,) * 2,
        out_shape=(sds((tokens, width), BF16),) * 2,
        compiler_params=grant(4),
        cost_estimate=cost(3_000_000_000, tokens * width * 6),
        name="scale",
    )(mixer_input, factors, rows)

    half = width // 2
    carried = (sds((state + 8, half), BF16), sds((state, half), F32), sds((8, half), F32))
    first_out, second_out, mine, mine_exp = pl.pallas_call(
        functools.partial(state_kernel, layout),
        in_specs=[VMEM_SPEC] * 3,
        out_specs=(VMEM_SPEC,) * 4,
        out_shape=carried[:1] + carried,
        scratch_shapes=[pltpu.VMEM((state, width), F32)],
        compiler_params=grant(4),
        cost_estimate=cost(2 * tokens * width * state, tokens * width * 2),
        name="state",
    )(to_total, write_t, rows)

    def local(first, count, slots, after):
        return pl.pallas_call(
            functools.partial(
                local_kernel, heads, padded, local_bits, first, count, layout, tile
            ),
            in_specs=[VMEM_SPEC] * 10 + [ANY_SPEC],
            out_specs=(VMEM_SPEC,) * 3,
            out_shape=(
                sds((count * BLOCK, width), F32), sds((count * BLOCK, width), F32),
                sds((local_bits, state, width), F32),
            ),
            scratch_shapes=[
                pltpu.VMEM((2, HALF, HALF), F32),
                pltpu.VMEM((local_bits * state, width), BF16),
                pltpu.VMEM((HALF, HALF), BF16),
                pltpu.VMEM((local_bits * state, BLOCK), BF16),
            ],
            compiler_params=grant(8),
            cost_estimate=cost(count * BLOCK * width * 2 * 2000, count * BLOCK * width * 8),
            name="local",
        )(
            mixer_input, scaled, write_t, read_t, factors, columns, cum_h, weight_h, rows,
            slots, after,
        )

    def swap(value, bit):
        return lax.ppermute(value, "seq", [(i, i ^ 1 << bit) for i in range(ranks)])

    shares = ([2] + [3] * (device_bits - 1))[:device_bits]
    starts = [0]
    for share in shares:
        starts.append(starts[-1] + max(1, blocks * share // sum(shares)))
    starts = [min(start, blocks) for start in starts[:-1]] + [blocks]

    slots = jnp.zeros((local_bits, 8, LANES), F32)
    bases, reaches = [], []
    own_parts = [swap(first_out, 0)]
    other_parts = [swap(second_out, 0)]
    after = rows
    payload = None
    for bit in range(device_bits):
        if starts[bit + 1] > starts[bit]:
            base, reach, slots = local(starts[bit], starts[bit + 1] - starts[bit], slots, after)
            bases.append(base)
            reaches.append(reach)
        if bit + 1 < device_bits:
            last = bit + 2 == device_bits
            shapes = carried[:1] if last else carried
            payload, *more = pl.pallas_call(
                functools.partial(merge_kernel, bit),
                in_specs=[VMEM_SPEC] * 3 + [ANY_SPEC],
                out_specs=(VMEM_SPEC,) * len(shapes),
                out_shape=shapes,
                compiler_params=grant(4),
                cost_estimate=cost(2 * state * width, state * width * 6),
                name="merge",
            )(own_parts[bit], mine, mine_exp, slots)
            if more:
                mine, mine_exp = more
            after = payload
            own_parts.append(swap(payload, bit + 1))
            if bit > 0:
                other_parts.append(swap(own_parts[bit], 0))
    starts = sorted(set(starts))

    if device_bits > 1:
        other_parts.append(swap(own_parts[-1], 0))

    def finish(side, operands, wanted, out):
        specs = [VMEM_SPEC] * len(operands)
        aliases = {}
        if out is not None:
            aliases = {len(operands): 0}
            operands = operands + [out]
            specs.append(ANY_SPEC)
        return pl.pallas_call(
            functools.partial(final_kernel, starts, local_bits, device_bits, wanted, side),
            in_specs=specs,
            out_specs=ANY_SPEC,
            out_shape=sds((tokens, width), BF16),
            input_output_aliases=aliases,
            scratch_shapes=[
                pltpu.VMEM((len(wanted) * state, half), BF16),
                pltpu.VMEM((blocks, BLOCK, half), BF16),
                pltpu.SemaphoreType.DMA((blocks,)),
            ],
            compiler_params=grant(6),
            cost_estimate=cost(tokens * width * state, tokens * width * 3),
            name="final",
        )(*operands)

    out = finish(0, [read_t, weight_h, *own_parts, *bases, *reaches], list(range(device_bits)), None)
    near_bits = device_bits - 1
    near = pl.pallas_call(
        functools.partial(near_kernel, starts, local_bits, near_bits),
        in_specs=[VMEM_SPEC] * (2 + near_bits + 2 * len(bases)),
        out_specs=VMEM_SPEC,
        out_shape=sds((tokens, half), F32),
        scratch_shapes=[pltpu.VMEM((near_bits * state, half), BF16)],
        compiler_params=grant(4),
        cost_estimate=cost(tokens * width * state * 2, tokens * width * 3),
        name="near",
    )(read_t, weight_h, *other_parts[:-1], *bases, *reaches)
    return finish(1, [read_t, weight_h, *other_parts, near, *reaches], [device_bits - 1], out)


def solution(mesh):
    placed = (
        P("seq", "head"),
        P("seq", "head"),
        P("seq", "head"),
        P("head", "seq"),
        P("head", "seq"),
        P("head"),
        P(),
        P(None, "seq"),
    )

    return jax.shard_map(
        on_device, mesh=mesh, in_specs=placed, out_specs=P("seq", "head"), check_vma=False
    )
```

```python
import functools

import jax
import jax.numpy as jnp
from jax import lax
from jax.experimental import pallas as pl
from jax.experimental.pallas import tpu as pltpu
from jax.sharding import PartitionSpec as P


BLOCK = 256
HALF = BLOCK // 2
LANES = 128
LOG2E = 1.4426950408889634
F32 = jnp.float32
BF16 = jnp.bfloat16
NT = (((1,), (1,)), ((), ()))
NN = (((1,), (0,)), ((), ()))
TN = (((0,), (0,)), ((), ()))
VMEM_SPEC = pl.BlockSpec(memory_space=pltpu.VMEM)
SMEM_SPEC = pl.BlockSpec(memory_space=pltpu.SMEM)
ANY_SPEC = pl.BlockSpec(memory_space=pl.ANY)
HBM_SPEC = pl.BlockSpec(memory_space=pltpu.HBM)


def dot(a, b, dims=NN):
    return lax.dot_general(a, b, dims, preferred_element_type=F32)


def three(a):
    high = a.astype(BF16)
    rest = a - high.astype(F32)
    middle = rest.astype(BF16)
    return high, middle, (rest - middle.astype(F32)).astype(BF16)


def two(a):
    high = a.astype(BF16).astype(F32)
    return high, a - high


def iota(shape, dim):
    return lax.broadcasted_iota(jnp.int32, shape, dim)


def as_bf16(mask):
    return mask.astype(F32).astype(BF16)


def spread(first_row, padded, heads, width):
    per_head = width // heads
    row = iota((4 * padded, width), 0) - first_row
    lane = iota((4 * padded, width), 1)
    inside = (row >= 0) & (row < 2 * padded)
    row = jnp.where(row >= padded, row - padded, row)
    own = (row * per_head <= lane) & (lane < (row + 1) * per_head) & (row < heads)
    return as_bf16(own & inside)


class Rows:
    def __init__(self, blocks):
        halves = 2 * blocks
        self.after, self.run = 0, halves
        self.middle, self.upper, self.decay = 2 * halves, 2 * halves + blocks, 2 * halves + 2 * blocks
        self.total = 2 * halves + 3 * blocks
        self.skip = self.total + 8 - self.total % 8
        self.count = -(-(self.skip + 8) // 16) * 16

    def ranges(self, tokens):
        halves = tokens // HALF
        blocks = halves // 2
        k = iota((self.count, 1), 0)
        low = (k + 1) * HALF
        high = jnp.full_like(k, tokens)
        low = jnp.where(k >= self.run, 0, low)
        high = jnp.where(k >= self.run, (k - self.run) * HALF, high)
        for first, start, size in (
            (self.middle, 0, HALF), (self.upper, HALF, HALF), (self.decay, 0, BLOCK)
        ):
            here = (k - first) * BLOCK + start
            low = jnp.where(k >= first, here, low)
            high = jnp.where(k >= first, here + size, high)
        low = jnp.where(k >= self.total, 0, low)
        high = jnp.where(k == self.total, tokens, jnp.where(k > self.total, 0, high))
        return low, high


def prep_kernel(
    heads, padded, layout, log_decay_far, step_size_far, level_index_far, level_table_far, gain_far,
    factors, columns, cum_h, weight_h, rows,
    log_decay, step_size, level_index, level_table, gain, decay, steps, packed, sems,
):
    pairs = (
        (log_decay_far, log_decay), (step_size_far, step_size), (level_index_far, level_index),
        (level_table_far, level_table), (gain_far, gain),
    )
    copies = [pltpu.make_async_copy(far, near, sems.at[n]) for n, (far, near) in enumerate(pairs)]
    for copy in copies:
        copy.start()
    tokens = log_decay.shape[1]
    width = rows.shape[1]
    blocks = tokens // BLOCK
    decay[...] = jnp.zeros_like(decay)
    steps[...] = jnp.zeros_like(steps)
    for copy in copies:
        copy.wait()
    decay[0:heads, :] = log_decay[...]
    steps[0:heads, :] = step_size[...]
    lower = as_bf16(iota((BLOCK, BLOCK), 0) >= iota((BLOCK, BLOCK), 1))
    levels = level_index.shape[0]
    weight = jnp.zeros(level_index.shape, F32)
    index = level_index[...]
    for entry in range(level_table.shape[1]):
        weight = weight + jnp.where(index == entry, level_table[:, entry : entry + 1], 0.0)
    weight_h[...] = weight
    packed[...] = jnp.zeros_like(packed)
    for c in range(blocks):
        at = slice(c * BLOCK, (c + 1) * BLOCK)
        high, middle, low = three(decay[:, at])
        cum = (dot(low, lower, NT) + dot(middle, lower, NT)) + dot(high, lower, NT)
        step = steps[:, at]
        mid = cum[:, HALF - 1 : HALF]
        end = cum[:, BLOCK - 1 : BLOCK]
        first = iota((padded, BLOCK), 1) < HALF
        column = two(step * jnp.exp(jnp.where(first, mid, end) - cum))
        row = two(jnp.exp(cum - jnp.where(first, 0.0, mid)))
        four = jnp.concatenate([column[0], column[1], row[0], row[1]], 0)
        factors[at, :] = four.T.astype(BF16)
        scaled = cum * LOG2E
        cum_h[:, at] = scaled - jnp.log2(step)
        packed[0:padded, :] = scaled
        packed[padded : padded + levels, :] = weight_h[:, at]
        columns[at, :] = packed[...].T
    token = iota((rows.shape[0], tokens), 1)
    begin, finish = layout.ranges(tokens)
    chosen = as_bf16((token >= begin) & (token < finish))
    high, middle, low = three(decay[...])
    sums = (dot(chosen, low, NT) + dot(chosen, middle, NT)) + dot(chosen, high, NT)
    high, low = two(jnp.exp(sums))
    per_head = width // heads
    head = iota((padded, width), 0) * per_head
    lane = iota((padded, width), 1)
    own = as_bf16((head <= lane) & (lane < head + per_head))
    rows[...] = dot(high.astype(BF16), own) + dot(low.astype(BF16), own)
    gains = jnp.broadcast_to(gain[...], (8, heads))
    high, middle, low = three(gains)
    own = own[:heads]
    rows[layout.skip : layout.skip + 8, :] = (dot(low, own) + dot(middle, own)) + dot(high, own)


def own_columns(width):
    rank = lax.axis_index("seq")
    mine = (rank & 1) * (width // 2)
    other = width // 2 - mine
    aligned = lambda at: pl.ds(pl.multiple_of(at, LANES), width // 2)
    return aligned(mine), aligned(other)


def scale_kernel(heads, padded, layout, side, mixer, factors, rows, *rest):
    scaled, to_total, wide = rest[-3:]
    tokens, width = mixer.shape
    columns = own_columns(width)[side]
    wide[...] = spread(0, padded, heads, width)

    def step(a, carry):
        at = pl.ds(pl.multiple_of(a * HALF, HALF), HALF)
        row = rows[pl.ds(layout.after + a, 1), columns]
        value = mixer[at, columns].astype(F32) * dot(factors[at, :], wide[:, columns])
        scaled[at, columns] = value.astype(BF16)
        to_total[at, :] = (value * row).astype(BF16)
        return carry

    lax.fori_loop(0, tokens // HALF, step, 0, unroll=4)


def exp_rows(total, count):
    where = iota((count, total.shape[1]), 0)
    high = total.astype(BF16).astype(F32)
    return jnp.where(where == 0, high, jnp.where(where == 1, total - high, 0.0)).astype(BF16)


def state_kernel(layout, side, to_total, write_t, rows, payload, *more):
    state = write_t.shape[0]
    columns = own_columns(rows.shape[1])[side]
    new = dot(write_t[...], to_total[...])
    payload[0:state, :] = new.astype(BF16)
    total = rows[pl.ds(layout.total, 1), columns]
    payload[state:, :] = exp_rows(total, payload.shape[0] - state)
    if more:
        mine, mine_exp = more
        mine[...] = new
        mine_exp[...] = jnp.broadcast_to(total, mine_exp.shape)


def upper_half(bit, width):
    rank = lax.axis_index("seq")
    return ((jnp.zeros((1, width), jnp.int32) + rank) >> bit) & 1 > 0


def merge_kernel(bit, received, mine, mine_exp, after, payload, *more):
    state, width = mine.shape
    extra = received[state:, :].astype(F32)
    other_exp = extra[0:1] + extra[1:2]
    own_exp = mine_exp[0:1, :]
    upper = upper_half(bit, width)
    own_scale = jnp.where(upper, 1.0, other_exp)
    other_scale = jnp.where(upper, own_exp, 1.0)
    new = own_scale * mine[...] + other_scale * received[0:state, :].astype(F32)
    payload[0:state, :] = new.astype(BF16)
    total = own_exp * other_exp
    payload[state:, :] = exp_rows(total, payload.shape[0] - state)
    if more:
        merged, merged_exp = more
        merged[...] = new
        merged_exp[...] = jnp.broadcast_to(total, merged_exp.shape)


def join_kernel(first, second, *rest):
    joined = rest[-1]
    joined[: first.shape[0], :] = first[...]
    joined[first.shape[0] :, :] = second[...]


def local_kernel(
    heads, padded, bits, first, count, layout, tile,
    mixer, scaled, write_t, read_t, factors, columns, cum_h, weight_h, rows, slots_in, after,
    base, reach, slots, scores, narrow, off_scores, queries,
):
    width = mixer.shape[1]
    state = write_t.shape[0]
    per_head = width // heads
    heads_here = LANES // per_head
    wide = spread(2 * padded, padded, heads, width)
    causal = iota((HALF, HALF), 0) >= iota((HALF, HALF), 1)
    lane = iota((HALF, LANES), 1)
    own = [(lane >= k * per_head) & (lane < (k + 1) * per_head) for k in range(heads_here)]
    live = [bit for bit in range(bits) if (first >> bit) & 1]
    for bit in live:
        slots[bit] = slots_in[bit]
        narrow[bit * state : (bit + 1) * state, :] = slots_in[bit].astype(BF16)

    def head_part(c):
        at = slice(c * BLOCK, (c + 1) * BLOCK)
        live = [bit for bit in range(bits) if (c >> bit) & 1]
        if live:
            queries[0 : len(live) * state, :] = read_levels(read_t, weight_h, at, [bit + 1 for bit in live])
        weighted = dot(read_t[:, at], write_t[:, at], TN) * columns[at, padded : padded + 1]
        off_scores[...] = weighted[HALF:, :HALF].astype(BF16)
        scores[0] = jnp.where(causal, weighted[:HALF, :HALF], 0.0)
        scores[1] = jnp.where(causal, weighted[HALF:, HALF:], 0.0)

    def half_part(c, half):
        live = [bit for bit in range(bits) if (c >> bit) & 1]
        low = c * BLOCK + half * HALF
        half_at = slice(low, low + HALF)
        put_at = slice(low - first * BLOCK, low - first * BLOCK + HALF)
        for left in range(0, width, tile):
            lanes = slice(left, left + tile)
            near = dot(factors[half_at, :], wide[:, lanes])
            reach[put_at, lanes] = near * rows[layout.run + 2 * c + half : layout.run + 2 * c + half + 1, lanes]
            rest = None
            if half == 1:
                rest = dot(off_scores[...], scaled[c * BLOCK : c * BLOCK + HALF, lanes])
            if live:
                stored = [narrow[bit * state : (bit + 1) * state, lanes] for bit in live]
                stored = jnp.concatenate(stored, 0) if len(stored) > 1 else stored[0]
                level = dot(
                    queries[0 : len(live) * state, half * HALF : (half + 1) * HALF], stored, TN
                )
                middle = rows[layout.middle + c : layout.middle + c + 1, lanes]
                rest = level if rest is None else rest + middle * level
            skipped = rows[layout.skip : layout.skip + 1, lanes] * mixer[half_at, lanes].astype(F32)
            rest = skipped if rest is None else skipped + near * rest
            for inner in range(0, tile, LANES):
                here = slice(left + inner, left + inner + LANES)
                head = (left + inner) // per_head
                value = mixer[half_at, here]
                left_side = []
                for k in range(heads_here):
                    gap = columns[half_at, head + k : head + k + 1] - cum_h[head + k : head + k + 1, half_at]
                    mixing = scores[half] * jnp.exp2(jnp.minimum(gap, 0.0))
                    left_side.append(mixing.astype(BF16))
                part = dot(
                    jnp.concatenate(left_side, 1),
                    jnp.concatenate(
                        [jnp.where(mask, value.astype(F32), 0.0).astype(BF16) for mask in own], 0
                    ),
                )
                base[put_at, here] = part + rest[:, inner : inner + LANES]

    def update_part(c):
        live = [bit for bit in range(bits) if (c >> bit) & 1]
        ones = 0
        while ones < bits and (c >> ones) & 1:
            ones += 1
        low = c * BLOCK
        if ones == bits:
            return
        for left in range(0, width, tile):
            lanes = slice(left, left + tile)
            shrink = rows[layout.decay + c : layout.decay + c + 1, lanes]
            upper = rows[layout.upper + c : layout.upper + c + 1, lanes]
            fresh = upper * dot(
                write_t[:, low : low + HALF], scaled[low : low + HALF, lanes]
            ) + dot(write_t[:, low + HALF : low + BLOCK], scaled[low + HALF : low + BLOCK, lanes])
            for bit in range(ones):
                fresh = fresh + shrink * slots[bit, :, lanes]
            slots[ones, :, lanes] = fresh
            narrow[ones * state : (ones + 1) * state, lanes] = fresh.astype(BF16)
            for bit in live:
                if bit > ones:
                    kept = shrink * slots[bit, :, lanes]
                    slots[bit, :, lanes] = kept
                    narrow[bit * state : (bit + 1) * state, lanes] = kept.astype(BF16)

    def first_region(c):
        head_part(c)
        half_part(c, 0)

    def second_region(c):
        half_part(c, 1)
        update_part(c)

    when_here = pl.when(lax.axis_index("seq") >= 0)
    for c in range(first, first + count):
        when_here(functools.partial(first_region, c))
        when_here(functools.partial(second_region, c))


def bucket_rows(received, bits, state, width, wanted):
    running = jnp.ones((1, width), F32)
    out = []
    for bit in range(bits):
        upper = upper_half(bit, width)
        if bit in wanted:
            scale = jnp.where(upper, running, 0.0)
            out.append((received[bit][0:state, :].astype(F32) * scale).astype(BF16))
        if bit + 1 < bits:
            extra = received[bit][state:, :].astype(F32)
            running = jnp.where(upper, running * (extra[0:1] + extra[1:2]), running)
    return jnp.concatenate(out, 0) if len(out) > 1 else out[0]


def read_levels(read_t, weight_h, at, levels):
    read_f = read_t[:, at].astype(F32)
    queries = [(read_f * weight_h[level : level + 1, at]).astype(BF16) for level in levels]
    return jnp.concatenate(queries, 0) if len(queries) > 1 else queries[0]


def near_kernel(starts, local_bits, bits, read_t, weight_h, *rest):
    pieces = len(starts) - 1
    received, rest = rest[:bits], rest[bits:]
    bases, reaches, rest = rest[:pieces], rest[pieces : 2 * pieces], rest[2 * pieces :]
    out, buckets = rest
    columns = own_columns(bases[0].shape[1])[1]
    buckets[...] = bucket_rows(received, bits, read_t.shape[0], buckets.shape[1], range(bits))
    levels = [local_bits + 1 + bit for bit in range(bits)]
    for piece in range(pieces):

        def block(g, carry, piece=piece):
            at = pl.ds(pl.multiple_of((starts[piece] + g) * BLOCK, BLOCK), BLOCK)
            here = pl.ds(pl.multiple_of(g * BLOCK, BLOCK), BLOCK)
            part = dot(read_levels(read_t, weight_h, at, levels), buckets[...], TN)
            out[at, :] = bases[piece][here, columns] + part * reaches[piece][here, columns]
            return carry

        lax.fori_loop(0, starts[piece + 1] - starts[piece], block, 0, unroll=True)


def final_kernel(starts, local_bits, bits, wanted, side, read_t, weight_h, *rest):
    pieces = len(starts) - 1
    received, rest = rest[:bits], rest[bits:]
    near = None
    if side:
        near, rest = rest[0], rest[1:]
        reaches = rest[:pieces]
    else:
        bases, reaches = rest[:pieces], rest[pieces : 2 * pieces]
    out, buckets, ready, sems = rest[-4:]
    columns = own_columns(out.shape[1])[side]
    buckets[...] = bucket_rows(received, bits, read_t.shape[0], buckets.shape[1], wanted)
    levels = [local_bits + 1 + bit for bit in wanted]

    def copy(c, at):
        return pltpu.make_async_copy(ready.at[c], out.at[pl.ds(at, BLOCK), columns], sems.at[c])

    for piece in range(pieces):

        def block(g, carry, piece=piece):
            c = starts[piece] + g
            at = pl.multiple_of(c * BLOCK, BLOCK)
            here = pl.ds(pl.multiple_of(g * BLOCK, BLOCK), BLOCK)
            query = read_levels(read_t, weight_h, pl.ds(at, BLOCK), levels)
            part = dot(query, buckets[...], TN)
            if side:
                base = near[pl.ds(at, BLOCK), :]
            else:
                base = bases[piece][here, columns]
            ready[c] = (base + part * reaches[piece][here, columns]).astype(BF16)
            copy(c, at).start()
            return carry

        lax.fori_loop(0, starts[piece + 1] - starts[piece], block, 0, unroll=True)
    for c in range(starts[-1]):
        copy(c, c * BLOCK).wait()


def gather_columns(mine, axis, after):
    pieces = mine
    size = lax.axis_size(axis)
    stride = size // 2
    while stride:
        other = lax.ppermute(pieces, axis, [(i, i ^ stride) for i in range(size)])
        pieces = pl.pallas_call(
            join_kernel,
            in_specs=[VMEM_SPEC] * 2 + [ANY_SPEC],
            out_specs=VMEM_SPEC,
            out_shape=jax.ShapeDtypeStruct((2 * pieces.shape[0], pieces.shape[1]), BF16),
            compiler_params=grant(2),
            cost_estimate=cost(0, 4 * pieces.size),
            name="join",
        )(pieces, other, after)
        stride //= 2
    return pieces


def cost(flops, bytes_accessed):
    return pl.CostEstimate(flops=flops, bytes_accessed=bytes_accessed, transcendentals=0)


def grant(mebibytes):
    return pltpu.CompilerParams(vmem_limit_bytes=mebibytes << 20)


def on_device(
    mixer_input, write_map, read_map, step_size, log_decay, skip_gain, level_table, level_index
):
    tokens, width = mixer_input.shape
    heads = log_decay.shape[0]
    blocks = tokens // BLOCK
    local_bits = blocks.bit_length() - 1
    ranks = lax.axis_size("seq")
    device_bits = ranks.bit_length() - 1
    levels = level_table.shape[0]
    padded = LANES // 4
    tile = 256
    layout = Rows(blocks)
    sds = jax.ShapeDtypeStruct

    factors, columns, cum_h, weight_h, rows = pl.pallas_call(
        functools.partial(prep_kernel, heads, padded, layout),
        in_specs=[HBM_SPEC] * 5,
        out_specs=(VMEM_SPEC,) * 5,
        out_shape=(
            sds((tokens, LANES), BF16), sds((tokens, LANES), F32), sds((padded, tokens), F32),
            sds((levels, tokens), F32), sds((layout.count, width), F32),
        ),
        scratch_shapes=[
            pltpu.VMEM((heads, tokens), F32),
            pltpu.VMEM((heads, tokens), F32),
            pltpu.VMEM(level_index.shape, jnp.int32),
            pltpu.VMEM(level_table.shape, F32),
            pltpu.VMEM((1, heads), F32),
            pltpu.VMEM((padded, tokens), F32),
            pltpu.VMEM((padded, tokens), F32),
            pltpu.VMEM((LANES, BLOCK), F32),
            pltpu.SemaphoreType.DMA((5,)),
        ],
        compiler_params=grant(6),
        cost_estimate=cost(2_000_000_000, 4_000_000),
        name="prep",
    )(
        *(
            pltpu.with_memory_space_constraint(value, pltpu.HBM)
            for value in (log_decay, step_size, level_index, level_table, skip_gain[None, :])
        )
    )

    write_t = gather_columns(write_map.T, "head", rows)
    read_t = gather_columns(read_map.T, "head", rows)
    state = write_t.shape[0]

    half = width // 2
    carried = (sds((state + 8, half), BF16), sds((state, half), F32), sds((8, half), F32))

    def front(side, scaled):
        operands = [mixer_input, factors, rows]
        aliases = {}
        if scaled is not None:
            aliases = {len(operands): 0}
            operands.append(scaled)
        scaled, to_total = pl.pallas_call(
            functools.partial(scale_kernel, heads, padded, layout, side),
            in_specs=[VMEM_SPEC] * len(operands),
            out_specs=(VMEM_SPEC,) * 2,
            out_shape=(sds((tokens, width), BF16), sds((tokens, half), BF16)),
            input_output_aliases=aliases,
            scratch_shapes=[pltpu.VMEM((LANES, width), BF16)],
            compiler_params=grant(4),
            cost_estimate=cost(1_500_000_000, tokens * width * 3),
            name="scale",
        )(*operands)
        shapes = carried if side == 0 else carried[:1]
        results = pl.pallas_call(
            functools.partial(state_kernel, layout, side),
            in_specs=[VMEM_SPEC] * 3,
            out_specs=(VMEM_SPEC,) * len(shapes),
            out_shape=shapes,
            compiler_params=grant(4),
            cost_estimate=cost(tokens * width * state, tokens * width),
            name="state",
        )(to_total, write_t, rows)
        return scaled, results

    scaled, (first_out,) = front(1, None)
    scaled, (second_out, mine, mine_exp) = front(0, scaled)

    def local(first, count, slots, after):
        return pl.pallas_call(
            functools.partial(
                local_kernel, heads, padded, local_bits, first, count, layout, tile
            ),
            in_specs=[VMEM_SPEC] * 10 + [ANY_SPEC],
            out_specs=(VMEM_SPEC,) * 3,
            out_shape=(
                sds((count * BLOCK, width), F32), sds((count * BLOCK, width), F32),
                sds((local_bits, state, width), F32),
            ),
            scratch_shapes=[
                pltpu.VMEM((2, HALF, HALF), F32),
                pltpu.VMEM((local_bits * state, width), BF16),
                pltpu.VMEM((HALF, HALF), BF16),
                pltpu.VMEM((local_bits * state, BLOCK), BF16),
            ],
            compiler_params=grant(8),
            cost_estimate=cost(count * BLOCK * width * 2 * 2000, count * BLOCK * width * 8),
            name="local",
        )(
            mixer_input, scaled, write_t, read_t, factors, columns, cum_h, weight_h, rows,
            slots, after,
        )

    def swap(value, bit):
        return lax.ppermute(value, "seq", [(i, i ^ 1 << bit) for i in range(ranks)])

    shares = ([2] + [3] * (device_bits - 1))[:device_bits]
    starts = [0]
    for share in shares:
        starts.append(starts[-1] + max(1, blocks * share // sum(shares)))
    starts = [min(start, blocks) for start in starts[:-1]] + [blocks]

    slots = jnp.zeros((local_bits, 8, LANES), F32)
    bases, reaches = [], []
    own_parts = [swap(first_out, 0)]
    other_parts = [swap(second_out, 0)]
    after = rows
    payload = None
    for bit in range(device_bits):
        if starts[bit + 1] > starts[bit]:
            base, reach, slots = local(starts[bit], starts[bit + 1] - starts[bit], slots, after)
            bases.append(base)
            reaches.append(reach)
        if bit + 1 < device_bits:
            last = bit + 2 == device_bits
            shapes = carried[:1] if last else carried
            payload, *more = pl.pallas_call(
                functools.partial(merge_kernel, bit),
                in_specs=[VMEM_SPEC] * 3 + [ANY_SPEC],
                out_specs=(VMEM_SPEC,) * len(shapes),
                out_shape=shapes,
                compiler_params=grant(4),
                cost_estimate=cost(2 * state * width, state * width * 6),
                name="merge",
            )(own_parts[bit], mine, mine_exp, slots)
            if more:
                mine, mine_exp = more
            after = payload
            own_parts.append(swap(payload, bit + 1))
            if bit > 0:
                other_parts.append(swap(own_parts[bit], 0))
    starts = sorted(set(starts))

    if device_bits > 1:
        other_parts.append(swap(own_parts[-1], 0))

    def finish(side, operands, wanted, out):
        specs = [VMEM_SPEC] * len(operands)
        aliases = {}
        if out is not None:
            aliases = {len(operands): 0}
            operands = operands + [out]
            specs.append(ANY_SPEC)
        return pl.pallas_call(
            functools.partial(final_kernel, starts, local_bits, device_bits, wanted, side),
            in_specs=specs,
            out_specs=ANY_SPEC,
            out_shape=sds((tokens, width), BF16),
            input_output_aliases=aliases,
            scratch_shapes=[
                pltpu.VMEM((len(wanted) * state, half), BF16),
                pltpu.VMEM((blocks, BLOCK, half), BF16),
                pltpu.SemaphoreType.DMA((blocks,)),
            ],
            compiler_params=grant(6),
            cost_estimate=cost(tokens * width * state, tokens * width * 3),
            name="final",
        )(*operands)

    out = finish(0, [read_t, weight_h, *own_parts, *bases, *reaches], list(range(device_bits)), None)
    near_bits = device_bits - 1
    near = pl.pallas_call(
        functools.partial(near_kernel, starts, local_bits, near_bits),
        in_specs=[VMEM_SPEC] * (2 + near_bits + 2 * len(bases)),
        out_specs=VMEM_SPEC,
        out_shape=sds((tokens, half), F32),
        scratch_shapes=[pltpu.VMEM((near_bits * state, half), BF16)],
        compiler_params=grant(4),
        cost_estimate=cost(tokens * width * state * 2, tokens * width * 3),
        name="near",
    )(read_t, weight_h, *other_parts[:-1], *bases, *reaches)
    return finish(1, [read_t, weight_h, *other_parts, near, *reaches], [device_bits - 1], out)


def solution(mesh):
    placed = (
        P("seq", "head"),
        P("seq", "head"),
        P("seq", "head"),
        P("head", "seq"),
        P("head", "seq"),
        P("head"),
        P(),
        P(None, "seq"),
    )

    return jax.shard_map(
        on_device, mesh=mesh, in_specs=placed, out_specs=P("seq", "head"), check_vma=False
    )
```

```python
import functools

import jax
import jax.numpy as jnp
from jax import lax
from jax.experimental import pallas as pl
from jax.experimental.pallas import tpu as pltpu
from jax.sharding import PartitionSpec as P


BLOCK = 256
HALF = BLOCK // 2
LANES = 128
LOG2E = 1.4426950408889634
F32 = jnp.float32
BF16 = jnp.bfloat16
NT = (((1,), (1,)), ((), ()))
NN = (((1,), (0,)), ((), ()))
TN = (((0,), (0,)), ((), ()))
VMEM_SPEC = pl.BlockSpec(memory_space=pltpu.VMEM)
SMEM_SPEC = pl.BlockSpec(memory_space=pltpu.SMEM)
ANY_SPEC = pl.BlockSpec(memory_space=pl.ANY)
HBM_SPEC = pl.BlockSpec(memory_space=pltpu.HBM)


def dot(a, b, dims=NN):
    return lax.dot_general(a, b, dims, preferred_element_type=F32)


def three(a):
    high = a.astype(BF16)
    rest = a - high.astype(F32)
    middle = rest.astype(BF16)
    return high, middle, (rest - middle.astype(F32)).astype(BF16)


def two(a):
    high = a.astype(BF16).astype(F32)
    return high, a - high


def iota(shape, dim):
    return lax.broadcasted_iota(jnp.int32, shape, dim)


def as_bf16(mask):
    return mask.astype(F32).astype(BF16)


def spread(first_row, padded, heads, width):
    per_head = width // heads
    row = iota((4 * padded, width), 0) - first_row
    lane = iota((4 * padded, width), 1)
    inside = (row >= 0) & (row < 2 * padded)
    row = jnp.where(row >= padded, row - padded, row)
    own = (row * per_head <= lane) & (lane < (row + 1) * per_head) & (row < heads)
    return as_bf16(own & inside)


class Rows:
    def __init__(self, blocks):
        halves = 2 * blocks
        self.after, self.run = 0, halves
        self.middle, self.upper, self.decay = 2 * halves, 2 * halves + blocks, 2 * halves + 2 * blocks
        self.total = 2 * halves + 3 * blocks
        self.skip = self.total + 8 - self.total % 8
        self.count = -(-(self.skip + 8) // 16) * 16

    def ranges(self, tokens):
        halves = tokens // HALF
        blocks = halves // 2
        k = iota((self.count, 1), 0)
        low = (k + 1) * HALF
        high = jnp.full_like(k, tokens)
        low = jnp.where(k >= self.run, 0, low)
        high = jnp.where(k >= self.run, (k - self.run) * HALF, high)
        for first, start, size in (
            (self.middle, 0, HALF), (self.upper, HALF, HALF), (self.decay, 0, BLOCK)
        ):
            here = (k - first) * BLOCK + start
            low = jnp.where(k >= first, here, low)
            high = jnp.where(k >= first, here + size, high)
        low = jnp.where(k >= self.total, 0, low)
        high = jnp.where(k == self.total, tokens, jnp.where(k > self.total, 0, high))
        return low, high


def prep_kernel(
    heads, padded, layout, log_decay_far, step_size_far, level_index_far, level_table_far, gain_far,
    factors, columns, cum_h, weight_h, rows,
    log_decay, step_size, level_index, level_table, gain, decay, steps, packed, sems,
):
    pairs = (
        (log_decay_far, log_decay), (step_size_far, step_size), (level_index_far, level_index),
        (level_table_far, level_table), (gain_far, gain),
    )
    copies = [pltpu.make_async_copy(far, near, sems.at[n]) for n, (far, near) in enumerate(pairs)]
    for copy in copies:
        copy.start()
    tokens = log_decay.shape[1]
    width = rows.shape[1]
    blocks = tokens // BLOCK
    decay[...] = jnp.zeros_like(decay)
    steps[...] = jnp.zeros_like(steps)
    for copy in copies:
        copy.wait()
    decay[0:heads, :] = log_decay[...]
    steps[0:heads, :] = step_size[...]
    lower = as_bf16(iota((BLOCK, BLOCK), 0) >= iota((BLOCK, BLOCK), 1))
    levels = level_index.shape[0]
    weight = jnp.zeros(level_index.shape, F32)
    index = level_index[...]
    for entry in range(level_table.shape[1]):
        weight = weight + jnp.where(index == entry, level_table[:, entry : entry + 1], 0.0)
    weight_h[...] = weight
    packed[...] = jnp.zeros_like(packed)
    for c in range(blocks):
        at = slice(c * BLOCK, (c + 1) * BLOCK)
        high, middle, low = three(decay[:, at])
        cum = (dot(low, lower, NT) + dot(middle, lower, NT)) + dot(high, lower, NT)
        step = steps[:, at]
        mid = cum[:, HALF - 1 : HALF]
        end = cum[:, BLOCK - 1 : BLOCK]
        first = iota((padded, BLOCK), 1) < HALF
        column = two(step * jnp.exp(jnp.where(first, mid, end) - cum))
        row = two(jnp.exp(cum - jnp.where(first, 0.0, mid)))
        four = jnp.concatenate([column[0], column[1], row[0], row[1]], 0)
        factors[at, :] = four.T.astype(BF16)
        scaled = cum * LOG2E
        cum_h[:, at] = scaled - jnp.log2(step)
        packed[0:padded, :] = scaled
        packed[padded : padded + levels, :] = weight_h[:, at]
        columns[at, :] = packed[...].T
    token = iota((rows.shape[0], tokens), 1)
    begin, finish = layout.ranges(tokens)
    chosen = as_bf16((token >= begin) & (token < finish))
    high, middle, low = three(decay[...])
    sums = (dot(chosen, low, NT) + dot(chosen, middle, NT)) + dot(chosen, high, NT)
    high, low = two(jnp.exp(sums))
    per_head = width // heads
    head = iota((padded, width), 0) * per_head
    lane = iota((padded, width), 1)
    own = as_bf16((head <= lane) & (lane < head + per_head))
    rows[...] = dot(high.astype(BF16), own) + dot(low.astype(BF16), own)
    gains = jnp.broadcast_to(gain[...], (8, heads))
    high, middle, low = three(gains)
    own = own[:heads]
    rows[layout.skip : layout.skip + 8, :] = (dot(low, own) + dot(middle, own)) + dot(high, own)


def own_columns(width):
    rank = lax.axis_index("seq")
    mine = (rank & 1) * (width // 2)
    other = width // 2 - mine
    aligned = lambda at: pl.ds(pl.multiple_of(at, LANES), width // 2)
    return aligned(mine), aligned(other)


def scale_kernel(heads, padded, layout, side, mixer, factors, rows, *rest):
    scaled, to_total, wide = rest[-3:]
    tokens, width = mixer.shape
    columns = own_columns(width)[side]
    wide[...] = spread(0, padded, heads, width)

    def step(a, carry):
        at = pl.ds(pl.multiple_of(a * HALF, HALF), HALF)
        row = rows[pl.ds(layout.after + a, 1), columns]
        value = mixer[at, columns].astype(F32) * dot(factors[at, :], wide[:, columns])
        scaled[at, columns] = value.astype(BF16)
        to_total[at, :] = (value * row).astype(BF16)
        return carry

    lax.fori_loop(0, tokens // HALF, step, 0, unroll=4)


def exp_rows(total, count):
    where = iota((count, total.shape[1]), 0)
    high = total.astype(BF16).astype(F32)
    return jnp.where(where == 0, high, jnp.where(where == 1, total - high, 0.0)).astype(BF16)


def state_kernel(layout, side, to_total, write_t, rows, payload, *more):
    state = write_t.shape[0]
    columns = own_columns(rows.shape[1])[side]
    new = dot(write_t[...], to_total[...])
    payload[0:state, :] = new.astype(BF16)
    total = rows[pl.ds(layout.total, 1), columns]
    payload[state:, :] = exp_rows(total, payload.shape[0] - state)
    if more:
        mine, mine_exp = more
        mine[...] = new
        mine_exp[...] = jnp.broadcast_to(total, mine_exp.shape)


def upper_half(bit, width):
    rank = lax.axis_index("seq")
    return ((jnp.zeros((1, width), jnp.int32) + rank) >> bit) & 1 > 0


def merge_kernel(bit, received, mine, mine_exp, after, payload, *more):
    state, width = mine.shape
    extra = received[state:, :].astype(F32)
    other_exp = extra[0:1] + extra[1:2]
    own_exp = mine_exp[0:1, :]
    upper = upper_half(bit, width)
    own_scale = jnp.where(upper, 1.0, other_exp)
    other_scale = jnp.where(upper, own_exp, 1.0)
    new = own_scale * mine[...] + other_scale * received[0:state, :].astype(F32)
    payload[0:state, :] = new.astype(BF16)
    total = own_exp * other_exp
    payload[state:, :] = exp_rows(total, payload.shape[0] - state)
    if more:
        merged, merged_exp = more
        merged[...] = new
        merged_exp[...] = jnp.broadcast_to(total, merged_exp.shape)


def join_kernel(first, second, *rest):
    joined = rest[-1]
    joined[: first.shape[0], :] = first[...]
    joined[first.shape[0] :, :] = second[...]


def local_kernel(
    heads, padded, bits, first, count, layout, tile,
    mixer, scaled, write_t, read_t, factors, columns, cum_h, weight_h, rows, slots_in, after,
    base, reach, slots, scores, narrow, off_scores, queries,
):
    width = mixer.shape[1]
    state = write_t.shape[0]
    per_head = width // heads
    heads_here = LANES // per_head
    wide = spread(2 * padded, padded, heads, width)
    causal = iota((HALF, HALF), 0) >= iota((HALF, HALF), 1)
    lane = iota((HALF, LANES), 1)
    own = [(lane >= k * per_head) & (lane < (k + 1) * per_head) for k in range(heads_here)]
    live = [bit for bit in range(bits) if (first >> bit) & 1]
    for bit in live:
        slots[bit] = slots_in[bit]
        narrow[bit * state : (bit + 1) * state, :] = slots_in[bit].astype(BF16)

    def head_part(c):
        at = slice(c * BLOCK, (c + 1) * BLOCK)
        live = [bit for bit in range(bits) if (c >> bit) & 1]
        if live:
            queries[0 : len(live) * state, :] = read_levels(read_t, weight_h, at, [bit + 1 for bit in live])
        weighted = dot(read_t[:, at], write_t[:, at], TN) * columns[at, padded : padded + 1]
        off_scores[...] = weighted[HALF:, :HALF].astype(BF16)
        scores[0] = jnp.where(causal, weighted[:HALF, :HALF], 0.0)
        scores[1] = jnp.where(causal, weighted[HALF:, HALF:], 0.0)

    def half_part(c, half):
        live = [bit for bit in range(bits) if (c >> bit) & 1]
        low = c * BLOCK + half * HALF
        half_at = slice(low, low + HALF)
        put_at = slice(low - first * BLOCK, low - first * BLOCK + HALF)
        for left in range(0, width, tile):
            lanes = slice(left, left + tile)
            near = dot(factors[half_at, :], wide[:, lanes])
            reach[put_at, lanes] = near * rows[layout.run + 2 * c + half : layout.run + 2 * c + half + 1, lanes]
            rest = None
            if half == 1:
                rest = dot(off_scores[...], scaled[c * BLOCK : c * BLOCK + HALF, lanes])
            if live:
                stored = [narrow[bit * state : (bit + 1) * state, lanes] for bit in live]
                stored = jnp.concatenate(stored, 0) if len(stored) > 1 else stored[0]
                level = dot(
                    queries[0 : len(live) * state, half * HALF : (half + 1) * HALF], stored, TN
                )
                middle = rows[layout.middle + c : layout.middle + c + 1, lanes]
                rest = level if rest is None else rest + middle * level
            skipped = rows[layout.skip : layout.skip + 1, lanes] * mixer[half_at, lanes].astype(F32)
            rest = skipped if rest is None else skipped + near * rest
            for inner in range(0, tile, LANES):
                here = slice(left + inner, left + inner + LANES)
                head = (left + inner) // per_head
                value = mixer[half_at, here]
                left_side = []
                for k in range(heads_here):
                    gap = columns[half_at, head + k : head + k + 1] - cum_h[head + k : head + k + 1, half_at]
                    mixing = scores[half] * jnp.exp2(jnp.minimum(gap, 0.0))
                    left_side.append(mixing.astype(BF16))
                part = dot(
                    jnp.concatenate(left_side, 1),
                    jnp.concatenate(
                        [jnp.where(mask, value.astype(F32), 0.0).astype(BF16) for mask in own], 0
                    ),
                )
                base[put_at, here] = part + rest[:, inner : inner + LANES]

    def update_part(c):
        live = [bit for bit in range(bits) if (c >> bit) & 1]
        ones = 0
        while ones < bits and (c >> ones) & 1:
            ones += 1
        low = c * BLOCK
        if ones == bits:
            return
        for left in range(0, width, tile):
            lanes = slice(left, left + tile)
            shrink = rows[layout.decay + c : layout.decay + c + 1, lanes]
            upper = rows[layout.upper + c : layout.upper + c + 1, lanes]
            fresh = upper * dot(
                write_t[:, low : low + HALF], scaled[low : low + HALF, lanes]
            ) + dot(write_t[:, low + HALF : low + BLOCK], scaled[low + HALF : low + BLOCK, lanes])
            for bit in range(ones):
                fresh = fresh + shrink * slots[bit, :, lanes]
            slots[ones, :, lanes] = fresh
            narrow[ones * state : (ones + 1) * state, lanes] = fresh.astype(BF16)
            for bit in live:
                if bit > ones:
                    kept = shrink * slots[bit, :, lanes]
                    slots[bit, :, lanes] = kept
                    narrow[bit * state : (bit + 1) * state, lanes] = kept.astype(BF16)

    def first_region(c):
        head_part(c)
        half_part(c, 0)

    def second_region(c):
        half_part(c, 1)
        update_part(c)

    when_here = pl.when(lax.axis_index("seq") >= 0)
    for c in range(first, first + count):
        when_here(functools.partial(first_region, c))
        when_here(functools.partial(second_region, c))


def bucket_rows(received, bits, state, width, wanted):
    running = jnp.ones((1, width), F32)
    out = []
    for bit in range(bits):
        upper = upper_half(bit, width)
        if bit in wanted:
            scale = jnp.where(upper, running, 0.0)
            out.append((received[bit][0:state, :].astype(F32) * scale).astype(BF16))
        if bit + 1 < bits:
            extra = received[bit][state:, :].astype(F32)
            running = jnp.where(upper, running * (extra[0:1] + extra[1:2]), running)
    return jnp.concatenate(out, 0) if len(out) > 1 else out[0]


def read_levels(read_t, weight_h, at, levels):
    read_f = read_t[:, at].astype(F32)
    queries = [(read_f * weight_h[level : level + 1, at]).astype(BF16) for level in levels]
    return jnp.concatenate(queries, 0) if len(queries) > 1 else queries[0]


def views(received):
    first = received[0]
    count = first.shape[0] // 2
    return [first.at[pl.ds(0, count), :], first.at[pl.ds(count, count), :]] + list(received[1:])


def near_kernel(starts, local_bits, bits, read_t, weight_h, *rest):
    pieces = len(starts) - 1
    received, rest = views(rest[: bits - 1]), rest[bits - 1 :]
    bases, reaches, rest = rest[:pieces], rest[pieces : 2 * pieces], rest[2 * pieces :]
    out, buckets = rest
    columns = own_columns(bases[0].shape[1])[1]
    buckets[...] = bucket_rows(received, bits, read_t.shape[0], buckets.shape[1], range(bits))
    levels = [local_bits + 1 + bit for bit in range(bits)]
    for piece in range(pieces):

        def block(g, carry, piece=piece):
            at = pl.ds(pl.multiple_of((starts[piece] + g) * BLOCK, BLOCK), BLOCK)
            here = pl.ds(pl.multiple_of(g * BLOCK, BLOCK), BLOCK)
            part = dot(read_levels(read_t, weight_h, at, levels), buckets[...], TN)
            out[at, :] = bases[piece][here, columns] + part * reaches[piece][here, columns]
            return carry

        lax.fori_loop(0, starts[piece + 1] - starts[piece], block, 0, unroll=True)


def final_kernel(starts, local_bits, bits, wanted, side, read_t, weight_h, *rest):
    pieces = len(starts) - 1
    near = None
    if side:
        received, near, rest = views(rest[: bits - 1]), rest[bits - 1], rest[bits:]
        reaches = rest[:pieces]
    else:
        received, rest = rest[:bits], rest[bits:]
        bases, reaches = rest[:pieces], rest[pieces : 2 * pieces]
    out, buckets, ready, sems = rest[-4:]
    columns = own_columns(out.shape[1])[side]
    buckets[...] = bucket_rows(received, bits, read_t.shape[0], buckets.shape[1], wanted)
    levels = [local_bits + 1 + bit for bit in wanted]

    def copy(c, at):
        return pltpu.make_async_copy(ready.at[c], out.at[pl.ds(at, BLOCK), columns], sems.at[c])

    for piece in range(pieces):

        def block(g, carry, piece=piece):
            c = starts[piece] + g
            at = pl.multiple_of(c * BLOCK, BLOCK)
            here = pl.ds(pl.multiple_of(g * BLOCK, BLOCK), BLOCK)
            query = read_levels(read_t, weight_h, pl.ds(at, BLOCK), levels)
            part = dot(query, buckets[...], TN)
            if side:
                base = near[pl.ds(at, BLOCK), :]
            else:
                base = bases[piece][here, columns]
            ready[c] = (base + part * reaches[piece][here, columns]).astype(BF16)
            copy(c, at).start()
            return carry

        lax.fori_loop(0, starts[piece + 1] - starts[piece], block, 0, unroll=True)
    for c in range(starts[-1]):
        copy(c, c * BLOCK).wait()


def gather_columns(mine, axis, after):
    pieces = mine
    size = lax.axis_size(axis)
    stride = size // 2
    while stride:
        other = lax.ppermute(pieces, axis, [(i, i ^ stride) for i in range(size)])
        pieces = pl.pallas_call(
            join_kernel,
            in_specs=[VMEM_SPEC] * 2 + [ANY_SPEC],
            out_specs=VMEM_SPEC,
            out_shape=jax.ShapeDtypeStruct((2 * pieces.shape[0], pieces.shape[1]), BF16),
            compiler_params=grant(2),
            cost_estimate=cost(0, 4 * pieces.size),
            name="join",
        )(pieces, other, after)
        stride //= 2
    return pieces


def cost(flops, bytes_accessed):
    return pl.CostEstimate(flops=flops, bytes_accessed=bytes_accessed, transcendentals=0)


def grant(mebibytes):
    return pltpu.CompilerParams(vmem_limit_bytes=mebibytes << 20)


def on_device(
    mixer_input, write_map, read_map, step_size, log_decay, skip_gain, level_table, level_index
):
    tokens, width = mixer_input.shape
    heads = log_decay.shape[0]
    blocks = tokens // BLOCK
    local_bits = blocks.bit_length() - 1
    ranks = lax.axis_size("seq")
    device_bits = ranks.bit_length() - 1
    levels = level_table.shape[0]
    padded = LANES // 4
    tile = 256
    layout = Rows(blocks)
    sds = jax.ShapeDtypeStruct

    factors, columns, cum_h, weight_h, rows = pl.pallas_call(
        functools.partial(prep_kernel, heads, padded, layout),
        in_specs=[HBM_SPEC] * 5,
        out_specs=(VMEM_SPEC,) * 5,
        out_shape=(
            sds((tokens, LANES), BF16), sds((tokens, LANES), F32), sds((padded, tokens), F32),
            sds((levels, tokens), F32), sds((layout.count, width), F32),
        ),
        scratch_shapes=[
            pltpu.VMEM((heads, tokens), F32),
            pltpu.VMEM((heads, tokens), F32),
            pltpu.VMEM(level_index.shape, jnp.int32),
            pltpu.VMEM(level_table.shape, F32),
            pltpu.VMEM((1, heads), F32),
            pltpu.VMEM((padded, tokens), F32),
            pltpu.VMEM((padded, tokens), F32),
            pltpu.VMEM((LANES, BLOCK), F32),
            pltpu.SemaphoreType.DMA((5,)),
        ],
        compiler_params=grant(6),
        cost_estimate=cost(2_000_000_000, 4_000_000),
        name="prep",
    )(
        *(
            pltpu.with_memory_space_constraint(value, pltpu.HBM)
            for value in (log_decay, step_size, level_index, level_table, skip_gain[None, :])
        )
    )

    write_t = gather_columns(write_map.T, "head", rows)
    read_t = gather_columns(read_map.T, "head", rows)
    state = write_t.shape[0]

    half = width // 2
    carried = (sds((state + 8, half), BF16), sds((state, half), F32), sds((8, half), F32))

    def front(side, scaled):
        operands = [mixer_input, factors, rows]
        aliases = {}
        if scaled is not None:
            aliases = {len(operands): 0}
            operands.append(scaled)
        scaled, to_total = pl.pallas_call(
            functools.partial(scale_kernel, heads, padded, layout, side),
            in_specs=[VMEM_SPEC] * len(operands),
            out_specs=(VMEM_SPEC,) * 2,
            out_shape=(sds((tokens, width), BF16), sds((tokens, half), BF16)),
            input_output_aliases=aliases,
            scratch_shapes=[pltpu.VMEM((LANES, width), BF16)],
            compiler_params=grant(4),
            cost_estimate=cost(1_500_000_000, tokens * width * 3),
            name="scale",
        )(*operands)
        shapes = carried if side == 0 else carried[:1]
        results = pl.pallas_call(
            functools.partial(state_kernel, layout, side),
            in_specs=[VMEM_SPEC] * 3,
            out_specs=(VMEM_SPEC,) * len(shapes),
            out_shape=shapes,
            compiler_params=grant(4),
            cost_estimate=cost(tokens * width * state, tokens * width),
            name="state",
        )(to_total, write_t, rows)
        return scaled, results

    scaled, (first_out,) = front(1, None)
    scaled, (second_out, mine, mine_exp) = front(0, scaled)

    def local(first, count, slots, after):
        return pl.pallas_call(
            functools.partial(
                local_kernel, heads, padded, local_bits, first, count, layout, tile
            ),
            in_specs=[VMEM_SPEC] * 10 + [ANY_SPEC],
            out_specs=(VMEM_SPEC,) * 3,
            out_shape=(
                sds((count * BLOCK, width), F32), sds((count * BLOCK, width), F32),
                sds((local_bits, state, width), F32),
            ),
            scratch_shapes=[
                pltpu.VMEM((2, HALF, HALF), F32),
                pltpu.VMEM((local_bits * state, width), BF16),
                pltpu.VMEM((HALF, HALF), BF16),
                pltpu.VMEM((local_bits * state, BLOCK), BF16),
            ],
            compiler_params=grant(8),
            cost_estimate=cost(count * BLOCK * width * 2 * 2000, count * BLOCK * width * 8),
            name="local",
        )(
            mixer_input, scaled, write_t, read_t, factors, columns, cum_h, weight_h, rows,
            slots, after,
        )

    def swap(value, bit):
        return lax.ppermute(value, "seq", [(i, i ^ 1 << bit) for i in range(ranks)])

    shares = ([2] + [3] * (device_bits - 1))[:device_bits]
    starts = [0]
    for share in shares:
        starts.append(starts[-1] + max(1, blocks * share // sum(shares)))
    starts = [min(start, blocks) for start in starts[:-1]] + [blocks]

    slots = jnp.zeros((local_bits, 8, LANES), F32)
    bases, reaches = [], []
    own_parts = [swap(first_out, 0)]
    other_parts = []
    after = rows
    payload = None
    for bit in range(device_bits):
        if starts[bit + 1] > starts[bit]:
            base, reach, slots = local(starts[bit], starts[bit + 1] - starts[bit], slots, after)
            bases.append(base)
            reaches.append(reach)
        if bit + 1 < device_bits:
            last = bit + 2 == device_bits
            shapes = carried[:1] if last else carried
            payload, *more = pl.pallas_call(
                functools.partial(merge_kernel, bit),
                in_specs=[VMEM_SPEC] * 3 + [ANY_SPEC],
                out_specs=(VMEM_SPEC,) * len(shapes),
                out_shape=shapes,
                compiler_params=grant(4),
                cost_estimate=cost(2 * state * width, state * width * 6),
                name="merge",
            )(own_parts[bit], mine, mine_exp, slots)
            if more:
                mine, mine_exp = more
            after = payload
            own_parts.append(swap(payload, bit + 1))
            if bit == 1:
                both = pl.pallas_call(
                    join_kernel,
                    in_specs=[VMEM_SPEC] * 2,
                    out_specs=VMEM_SPEC,
                    out_shape=sds((2 * payload.shape[0], half), BF16),
                    compiler_params=grant(2),
                    cost_estimate=cost(0, 8 * payload.size),
                    name="both",
                )(second_out, own_parts[1])
                other_parts.append(swap(both, 0))
            elif bit > 1:
                other_parts.append(swap(own_parts[bit], 0))
    starts = sorted(set(starts))

    if device_bits > 1:
        other_parts.append(swap(own_parts[-1], 0))

    def finish(side, operands, wanted, out):
        specs = [VMEM_SPEC] * len(operands)
        aliases = {}
        if out is not None:
            aliases = {len(operands): 0}
            operands = operands + [out]
            specs.append(ANY_SPEC)
        return pl.pallas_call(
            functools.partial(final_kernel, starts, local_bits, device_bits, wanted, side),
            in_specs=specs,
            out_specs=ANY_SPEC,
            out_shape=sds((tokens, width), BF16),
            input_output_aliases=aliases,
            scratch_shapes=[
                pltpu.VMEM((len(wanted) * state, half), BF16),
                pltpu.VMEM((blocks, BLOCK, half), BF16),
                pltpu.SemaphoreType.DMA((blocks,)),
            ],
            compiler_params=grant(6),
            cost_estimate=cost(tokens * width * state, tokens * width * 3),
            name="final",
        )(*operands)

    out = finish(0, [read_t, weight_h, *own_parts, *bases, *reaches], list(range(device_bits)), None)
    near_bits = device_bits - 1
    near = pl.pallas_call(
        functools.partial(near_kernel, starts, local_bits, near_bits),
        in_specs=[VMEM_SPEC] * (2 + near_bits - 1 + 2 * len(bases)),
        out_specs=VMEM_SPEC,
        out_shape=sds((tokens, half), F32),
        scratch_shapes=[pltpu.VMEM((near_bits * state, half), BF16)],
        compiler_params=grant(4),
        cost_estimate=cost(tokens * width * state * 2, tokens * width * 3),
        name="near",
    )(read_t, weight_h, *other_parts[:-1], *bases, *reaches)
    return finish(1, [read_t, weight_h, *other_parts, near, *reaches], [device_bits - 1], out)


def solution(mesh):
    placed = (
        P("seq", "head"),
        P("seq", "head"),
        P("seq", "head"),
        P("head", "seq"),
        P("head", "seq"),
        P("head"),
        P(),
        P(None, "seq"),
    )

    return jax.shard_map(
        on_device, mesh=mesh, in_specs=placed, out_specs=P("seq", "head"), check_vma=False
    )
```

```python
import functools

import jax
import jax.numpy as jnp
from jax import lax
from jax.experimental import pallas as pl
from jax.experimental.pallas import tpu as pltpu
from jax.sharding import PartitionSpec as P


BLOCK = 256
HALF = BLOCK // 2
LANES = 128
LOG2E = 1.4426950408889634
F32 = jnp.float32
BF16 = jnp.bfloat16
NT = (((1,), (1,)), ((), ()))
NN = (((1,), (0,)), ((), ()))
TN = (((0,), (0,)), ((), ()))
VMEM_SPEC = pl.BlockSpec(memory_space=pltpu.VMEM)
SMEM_SPEC = pl.BlockSpec(memory_space=pltpu.SMEM)
ANY_SPEC = pl.BlockSpec(memory_space=pl.ANY)
HBM_SPEC = pl.BlockSpec(memory_space=pltpu.HBM)


def dot(a, b, dims=NN):
    return lax.dot_general(a, b, dims, preferred_element_type=F32)


def three(a):
    high = a.astype(BF16)
    rest = a - high.astype(F32)
    middle = rest.astype(BF16)
    return high, middle, (rest - middle.astype(F32)).astype(BF16)


def two(a):
    high = a.astype(BF16).astype(F32)
    return high, a - high


def iota(shape, dim):
    return lax.broadcasted_iota(jnp.int32, shape, dim)


def as_bf16(mask):
    return mask.astype(F32).astype(BF16)


def spread(first_row, padded, heads, width, per_head=None, offset=0):
    per_head = per_head or width // heads
    row = iota((4 * padded, width), 0) - first_row
    lane = iota((4 * padded, width), 1) + offset
    inside = (row >= 0) & (row < 2 * padded)
    row = jnp.where(row >= padded, row - padded, row)
    own = (row * per_head <= lane) & (lane < (row + 1) * per_head) & (row < heads)
    return as_bf16(own & inside)


class Rows:
    def __init__(self, blocks):
        halves = 2 * blocks
        self.after, self.run = 0, halves
        self.middle, self.upper, self.decay = 2 * halves, 2 * halves + blocks, 2 * halves + 2 * blocks
        self.total = 2 * halves + 3 * blocks
        self.skip = self.total + 8 - self.total % 8
        self.count = -(-(self.skip + 8) // 16) * 16

    def ranges(self, tokens):
        halves = tokens // HALF
        blocks = halves // 2
        k = iota((self.count, 1), 0)
        low = (k + 1) * HALF
        high = jnp.full_like(k, tokens)
        low = jnp.where(k >= self.run, 0, low)
        high = jnp.where(k >= self.run, (k - self.run) * HALF, high)
        for first, start, size in (
            (self.middle, 0, HALF), (self.upper, HALF, HALF), (self.decay, 0, BLOCK)
        ):
            here = (k - first) * BLOCK + start
            low = jnp.where(k >= first, here, low)
            high = jnp.where(k >= first, here + size, high)
        low = jnp.where(k >= self.total, 0, low)
        high = jnp.where(k == self.total, tokens, jnp.where(k > self.total, 0, high))
        return low, high


def prep_kernel(
    heads, padded, layout, log_decay_far, step_size_far, level_index_far, level_table_far, gain_far,
    factors, columns, cum_h, weight_h, rows,
    log_decay, step_size, level_index, level_table, gain, decay, steps, packed, sems,
):
    pairs = (
        (log_decay_far, log_decay), (step_size_far, step_size), (level_index_far, level_index),
        (level_table_far, level_table), (gain_far, gain),
    )
    copies = [pltpu.make_async_copy(far, near, sems.at[n]) for n, (far, near) in enumerate(pairs)]
    for copy in copies:
        copy.start()
    tokens = log_decay.shape[1]
    width = rows.shape[1]
    blocks = tokens // BLOCK
    decay[...] = jnp.zeros_like(decay)
    steps[...] = jnp.zeros_like(steps)
    for copy in copies:
        copy.wait()
    decay[0:heads, :] = log_decay[...]
    steps[0:heads, :] = step_size[...]
    lower = as_bf16(iota((BLOCK, BLOCK), 0) >= iota((BLOCK, BLOCK), 1))
    levels = level_index.shape[0]
    weight = jnp.zeros(level_index.shape, F32)
    index = level_index[...]
    for entry in range(level_table.shape[1]):
        weight = weight + jnp.where(index == entry, level_table[:, entry : entry + 1], 0.0)
    weight_h[...] = weight
    packed[...] = jnp.zeros_like(packed)
    for c in range(blocks):
        at = slice(c * BLOCK, (c + 1) * BLOCK)
        high, middle, low = three(decay[:, at])
        cum = (dot(low, lower, NT) + dot(middle, lower, NT)) + dot(high, lower, NT)
        step = steps[:, at]
        mid = cum[:, HALF - 1 : HALF]
        end = cum[:, BLOCK - 1 : BLOCK]
        first = iota((padded, BLOCK), 1) < HALF
        column = two(step * jnp.exp(jnp.where(first, mid, end) - cum))
        row = two(jnp.exp(cum - jnp.where(first, 0.0, mid)))
        four = jnp.concatenate([column[0], column[1], row[0], row[1]], 0)
        factors[at, :] = four.T.astype(BF16)
        scaled = cum * LOG2E
        cum_h[:, at] = scaled - jnp.log2(step)
        packed[0:padded, :] = scaled
        packed[padded : padded + levels, :] = weight_h[:, at]
        columns[at, :] = packed[...].T
    token = iota((rows.shape[0], tokens), 1)
    begin, finish = layout.ranges(tokens)
    chosen = as_bf16((token >= begin) & (token < finish))
    high, middle, low = three(decay[...])
    sums = (dot(chosen, low, NT) + dot(chosen, middle, NT)) + dot(chosen, high, NT)
    high, low = two(jnp.exp(sums))
    per_head = width // heads
    head = iota((padded, width), 0) * per_head
    lane = iota((padded, width), 1)
    own = as_bf16((head <= lane) & (lane < head + per_head))
    rows[...] = dot(high.astype(BF16), own) + dot(low.astype(BF16), own)
    gains = jnp.broadcast_to(gain[...], (8, heads))
    high, middle, low = three(gains)
    own = own[:heads]
    rows[layout.skip : layout.skip + 8, :] = (dot(low, own) + dot(middle, own)) + dot(high, own)


def own_columns(width):
    rank = lax.axis_index("seq")
    mine = (rank & 1) * (width // 2)
    other = width // 2 - mine
    aligned = lambda at: pl.ds(pl.multiple_of(at, LANES), width // 2)
    return aligned(mine), aligned(other)


def scale_kernel(heads, padded, layout, side, mixer, factors, rows, *rest):
    scaled, to_total = rest[-2:]
    tokens, width = mixer.shape
    columns = own_columns(width)[side]
    rank = lax.axis_index("seq")
    first = ((rank + side) & 1) * (width // 2)
    wide = spread(0, padded, heads, width // 2, width // heads, first)

    def step(a, carry):
        at = pl.ds(pl.multiple_of(a * HALF, HALF), HALF)
        row = rows[pl.ds(layout.after + a, 1), columns]
        value = mixer[at, columns].astype(F32) * dot(factors[at, :], wide)
        scaled[at, columns] = value.astype(BF16)
        to_total[at, :] = (value * row).astype(BF16)
        return carry

    lax.fori_loop(0, tokens // HALF, step, 0, unroll=8)


def exp_rows(total, count):
    where = iota((count, total.shape[1]), 0)
    high = total.astype(BF16).astype(F32)
    return jnp.where(where == 0, high, jnp.where(where == 1, total - high, 0.0)).astype(BF16)


def state_kernel(layout, side, to_total, write_t, rows, payload, *more):
    state = write_t.shape[0]
    columns = own_columns(rows.shape[1])[side]
    new = dot(write_t[...], to_total[...])
    payload[0:state, :] = new.astype(BF16)
    total = rows[pl.ds(layout.total, 1), columns]
    payload[state:, :] = exp_rows(total, payload.shape[0] - state)
    if more:
        mine, mine_exp = more
        mine[...] = new
        mine_exp[...] = jnp.broadcast_to(total, mine_exp.shape)


def upper_half(bit, width):
    rank = lax.axis_index("seq")
    return ((jnp.zeros((1, width), jnp.int32) + rank) >> bit) & 1 > 0


def merge_kernel(bit, received, mine, mine_exp, after, payload, *more):
    state, width = mine.shape
    extra = received[state:, :].astype(F32)
    other_exp = extra[0:1] + extra[1:2]
    own_exp = mine_exp[0:1, :]
    upper = upper_half(bit, width)
    own_scale = jnp.where(upper, 1.0, other_exp)
    other_scale = jnp.where(upper, own_exp, 1.0)
    new = own_scale * mine[...] + other_scale * received[0:state, :].astype(F32)
    payload[0:state, :] = new.astype(BF16)
    total = own_exp * other_exp
    payload[state:, :] = exp_rows(total, payload.shape[0] - state)
    if more:
        merged, merged_exp = more
        merged[...] = new
        merged_exp[...] = jnp.broadcast_to(total, merged_exp.shape)


def join_kernel(first, second, *rest):
    joined = rest[-1]
    joined[: first.shape[0], :] = first[...]
    joined[first.shape[0] :, :] = second[...]


def local_kernel(
    heads, padded, bits, first, count, layout, tile,
    mixer, scaled, write_t, read_t, factors, columns, cum_h, weight_h, rows, slots_in, after,
    base, reach, slots, scores, narrow, off_scores, queries,
):
    width = mixer.shape[1]
    state = write_t.shape[0]
    per_head = width // heads
    heads_here = LANES // per_head
    wide = spread(2 * padded, padded, heads, width)
    causal = iota((HALF, HALF), 0) >= iota((HALF, HALF), 1)
    lane = iota((HALF, LANES), 1)
    own = [(lane >= k * per_head) & (lane < (k + 1) * per_head) for k in range(heads_here)]
    live = [bit for bit in range(bits) if (first >> bit) & 1]
    for bit in live:
        slots[bit] = slots_in[bit]
        narrow[bit * state : (bit + 1) * state, :] = slots_in[bit].astype(BF16)

    def head_part(c):
        at = slice(c * BLOCK, (c + 1) * BLOCK)
        live = [bit for bit in range(bits) if (c >> bit) & 1]
        if live:
            queries[0 : len(live) * state, :] = read_levels(read_t, weight_h, at, [bit + 1 for bit in live])
        weighted = dot(read_t[:, at], write_t[:, at], TN) * columns[at, padded : padded + 1]
        off_scores[...] = weighted[HALF:, :HALF].astype(BF16)
        scores[0] = jnp.where(causal, weighted[:HALF, :HALF], 0.0)
        scores[1] = jnp.where(causal, weighted[HALF:, HALF:], 0.0)

    def half_part(c, half):
        live = [bit for bit in range(bits) if (c >> bit) & 1]
        low = c * BLOCK + half * HALF
        half_at = slice(low, low + HALF)
        put_at = slice(low - first * BLOCK, low - first * BLOCK + HALF)
        for left in range(0, width, tile):
            lanes = slice(left, left + tile)
            near = dot(factors[half_at, :], wide[:, lanes])
            reach[put_at, lanes] = near * rows[layout.run + 2 * c + half : layout.run + 2 * c + half + 1, lanes]
            rest = None
            if half == 1:
                rest = dot(off_scores[...], scaled[c * BLOCK : c * BLOCK + HALF, lanes])
            if live:
                stored = [narrow[bit * state : (bit + 1) * state, lanes] for bit in live]
                stored = jnp.concatenate(stored, 0) if len(stored) > 1 else stored[0]
                level = dot(
                    queries[0 : len(live) * state, half * HALF : (half + 1) * HALF], stored, TN
                )
                middle = rows[layout.middle + c : layout.middle + c + 1, lanes]
                rest = level if rest is None else rest + middle * level
            skipped = rows[layout.skip : layout.skip + 1, lanes] * mixer[half_at, lanes].astype(F32)
            rest = skipped if rest is None else skipped + near * rest
            for inner in range(0, tile, LANES):
                here = slice(left + inner, left + inner + LANES)
                head = (left + inner) // per_head
                value = mixer[half_at, here]
                left_side = []
                for k in range(heads_here):
                    gap = columns[half_at, head + k : head + k + 1] - cum_h[head + k : head + k + 1, half_at]
                    mixing = scores[half] * jnp.exp2(jnp.minimum(gap, 0.0))
                    left_side.append(mixing.astype(BF16))
                part = dot(
                    jnp.concatenate(left_side, 1),
                    jnp.concatenate(
                        [jnp.where(mask, value.astype(F32), 0.0).astype(BF16) for mask in own], 0
                    ),
                )
                base[put_at, here] = part + rest[:, inner : inner + LANES]

    def update_part(c):
        live = [bit for bit in range(bits) if (c >> bit) & 1]
        ones = 0
        while ones < bits and (c >> ones) & 1:
            ones += 1
        low = c * BLOCK
        if ones == bits:
            return
        for left in range(0, width, tile):
            lanes = slice(left, left + tile)
            shrink = rows[layout.decay + c : layout.decay + c + 1, lanes]
            upper = rows[layout.upper + c : layout.upper + c + 1, lanes]
            fresh = upper * dot(
                write_t[:, low : low + HALF], scaled[low : low + HALF, lanes]
            ) + dot(write_t[:, low + HALF : low + BLOCK], scaled[low + HALF : low + BLOCK, lanes])
            for bit in range(ones):
                fresh = fresh + shrink * slots[bit, :, lanes]
            slots[ones, :, lanes] = fresh
            narrow[ones * state : (ones + 1) * state, lanes] = fresh.astype(BF16)
            for bit in live:
                if bit > ones:
                    kept = shrink * slots[bit, :, lanes]
                    slots[bit, :, lanes] = kept
                    narrow[bit * state : (bit + 1) * state, lanes] = kept.astype(BF16)

    def first_region(c):
        head_part(c)
        half_part(c, 0)

    def second_region(c):
        half_part(c, 1)
        update_part(c)

    when_here = pl.when(lax.axis_index("seq") >= 0)
    for c in range(first, first + count):
        when_here(functools.partial(first_region, c))
        when_here(functools.partial(second_region, c))


def bucket_rows(received, bits, state, width, wanted):
    running = jnp.ones((1, width), F32)
    out = []
    for bit in range(bits):
        upper = upper_half(bit, width)
        if bit in wanted:
            scale = jnp.where(upper, running, 0.0)
            out.append((received[bit][0:state, :].astype(F32) * scale).astype(BF16))
        if bit + 1 < bits:
            extra = received[bit][state:, :].astype(F32)
            running = jnp.where(upper, running * (extra[0:1] + extra[1:2]), running)
    return jnp.concatenate(out, 0) if len(out) > 1 else out[0]


def read_levels(read_t, weight_h, at, levels):
    read_f = read_t[:, at].astype(F32)
    queries = [(read_f * weight_h[level : level + 1, at]).astype(BF16) for level in levels]
    return jnp.concatenate(queries, 0) if len(queries) > 1 else queries[0]


def views(received):
    first = received[0]
    count = first.shape[0] // 2
    return [first.at[pl.ds(0, count), :], first.at[pl.ds(count, count), :]] + list(received[1:])


def near_kernel(starts, local_bits, bits, read_t, weight_h, *rest):
    pieces = len(starts) - 1
    received, rest = views(rest[: bits - 1]), rest[bits - 1 :]
    bases, reaches, rest = rest[:pieces], rest[pieces : 2 * pieces], rest[2 * pieces :]
    out, buckets = rest
    columns = own_columns(bases[0].shape[1])[1]
    buckets[...] = bucket_rows(received, bits, read_t.shape[0], buckets.shape[1], range(bits))
    levels = [local_bits + 1 + bit for bit in range(bits)]
    for piece in range(pieces):

        def block(g, carry, piece=piece):
            at = pl.ds(pl.multiple_of((starts[piece] + g) * BLOCK, BLOCK), BLOCK)
            here = pl.ds(pl.multiple_of(g * BLOCK, BLOCK), BLOCK)
            part = dot(read_levels(read_t, weight_h, at, levels), buckets[...], TN)
            out[at, :] = bases[piece][here, columns] + part * reaches[piece][here, columns]
            return carry

        lax.fori_loop(0, starts[piece + 1] - starts[piece], block, 0, unroll=True)


def final_kernel(starts, local_bits, bits, wanted, side, read_t, weight_h, *rest):
    pieces = len(starts) - 1
    near = None
    if side:
        received, near, rest = views(rest[: bits - 1]), rest[bits - 1], rest[bits:]
        reaches = rest[:pieces]
    else:
        received, rest = rest[:bits], rest[bits:]
        bases, reaches = rest[:pieces], rest[pieces : 2 * pieces]
    out, buckets, ready, sems = rest[-4:]
    columns = own_columns(out.shape[1])[side]
    buckets[...] = bucket_rows(received, bits, read_t.shape[0], buckets.shape[1], wanted)
    levels = [local_bits + 1 + bit for bit in wanted]

    def copy(c, at):
        return pltpu.make_async_copy(ready.at[c], out.at[pl.ds(at, BLOCK), columns], sems.at[c])

    for piece in range(pieces):

        def block(g, carry, piece=piece):
            c = starts[piece] + g
            at = pl.multiple_of(c * BLOCK, BLOCK)
            here = pl.ds(pl.multiple_of(g * BLOCK, BLOCK), BLOCK)
            query = read_levels(read_t, weight_h, pl.ds(at, BLOCK), levels)
            part = dot(query, buckets[...], TN)
            if side:
                base = near[pl.ds(at, BLOCK), :]
            else:
                base = bases[piece][here, columns]
            ready[c] = (base + part * reaches[piece][here, columns]).astype(BF16)
            copy(c, at).start()
            return carry

        lax.fori_loop(0, starts[piece + 1] - starts[piece], block, 0, unroll=True)
    for c in range(starts[-1]):
        copy(c, c * BLOCK).wait()


def gather_columns(mine, axis, after):
    pieces = mine
    size = lax.axis_size(axis)
    stride = size // 2
    while stride:
        other = lax.ppermute(pieces, axis, [(i, i ^ stride) for i in range(size)])
        pieces = pl.pallas_call(
            join_kernel,
            in_specs=[VMEM_SPEC] * 2 + [ANY_SPEC],
            out_specs=VMEM_SPEC,
            out_shape=jax.ShapeDtypeStruct((2 * pieces.shape[0], pieces.shape[1]), BF16),
            compiler_params=grant(2),
            cost_estimate=cost(0, 4 * pieces.size),
            name="join",
        )(pieces, other, after)
        stride //= 2
    return pieces


def cost(flops, bytes_accessed):
    return pl.CostEstimate(flops=flops, bytes_accessed=bytes_accessed, transcendentals=0)


def grant(mebibytes):
    return pltpu.CompilerParams(vmem_limit_bytes=mebibytes << 20)


def on_device(
    mixer_input, write_map, read_map, step_size, log_decay, skip_gain, level_table, level_index
):
    tokens, width = mixer_input.shape
    heads = log_decay.shape[0]
    blocks = tokens // BLOCK
    local_bits = blocks.bit_length() - 1
    ranks = lax.axis_size("seq")
    device_bits = ranks.bit_length() - 1
    levels = level_table.shape[0]
    padded = LANES // 4
    tile = 256
    layout = Rows(blocks)
    sds = jax.ShapeDtypeStruct

    factors, columns, cum_h, weight_h, rows = pl.pallas_call(
        functools.partial(prep_kernel, heads, padded, layout),
        in_specs=[HBM_SPEC] * 5,
        out_specs=(VMEM_SPEC,) * 5,
        out_shape=(
            sds((tokens, LANES), BF16), sds((tokens, LANES), F32), sds((padded, tokens), F32),
            sds((levels, tokens), F32), sds((layout.count, width), F32),
        ),
        scratch_shapes=[
            pltpu.VMEM((heads, tokens), F32),
            pltpu.VMEM((heads, tokens), F32),
            pltpu.VMEM(level_index.shape, jnp.int32),
            pltpu.VMEM(level_table.shape, F32),
            pltpu.VMEM((1, heads), F32),
            pltpu.VMEM((padded, tokens), F32),
            pltpu.VMEM((padded, tokens), F32),
            pltpu.VMEM((LANES, BLOCK), F32),
            pltpu.SemaphoreType.DMA((5,)),
        ],
        compiler_params=grant(6),
        cost_estimate=cost(2_000_000_000, 4_000_000),
        name="prep",
    )(
        *(
            pltpu.with_memory_space_constraint(value, pltpu.HBM)
            for value in (log_decay, step_size, level_index, level_table, skip_gain[None, :])
        )
    )

    write_t = gather_columns(write_map.T, "head", rows)
    read_t = gather_columns(read_map.T, "head", rows)
    state = write_t.shape[0]

    half = width // 2
    carried = (sds((state + 8, half), BF16), sds((state, half), F32), sds((8, half), F32))

    def front(side, scaled):
        operands = [mixer_input, factors, rows]
        aliases = {}
        if scaled is not None:
            aliases = {len(operands): 0}
            operands.append(scaled)
        scaled, to_total = pl.pallas_call(
            functools.partial(scale_kernel, heads, padded, layout, side),
            in_specs=[VMEM_SPEC] * len(operands),
            out_specs=(VMEM_SPEC,) * 2,
            out_shape=(sds((tokens, width), BF16), sds((tokens, half), BF16)),
            input_output_aliases=aliases,
            compiler_params=grant(4),
            cost_estimate=cost(1_500_000_000, tokens * width * 3),
            name="scale",
        )(*operands)
        shapes = carried if side == 0 else carried[:1]
        results = pl.pallas_call(
            functools.partial(state_kernel, layout, side),
            in_specs=[VMEM_SPEC] * 3,
            out_specs=(VMEM_SPEC,) * len(shapes),
            out_shape=shapes,
            compiler_params=grant(4),
            cost_estimate=cost(tokens * width * state, tokens * width),
            name="state",
        )(to_total, write_t, rows)
        return scaled, results

    scaled, (first_out,) = front(1, None)
    scaled, (second_out, mine, mine_exp) = front(0, scaled)

    def local(first, count, slots, after):
        return pl.pallas_call(
            functools.partial(
                local_kernel, heads, padded, local_bits, first, count, layout, tile
            ),
            in_specs=[VMEM_SPEC] * 10 + [ANY_SPEC],
            out_specs=(VMEM_SPEC,) * 3,
            out_shape=(
                sds((count * BLOCK, width), F32), sds((count * BLOCK, width), F32),
                sds((local_bits, state, width), F32),
            ),
            scratch_shapes=[
                pltpu.VMEM((2, HALF, HALF), F32),
                pltpu.VMEM((local_bits * state, width), BF16),
                pltpu.VMEM((HALF, HALF), BF16),
                pltpu.VMEM((local_bits * state, BLOCK), BF16),
            ],
            compiler_params=grant(8),
            cost_estimate=cost(count * BLOCK * width * 2 * 2000, count * BLOCK * width * 8),
            name="local",
        )(
            mixer_input, scaled, write_t, read_t, factors, columns, cum_h, weight_h, rows,
            slots, after,
        )

    def swap(value, bit):
        return lax.ppermute(value, "seq", [(i, i ^ 1 << bit) for i in range(ranks)])

    shares = ([2] + [3] * (device_bits - 1))[:device_bits]
    starts = [0]
    for share in shares:
        starts.append(starts[-1] + max(1, blocks * share // sum(shares)))
    starts = [min(start, blocks) for start in starts[:-1]] + [blocks]

    slots = jnp.zeros((local_bits, 8, LANES), F32)
    bases, reaches = [], []
    own_parts = [swap(first_out, 0)]
    other_parts = []
    after = rows
    payload = None
    for bit in range(device_bits):
        if starts[bit + 1] > starts[bit]:
            base, reach, slots = local(starts[bit], starts[bit + 1] - starts[bit], slots, after)
            bases.append(base)
            reaches.append(reach)
        if bit + 1 < device_bits:
            last = bit + 2 == device_bits
            shapes = carried[:1] if last else carried
            payload, *more = pl.pallas_call(
                functools.partial(merge_kernel, bit),
                in_specs=[VMEM_SPEC] * 3 + [ANY_SPEC],
                out_specs=(VMEM_SPEC,) * len(shapes),
                out_shape=shapes,
                compiler_params=grant(4),
                cost_estimate=cost(2 * state * width, state * width * 6),
                name="merge",
            )(own_parts[bit], mine, mine_exp, slots)
            if more:
                mine, mine_exp = more
            after = payload
            own_parts.append(swap(payload, bit + 1))
            if bit == 1:
                both = pl.pallas_call(
                    join_kernel,
                    in_specs=[VMEM_SPEC] * 2,
                    out_specs=VMEM_SPEC,
                    out_shape=sds((2 * payload.shape[0], half), BF16),
                    compiler_params=grant(2),
                    cost_estimate=cost(0, 8 * payload.size),
                    name="both",
                )(second_out, own_parts[1])
                other_parts.append(swap(both, 0))
            elif bit > 1:
                other_parts.append(swap(own_parts[bit], 0))
    starts = sorted(set(starts))

    if device_bits > 1:
        other_parts.append(swap(own_parts[-1], 0))

    def finish(side, operands, wanted, out):
        specs = [VMEM_SPEC] * len(operands)
        aliases = {}
        if out is not None:
            aliases = {len(operands): 0}
            operands = operands + [out]
            specs.append(ANY_SPEC)
        return pl.pallas_call(
            functools.partial(final_kernel, starts, local_bits, device_bits, wanted, side),
            in_specs=specs,
            out_specs=ANY_SPEC,
            out_shape=sds((tokens, width), BF16),
            input_output_aliases=aliases,
            scratch_shapes=[
                pltpu.VMEM((len(wanted) * state, half), BF16),
                pltpu.VMEM((blocks, BLOCK, half), BF16),
                pltpu.SemaphoreType.DMA((blocks,)),
            ],
            compiler_params=grant(6),
            cost_estimate=cost(tokens * width * state, tokens * width * 3),
            name="final",
        )(*operands)

    out = finish(0, [read_t, weight_h, *own_parts, *bases, *reaches], list(range(device_bits)), None)
    near_bits = device_bits - 1
    near = pl.pallas_call(
        functools.partial(near_kernel, starts, local_bits, near_bits),
        in_specs=[VMEM_SPEC] * (2 + near_bits - 1 + 2 * len(bases)),
        out_specs=VMEM_SPEC,
        out_shape=sds((tokens, half), F32),
        scratch_shapes=[pltpu.VMEM((near_bits * state, half), BF16)],
        compiler_params=grant(4),
        cost_estimate=cost(tokens * width * state * 2, tokens * width * 3),
        name="near",
    )(read_t, weight_h, *other_parts[:-1], *bases, *reaches)
    return finish(1, [read_t, weight_h, *other_parts, near, *reaches], [device_bits - 1], out)


def solution(mesh):
    placed = (
        P("seq", "head"),
        P("seq", "head"),
        P("seq", "head"),
        P("head", "seq"),
        P("head", "seq"),
        P("head"),
        P(),
        P(None, "seq"),
    )

    return jax.shard_map(
        on_device, mesh=mesh, in_specs=placed, out_specs=P("seq", "head"), check_vma=False
    )
```
